32 devices in a mesh: dp: 8 (over y, x, core), tensor: 4 (over z).
Axes of the slice: x: 2, y: 2, z: 4, core: 2. Of those that a mesh axis runs over, the one named last changes fastest.
Arguments:
- tokens: bfloat16 [16384, 1536], P(('dp', 'tensor')), may hold values from -6 to 6
- lengths: int32 [8], P('dp'), may hold values from 1024 to 2048, as said below
- cotangent: bfloat16 [16384, 1536], P(('dp', 'tensor')), may hold values from -6 to 6
- attn_gain: bfloat16 [1536], P('dp'), may hold values from 0.099609375 to 1.8984375
- query_weight: bfloat16 [1536, 1536], P('dp', 'tensor'), may hold values from -0.15625 to 0.15625
- key_matrix: bfloat16 [1536, 768], P('dp', 'tensor'), may hold values from -0.15625 to 0.15625
- value_matrix: bfloat16 [1536, 768], P('dp', 'tensor'), may hold values from -0.15625 to 0.15625
- out_weight: bfloat16 [1536, 1536], P('tensor', 'dp'), may hold values from -2.5 to 2.5
- mlp_gain: bfloat16 [1536], P('dp'), may hold values from 0.099609375 to 1.8984375
- gate_weight: bfloat16 [1536, 4096], P('dp', 'tensor'), may hold values from -0.15625 to 0.15625
- up_weight: bfloat16 [1536, 4096], P('dp', 'tensor'), may hold values from -0.15625 to 0.15625
- down_weight: bfloat16 [4096, 1536], P('tensor', 'dp'), may hold values from -0.09375 to 0.09375
Outputs:
- block_out: bfloat16 [16384, 1536], P(('dp', 'tensor'))
- tokens_grad: bfloat16 [16384, 1536], P(('dp', 'tensor'))
- attn_gain_grad: float32 [1536], P('dp')
- query_grad: float32 [1536, 1536], P('dp', 'tensor')
- key_grad: float32 [1536, 768], P('dp', 'tensor')
- value_grad: float32 [1536, 768], P('dp', 'tensor')
- out_grad: float32 [1536, 1536], P('tensor', 'dp')
- mlp_gain_grad: float32 [1536], P('dp')
- gate_grad: float32 [1536, 4096], P('dp', 'tensor')
- up_grad: float32 [1536, 4096], P('dp', 'tensor')
- down_grad: float32 [4096, 1536], P('tensor', 'dp')
The draws below stay inside these ranges and needn't reach their ends.
Inputs may be any that keep to these rules, and one draw needn't show every extreme that they name: `lengths`: in every draw one slot is full and one holds exactly half of 2048.
All inputs are finite; a program needn't handle non-finite values.
Results may differ from the reference program's by a relative error of at most 0.014.
Values may be sent and summed in bfloat16 or wider, within the bound.
A program may use at most 192 MiB of HBM per device.

```python
import math
import jax
import jax.numpy as jnp
from jax import lax

MODEL_WIDTH = 1536
QUERY_HEADS = 16
KEY_VALUE_HEADS = 8
HEAD_SIZE = 96
FF = 4096
SEQ = 2048
TOKENS = 16384
N_DP = 8


def draw_lengths(key, part):
    first, second = jax.random.split(key)
    values = jax.random.randint(first, (N_DP,), SEQ // 2, SEQ + 1, dtype=jnp.int32)
    order = jax.random.permutation(second, N_DP)
    values = values.at[order[0]].set(SEQ)
    values = values.at[order[1]].set(SEQ // 2)
    return values


def block_scale(own_key, extent, shards, least, top_value):
    level, own = 1.0, jax.random.fold_in(own_key, 6)
    for position, parts in shards:
        steps = jnp.exp(jax.random.uniform(jax.random.fold_in(own, position), (parts,), jnp.float32, least / len(shards), top_value / len(shards)))
        level = level * jnp.repeat(steps, extent[position] // parts).reshape([-1 if axis == position else 1 for axis in range(len(extent))])
    return level


def scatter_about(rng, extent, deviation, bound, shards=(), held_as=jnp.bfloat16):
    drawn = jax.random.normal(rng, extent, jnp.float32) * deviation
    if len(shards) > 0:
        drawn = block_scale(rng, extent, shards, -0.22, 0.18) * drawn
    return jnp.clip(drawn, min=-bound, max=bound).astype(held_as)


def setup_inputs(seed: int = 0) -> dict:
    key_list = jax.random.split(jax.random.key(seed), 13)
    tokens = scatter_about(key_list[0], (TOKENS, MODEL_WIDTH), 1.0, 6.0, ((0, 32),))
    lengths = draw_lengths(jax.random.fold_in(key_list[12], 71), 0)
    cotangent = scatter_about(key_list[2], (TOKENS, MODEL_WIDTH), 1.0, 6.0, ((0, 32),))
    attn_gain = jnp.clip(1.0 + 0.18 * jax.random.normal(key_list[3], (MODEL_WIDTH,), jnp.float32), 0.099609375, 1.8984375).astype(jnp.bfloat16)
    query_weight = scatter_about(key_list[4], (MODEL_WIDTH, QUERY_HEADS * HEAD_SIZE), MODEL_WIDTH ** -0.5, 0.15625, ((0, 8), (1, 4)))
    key_matrix = scatter_about(key_list[5], (MODEL_WIDTH, KEY_VALUE_HEADS * HEAD_SIZE), MODEL_WIDTH ** -0.5, 0.15625, ((0, 8), (1, 4)))
    value_matrix = scatter_about(key_list[6], (MODEL_WIDTH, KEY_VALUE_HEADS * HEAD_SIZE), MODEL_WIDTH ** -0.5, 0.15625, ((0, 8), (1, 4)))
    out_weight = scatter_about(key_list[7], (QUERY_HEADS * HEAD_SIZE, MODEL_WIDTH), (max(1, QUERY_HEADS * HEAD_SIZE // 256)) ** -0.5, 2.5, ((0, 4), (1, 8)))
    mlp_gain = jnp.clip(1.0 + 0.18 * jax.random.normal(key_list[8], (MODEL_WIDTH,), jnp.float32), 0.099609375, 1.8984375).astype(jnp.bfloat16)
    gate_weight = scatter_about(key_list[9], (MODEL_WIDTH, FF), MODEL_WIDTH ** -0.5, 0.15625, ((0, 8), (1, 4)))
    up_weight = scatter_about(key_list[10], (MODEL_WIDTH, FF), MODEL_WIDTH ** -0.5, 0.15625, ((0, 8), (1, 4)))
    down_weight = scatter_about(key_list[11], (FF, MODEL_WIDTH), FF ** -0.5, 0.09375, ((0, 4), (1, 8)))
    return {"tokens": tokens, "lengths": lengths, "cotangent": cotangent, "attn_gain": attn_gain, "query_weight": query_weight, "key_matrix": key_matrix, "value_matrix": value_matrix, "out_weight": out_weight, "mlp_gain": mlp_gain, "gate_weight": gate_weight, "up_weight": up_weight, "down_weight": down_weight}


eps_norm = 1e-05
rope_base = 100000.0

@jax.custom_vjp
def reduced_precision(v):
    return lax.optimization_barrier(v.astype(jnp.bfloat16)).astype(jnp.float32)

@jax.custom_vjp
def reduced_backward(v):
    return v

def low_keep(v):
    return (reduced_precision(v), None)

def low_pass(kept, grad):
    return (grad,)

def back_keep(v):
    return (v, None)

def back_low(kept, grad):
    return (reduced_precision(grad),)
reduced_precision.defvjp(low_keep, low_pass)
reduced_backward.defvjp(back_keep, back_low)

def tables(count):
    half = HEAD_SIZE // 2
    freqs = rope_base ** (-(jnp.arange(half, dtype=jnp.float32) * 2.0) / HEAD_SIZE)
    angles = jnp.arange(count, dtype=jnp.float32)[:, None] * freqs[None, :]
    cosine_table = jnp.cos(angles)
    sine_table = jnp.sin(angles)
    return (jnp.concatenate([cosine_table, cosine_table], axis=1), jnp.concatenate([sine_table, sine_table], axis=1))

def rotate_pairs(values, cosine_table, sine_table):
    half = values.shape[-1] // 2
    swapped = jnp.concatenate([-values[..., half:], values[..., :half]], axis=-1)
    return values * cosine_table[:, None, :] + swapped * sine_table[:, None, :]

def norm_rows(rows, gain):
    return rows * lax.rsqrt(lax.optimization_barrier(jnp.mean(rows * rows, axis=-1, keepdims=True)) + eps_norm) * gain

def precise_product(left, right):
    return jnp.dot(left, right, precision=lax.Precision.HIGHEST, preferred_element_type=jnp.float32)

def forward(xseq, gain_one, wq, key_projection, value_projection, wo, gain_two, wg, wu, wd, length):
    sequence_length = xseq.shape[0]
    cosine_table, sine_table = tables(sequence_length)
    first_normed = reduced_precision(norm_rows(xseq, gain_one))
    rotated_query = reduced_precision(rotate_pairs(reduced_backward(precise_product(first_normed, wq)).reshape(sequence_length, QUERY_HEADS, HEAD_SIZE), cosine_table, sine_table))
    rotated_key = reduced_precision(rotate_pairs(reduced_backward(precise_product(first_normed, key_projection)).reshape(sequence_length, KEY_VALUE_HEADS, HEAD_SIZE), cosine_table, sine_table))
    value_reduced = reduced_precision(reduced_backward(precise_product(first_normed, value_projection))).reshape(sequence_length, KEY_VALUE_HEADS, HEAD_SIZE)
    query_block = min(512, sequence_length)
    block_count = sequence_length // query_block
    query_block_list = rotated_query.reshape(block_count, query_block, KEY_VALUE_HEADS, QUERY_HEADS // KEY_VALUE_HEADS, HEAD_SIZE)
    starts = jnp.arange(block_count, dtype=jnp.int32) * query_block
    key_pos = jnp.arange(sequence_length, dtype=jnp.int32)
    scale = 1.0 / math.sqrt(HEAD_SIZE)

    def one_block(item):
        q_part, start = item
        raw = jnp.einsum('qgre,kge->grqk', q_part, rotated_key, precision=lax.Precision.HIGHEST)
        scores = reduced_backward(raw * scale)
        row_pos = start + jnp.arange(query_block, dtype=jnp.int32)
        allowed = (key_pos[None, :] <= row_pos[:, None]) & (key_pos[None, :] < length)
        scores = jnp.where(allowed, scores, -1e+30)
        probs = reduced_precision(jax.nn.softmax(scores, axis=-1))
        return jnp.einsum('grqk,kge->qgre', probs, value_reduced, precision=lax.Precision.HIGHEST)
    attended = lax.map(jax.checkpoint(one_block), (query_block_list, starts))
    attended = reduced_precision(reduced_backward(attended.reshape(sequence_length, QUERY_HEADS * HEAD_SIZE)))
    h_one = xseq + reduced_backward(precise_product(attended, wo))
    n2 = reduced_precision(norm_rows(h_one, gain_two))
    gate = reduced_backward(precise_product(n2, wg))
    upper = reduced_backward(precise_product(n2, wu))
    hidden = reduced_precision(jax.nn.silu(gate) * upper)
    live = (key_pos < length).astype(xseq.dtype)[:, None]
    return live * (h_one + reduced_backward(precise_product(hidden, wd)))

def reference(tokens, lengths, cotangent, attn_gain, query_weight, key_matrix, value_matrix, out_weight, mlp_gain, gate_weight, up_weight, down_weight):
    weights = tuple((w.astype(jnp.float32) for w in (attn_gain, query_weight, key_matrix, value_matrix, out_weight, mlp_gain, gate_weight, up_weight, down_weight)))
    seq_x = tokens.astype(jnp.float32).reshape(N_DP, SEQ, MODEL_WIDTH)
    seq_g = cotangent.astype(jnp.float32).reshape(N_DP, SEQ, MODEL_WIDTH)

    def one_sequence(totals, item):
        xseq, gseq, length = item

        def local(xv, *params):
            return forward(xv, *params, length)
        result, pull = jax.vjp(local, xseq, *weights)
        grads = pull(gseq)
        totals = tuple((a + b for a, b in zip(totals, grads[1:])))
        return (totals, (result.astype(jnp.bfloat16), grads[0].astype(jnp.bfloat16)))
    zeros = tuple((jnp.zeros(w.shape, jnp.float32) for w in weights))
    totals, (outputs, input_grads) = lax.scan(one_sequence, zeros, (seq_x, seq_g, lengths))
    return (outputs.reshape(TOKENS, MODEL_WIDTH), input_grads.reshape(TOKENS, MODEL_WIDTH), totals[0], totals[1], totals[2], totals[3], totals[4], totals[5], totals[6], totals[7], totals[8])
```

```python
import functools
import math

import jax
import jax.numpy as jnp
from jax import lax
from jax.experimental import pallas as pl
from jax.experimental.pallas import tpu as pltpu
from jax.sharding import PartitionSpec as P

HEAD_SIZE = 96
HALF = HEAD_SIZE // 2
GAIN_LANES = 128
CHUNKS = 4
KEY_TILE = 256
NEG = -1e30

eps_norm = 1e-05
rope_base = 100000.0
SCALE = 1.0 / math.sqrt(HEAD_SIZE)
SCALE2 = SCALE * math.log2(math.e)

f32 = jnp.float32
bf16 = jnp.bfloat16
VMEM_LIMIT = 56 * 1024 * 1024


def dot(a, b, dims=((1,), (0,))):
    return lax.dot_general(a, b, (dims, ((), ())), preferred_element_type=f32)


def params(*semantics):
    return pltpu.CompilerParams(dimension_semantics=semantics, vmem_limit_bytes=VMEM_LIMIT)


def cost(flops, nbytes, trans=0):
    return pl.CostEstimate(flops=int(flops), bytes_accessed=int(nbytes), transcendentals=int(trans))


def turn(y, cosine, sine, sign):
    parts = []
    for h in range(y.shape[0] // HEAD_SIZE):
        a = y[h * HEAD_SIZE : h * HEAD_SIZE + HALF]
        b = y[h * HEAD_SIZE + HALF : (h + 1) * HEAD_SIZE]
        parts.append(a * cosine - sign * (b * sine))
        parts.append(b * cosine + sign * (a * sine))
    return jnp.concatenate(parts, axis=0)


def qkv_kernel(nq, nk, n1_ref, w_ref, cos_ref, sin_ref, q_ref, kv_ref):
    w = w_ref[0, :, : nq + 2 * nk]
    y = dot(n1_ref[...], w).T
    cosine, sine = cos_ref[...], sin_ref[...]
    q_ref[0] = turn(y[:nq], cosine, sine, 1.0).astype(bf16)
    kv_ref[0] = turn(y[nq : nq + nk], cosine, sine, 1.0).astype(bf16)
    kv_ref[1] = y[nq + nk :].astype(bf16)


def qkv_project(n1, w, cosine, sine, nq, nk):
    rows, width = n1.shape
    zs, _, cols = w.shape
    return pl.pallas_call(
        functools.partial(qkv_kernel, nq, nk),
        grid=(zs,),
        in_specs=[
            pl.BlockSpec((rows, width), lambda z: (0, 0)),
            pl.BlockSpec((1, width, cols), lambda z: (z, 0, 0)),
            pl.BlockSpec((HALF, rows), lambda z: (0, 0)),
            pl.BlockSpec((HALF, rows), lambda z: (0, 0)),
        ],
        out_specs=[
            pl.BlockSpec((1, nq, rows), lambda z: (z, 0, 0)),
            pl.BlockSpec((2, nk, rows), lambda z: (0, z, 0)),
        ],
        out_shape=[
            jax.ShapeDtypeStruct((zs, nq, rows), bf16),
            jax.ShapeDtypeStruct((2, zs * nk, rows), bf16),
        ],
        compiler_params=params("arbitrary"),
        cost_estimate=cost(2 * rows * width * cols * zs, 2 * zs * width * cols + 8 * rows * width),
        name="qkv_project",
    )(n1, w, cosine, sine)


def out_kernel(att_ref, w_ref, x_ref, h_ref):
    z = pl.program_id(0)

    @pl.when(z == 0)
    def _():
        h_ref[...] = x_ref[...].astype(f32)

    h_ref[...] += dot(att_ref[0].T, w_ref[0], ((1,), (1,)))


def out_project(att, w, x, no, col):
    zs, _, rows = att.shape
    width = x.shape[1]
    return pl.pallas_call(
        out_kernel,
        grid=(zs,),
        in_specs=[
            pl.BlockSpec((1, no, rows), lambda z: (z, 0, 0)),
            pl.BlockSpec((1, width, no), lambda z: (z, 0, col)),
            pl.BlockSpec((rows, width), lambda z: (0, 0)),
        ],
        out_specs=pl.BlockSpec((rows, width), lambda z: (0, 0)),
        out_shape=jax.ShapeDtypeStruct((rows, width), f32),
        compiler_params=params("arbitrary"),
        cost_estimate=cost(2 * rows * width * no * zs, 2 * zs * width * no + 8 * rows * width),
        name="out_project",
    )(att, w, x)


def out_back_kernel(me_ref, dh_ref, dht_ref, att_ref, w_ref, da_ref, keep_ref, send_ref):
    w = w_ref[0]
    da_ref[0] = dot(dh_ref[...], w).T.astype(bf16)
    grad = dot(dht_ref[...], att_ref[0].T).astype(bf16)
    half = grad.shape[0] // 2
    keep_ref[0] = grad[:half]
    send_ref[0] = grad[half:]


def out_back(me, dh, dht, att, w, no, col):
    zs, _, rows = att.shape
    width = dh.shape[1]
    half = width // 2
    return pl.pallas_call(
        out_back_kernel,
        grid_spec=pltpu.PrefetchScalarGridSpec(
            num_scalar_prefetch=1,
            grid=(zs,),
            in_specs=[
                pl.BlockSpec((rows, width), lambda z, m: (0, 0)),
                pl.BlockSpec((width, rows), lambda z, m: (0, 0)),
                pl.BlockSpec((1, no, rows), lambda z, m: (z, 0, 0)),
                pl.BlockSpec((1, width, no), lambda z, m: (z, 0, col)),
            ],
            out_specs=[
                pl.BlockSpec((1, no, rows), lambda z, m: (z, 0, 0)),
                pl.BlockSpec((1, half, no), lambda z, m: (z ^ m[0], 0, 0)),
                pl.BlockSpec((1, half, no), lambda z, m: (z ^ m[0], 0, 0)),
            ],
        ),
        out_shape=[
            jax.ShapeDtypeStruct((zs, no, rows), bf16),
            jax.ShapeDtypeStruct((zs, half, no), bf16),
            jax.ShapeDtypeStruct((zs, half, no), bf16),
        ],
        compiler_params=params("arbitrary"),
        cost_estimate=cost(4 * rows * width * no * zs, 4 * zs * width * no + 8 * rows * width),
        name="out_back",
    )(me, dh, dht, att, w)


def qkv_back_kernel(
    nq, nk, me_ref, dq_ref, dkv_ref, cos_ref, sin_ref, n1t_ref, w_ref, dn_ref, keep_ref, send_ref
):
    z = pl.program_id(0)

    @pl.when(z == 0)
    def _():
        dn_ref[...] = jnp.zeros_like(dn_ref)

    cosine, sine = cos_ref[...], sin_ref[...]
    dq = turn(dq_ref[0], cosine, sine, -1.0).astype(bf16)
    dk = turn(dkv_ref[0].astype(f32), cosine, sine, -1.0).astype(bf16)
    d = jnp.concatenate([dq, dk, dkv_ref[1]], axis=0).T
    w = w_ref[0, :, : nq + 2 * nk]
    dn_ref[...] += dot(d, w, ((1,), (1,)))
    grad = dot(n1t_ref[...], d).astype(bf16)
    half = grad.shape[0] // 2
    keep_ref[0] = grad[:half]
    send_ref[0] = grad[half:]


def qkv_back(me, dq, dkv, cosine, sine, n1t, w, nq, nk):
    zs, _, rows = dq.shape
    width = n1t.shape[0]
    half = width // 2
    cols = w.shape[2]
    out = nq + 2 * nk
    return pl.pallas_call(
        functools.partial(qkv_back_kernel, nq, nk),
        grid_spec=pltpu.PrefetchScalarGridSpec(
            num_scalar_prefetch=1,
            grid=(zs,),
            in_specs=[
                pl.BlockSpec((1, nq, rows), lambda z, m: (z, 0, 0)),
                pl.BlockSpec((2, nk, rows), lambda z, m: (0, z, 0)),
                pl.BlockSpec((HALF, rows), lambda z, m: (0, 0)),
                pl.BlockSpec((HALF, rows), lambda z, m: (0, 0)),
                pl.BlockSpec((width, rows), lambda z, m: (0, 0)),
                pl.BlockSpec((1, width, cols), lambda z, m: (z, 0, 0)),
            ],
            out_specs=[
                pl.BlockSpec((rows, width), lambda z, m: (0, 0)),
                pl.BlockSpec((1, half, out), lambda z, m: (z ^ m[0], 0, 0)),
                pl.BlockSpec((1, half, out), lambda z, m: (z ^ m[0], 0, 0)),
            ],
        ),
        out_shape=[
            jax.ShapeDtypeStruct((rows, width), f32),
            jax.ShapeDtypeStruct((zs, half, out), bf16),
            jax.ShapeDtypeStruct((zs, half, out), bf16),
        ],
        compiler_params=params("arbitrary"),
        cost_estimate=cost(4 * rows * width * out * zs, 4 * zs * width * cols + 8 * rows * width),
        name="qkv_back",
    )(me, dq, dkv, cosine, sine, n1t, w)


def side_by_side(ref):
    group = ref.shape[0] // HEAD_SIZE
    return jnp.concatenate(
        [ref[a * HEAD_SIZE : (a + 1) * HEAD_SIZE] for a in range(group)], axis=1
    )


def key_mask(s, key_first, query_first, length, rows, diagonal):
    key = key_first + lax.broadcasted_iota(jnp.int32, (s.shape[0], 1), 0)
    ok = key < length
    if diagonal:
        lane = lax.broadcasted_iota(jnp.int32, s.shape, 1)
        query = query_first + lax.rem(lane, rows)
        ok = ok & (key <= query)
    return jnp.broadcast_to(ok, s.shape)


def attend_kernel(blocks, group, sc_ref, q_ref, *refs):
    kv_refs = refs[: 2 * blocks]
    o_ref, lse_ref, m_ref, l_ref, acc_ref = refs[2 * blocks :]
    z, length = sc_ref[0], sc_ref[1]
    rows = q_ref.shape[1]
    first = z * rows
    m_ref[...] = jnp.full_like(m_ref, NEG)
    l_ref[...] = jnp.zeros_like(l_ref)
    acc_ref[...] = jnp.zeros_like(acc_ref)

    for r in range(blocks):
        k_ref, v_ref = kv_refs[2 * r], kv_refs[2 * r + 1]

        @pl.when((z >= r) & (first - r * rows < length))
        def _():
            q = side_by_side(q_ref)
            for j in range(rows // KEY_TILE):
                part = slice(j * KEY_TILE, (j + 1) * KEY_TILE)
                k, v = k_ref[0, :, part], v_ref[0, :, part]
                s = dot(k, q, ((0,), (0,)))
                ok = key_mask(s, first - r * rows + j * KEY_TILE, first, length, rows, r == 0)
                s = jnp.where(ok, s, NEG)
                old = m_ref[...]
                new = jnp.maximum(old, jnp.max(s, axis=0, keepdims=True))
                shrink = jnp.exp2((old - new) * SCALE2)
                p = jnp.exp2(s * SCALE2 - new * SCALE2)
                l_ref[...] = l_ref[...] * shrink + jnp.sum(p, axis=0, keepdims=True)
                acc_ref[...] = acc_ref[...] * shrink + dot(v, p.astype(bf16))
                m_ref[...] = new

    total = l_ref[...]
    total = jnp.where(total > 0.0, total, 1.0)
    out = acc_ref[...] / total
    log_total = m_ref[...] * SCALE2 + jnp.log2(total)
    for a in range(group):
        lanes = slice(a * rows, (a + 1) * rows)
        o_ref[a * HEAD_SIZE : (a + 1) * HEAD_SIZE] = out[:, lanes].astype(bf16)
    lse_ref[0] = log_total


def attend(sc, q, kvs):
    heads_rows, rows = q.shape
    blocks = len(kvs)
    groups = kvs[0].shape[1] // HEAD_SIZE
    per = heads_rows // groups
    group = per // HEAD_SIZE
    kv_specs, kv_args = [], []
    for kv in kvs:
        for which in (0, 1):
            kv_specs.append(
                pl.BlockSpec((1, HEAD_SIZE, rows), lambda g, s, which=which: (which, g, 0))
            )
            kv_args.append(kv)
    work = heads_rows // HEAD_SIZE * rows * rows * blocks
    return pl.pallas_call(
        functools.partial(attend_kernel, blocks, group),
        grid_spec=pltpu.PrefetchScalarGridSpec(
            num_scalar_prefetch=1,
            grid=(groups,),
            in_specs=[pl.BlockSpec((per, rows), lambda g, s: (g, 0))] + kv_specs,
            out_specs=[
                pl.BlockSpec((per, rows), lambda g, s: (g, 0)),
                pl.BlockSpec((1, 1, group * rows), lambda g, s: (g, 0, 0)),
            ],
            scratch_shapes=[
                pltpu.VMEM((1, group * rows), f32),
                pltpu.VMEM((1, group * rows), f32),
                pltpu.VMEM((HEAD_SIZE, group * rows), f32),
            ],
        ),
        out_shape=[
            jax.ShapeDtypeStruct((heads_rows, rows), bf16),
            jax.ShapeDtypeStruct((groups, 1, group * rows), f32),
        ],
        compiler_params=params("arbitrary"),
        cost_estimate=cost(4 * work * HEAD_SIZE, 2 * (blocks + 2) * heads_rows * rows, work),
        name="attend",
    )(sc, q, *kv_args)


def mlp_kernel(
    tile, first, me_ref, n2_ref, n2t_ref, g_ref, gt_ref, w_ref, *refs
):
    if first:
        out_ref, dn_ref, keep_ref, send_ref = refs
    else:
        out_in, dn_in, out_ref, dn_ref, keep_ref, send_ref = refs
    z = pl.program_id(0)

    @pl.when(z == 0)
    def _():
        if first:
            out_ref[...] = jnp.zeros_like(out_ref)
            dn_ref[...] = jnp.zeros_like(dn_ref)
        else:
            out_ref[...] = out_in[...]
            dn_ref[...] = dn_in[...]

    wg = w_ref[0, :, :tile]
    wu = w_ref[0, :, tile : 2 * tile]
    wd = w_ref[0, :, 2 * tile : 3 * tile]
    n2, g = n2_ref[...], g_ref[...]
    gate = dot(n2, wg)
    up = dot(n2, wu)
    d_hidden = dot(g, wd)
    sigma = 1.0 / (1.0 + jnp.exp(-gate))
    active = gate * sigma
    hidden = (active * up).astype(bf16)
    d_gate = (d_hidden * up * (sigma * (1.0 + gate * (1.0 - sigma)))).astype(bf16)
    d_up = (d_hidden * active).astype(bf16)
    out_ref[...] += dot(hidden, wd, ((1,), (1,)))
    dn_ref[...] += dot(d_gate, wg, ((1,), (1,))) + dot(d_up, wu, ((1,), (1,)))
    half = n2t_ref.shape[0] // 2
    for ref, rows in ((keep_ref, slice(0, half)), (send_ref, slice(half, 2 * half))):
        n2t, gt = n2t_ref[rows], gt_ref[rows]
        ref[0, :, :tile] = dot(n2t, d_gate).astype(bf16)
        ref[0, :, tile : 2 * tile] = dot(n2t, d_up).astype(bf16)
        ref[0, :, 2 * tile :] = dot(gt, hidden).astype(bf16)


def mlp(me, n2, n2t, g, gt, w, chunk, tile, carry):
    rows, width = n2.shape
    zs = w.shape[0]
    half = width // 2
    full = pl.BlockSpec((rows, width), lambda z, m: (0, 0))
    full_t = pl.BlockSpec((width, rows), lambda z, m: (0, 0))
    grad_spec = pl.BlockSpec((1, half, 3 * tile), lambda z, m: (z ^ m[0], 0, 0))
    first = carry is None
    in_specs = [
        full,
        full_t,
        full,
        full_t,
        pl.BlockSpec((1, width, 3 * tile), lambda z, m: (z, 0, chunk)),
    ]
    args = [me, n2, n2t, g, gt, w]
    aliases = {}
    if not first:
        in_specs += [full, full]
        aliases = {6: 0, 7: 1}
        args += list(carry)
    return pl.pallas_call(
        functools.partial(mlp_kernel, tile, first),
        grid_spec=pltpu.PrefetchScalarGridSpec(
            num_scalar_prefetch=1,
            grid=(zs,),
            in_specs=in_specs,
            out_specs=[full, full, grad_spec, grad_spec],
        ),
        out_shape=[
            jax.ShapeDtypeStruct((rows, width), f32),
            jax.ShapeDtypeStruct((rows, width), f32),
            jax.ShapeDtypeStruct((zs, half, 3 * tile), bf16),
            jax.ShapeDtypeStruct((zs, half, 3 * tile), bf16),
        ],
        input_output_aliases=aliases,
        compiler_params=params("arbitrary"),
        cost_estimate=cost(
            18 * rows * width * tile * zs, 4 * zs * width * 3 * tile + 24 * rows * width
        ),
        name="mlp",
    )(*args)


def pairs(count, mask):
    return [(i, i ^ mask) for i in range(count)]


def bits_of(count):
    return [1 << b for b in range(count.bit_length() - 1)]


def relative_order(count):
    return [r for low in (0, 1) for r in range(count) if (r & 1) == low]


def to_relative(rows_first, me, count):
    block = rows_first.shape[0] // count
    parts = [
        lax.dynamic_slice_in_dim(rows_first, (me ^ r) * block, block, axis=0)
        for r in relative_order(count)
    ]
    return jnp.concatenate(parts, axis=0)


def reduce_small(values, me, n_dp, n_t):
    order = relative_order(n_dp)
    buf = values
    left = n_dp
    buf = buf[: left // 2] + lax.ppermute(buf[left // 2 :], "dp", pairs(n_dp, 1))
    left //= 2
    for bit in [b for b in bits_of(n_dp) if b > 1][::-1]:
        buf = buf[: left // 2] + lax.ppermute(buf[left // 2 :], "dp", pairs(n_dp, bit))
        left //= 2
    buf = buf[0]
    for bit in bits_of(n_t):
        buf = buf + lax.ppermute(buf, "tensor", pairs(n_t, bit))
    return buf


MESH = pl.DeviceIdType.MESH


def log2(n):
    return n.bit_length() - 1


def nearest_first(n_t):
    return [sorted(range(n_t), key=lambda p: (abs(p - z), p)) for z in range(n_t)]


def pick(values, z):
    out = jnp.int32(values[0])
    for i in range(1, len(values)):
        out = jnp.where(z == i, jnp.int32(values[i]), out)
    return out


def neighbours(n_dp, n_t, me, z):
    barrier = pltpu.get_barrier_semaphore()
    masks = [1 << b for b in range(log2(n_dp))]
    for mask in masks:
        pl.semaphore_signal(barrier, 1, device_id=(me ^ mask, z), device_id_type=MESH)

    @pl.when(z > 0)
    def _():
        pl.semaphore_signal(barrier, 1, device_id=(me, z - 1), device_id_type=MESH)

    @pl.when(z < n_t - 1)
    def _():
        pl.semaphore_signal(barrier, 1, device_id=(me, z + 1), device_id_type=MESH)

    count = len(masks) + (z > 0).astype(jnp.int32) + (z < n_t - 1).astype(jnp.int32)
    pl.semaphore_wait(barrier, count)


class Gather:
    def __init__(self, n_dp, n_t, me, z, index, shard, whole, sems):
        self.n_dp, self.n_t, self.me, self.z = n_dp, n_t, me, z
        self.index, self.shard, self.whole = index, shard, whole
        self.own, self.z_send, self.z_recv, self.x_send, self.x_recv = sems
        self.bits = log2(n_dp) - 1

    def local(self):
        return pltpu.make_async_copy(
            self.shard, self.whole.at[self.z, self.me], self.own.at[self.index]
        )

    def hop(self, piece, direction, hops):
        source = self.whole.at[piece, self.me]
        step = 1 - 2 * direction
        return pltpu.make_async_remote_copy(
            source,
            source,
            self.z_send.at[self.index, direction, hops],
            self.z_recv.at[self.index, direction, hops],
            device_id=(self.me, jnp.clip(self.z + step, 0, self.n_t - 1)),
            device_id_type=MESH,
        )

    def send_own(self):
        local = self.local()
        local.start()
        local.wait()

        @pl.when(self.z < self.n_t - 1)
        def _():
            self.hop(self.z, 0, 0).start()

        @pl.when(self.z > 0)
        def _():
            self.hop(self.z, 1, 0).start()

    def order(self, k):
        return pick([row[k] for row in nearest_first(self.n_t)], self.z)

    def arrive(self, k):
        if k == 0:
            return
        piece = self.order(k)
        direction = (piece > self.z).astype(jnp.int32)
        hops = jnp.abs(piece - self.z)
        self.hop(piece, direction, hops - 1).wait_recv()
        on = jnp.where(direction == 0, self.z < self.n_t - 1, self.z > 0)

        @pl.when(on)
        def _():
            self.hop(piece, direction, hops).start()

    def doubling(self, k, stage, i, incoming=False):
        piece = self.order(k)
        odd = (piece & 1) == 1
        bit = jnp.where(odd, 1 << (self.bits - stage), 2 << stage)
        shift = jnp.where(odd, self.bits - stage + 1, 1)
        partner = self.me ^ bit
        origin = partner if incoming else self.me
        held = self.whole.at[piece, origin ^ (i << shift)]
        at = (1 << stage) - 1 + i
        return pltpu.make_async_remote_copy(
            held,
            held,
            self.x_send.at[self.index, k, at],
            self.x_recv.at[self.index, k, at],
            device_id=(partner, self.z),
            device_id_type=MESH,
        )

    def core(self, k, i, incoming=False):
        piece = self.order(k)
        partner = self.me ^ 1
        origin = partner if incoming else self.me
        held = self.whole.at[piece, origin ^ (i << 1)]
        at = (1 << self.bits) - 1 + i
        return pltpu.make_async_remote_copy(
            held,
            held,
            self.x_send.at[self.index, k, at],
            self.x_recv.at[self.index, k, at],
            device_id=(partner, self.z),
            device_id_type=MESH,
        )

    def each(self, count, body):
        if count <= 4:
            for i in range(count):
                body(i)
        else:
            lax.fori_loop(0, count, lambda i, _: (body(i), 0)[1], 0)

    def spread(self, k, stage):
        if stage > 0:
            self.each(1 << (stage - 1), lambda i: self.doubling(k, stage - 1, i, True).wait_recv())
        if stage < self.bits:
            self.each(1 << stage, lambda i: self.doubling(k, stage, i).start())
        else:
            self.each(1 << self.bits, lambda i: self.core(k, i).start())

    def finish(self, k):
        self.each(1 << self.bits, lambda i: self.core(k, i, True).wait_recv())
        for stage in range(self.bits):
            self.each(1 << stage, lambda i: self.doubling(k, stage, i).wait_send())
        self.each(1 << self.bits, lambda i: self.core(k, i).wait_send())
        piece = self.order(k)
        hops = jnp.abs(piece - self.z)
        if k == 0:

            @pl.when(self.z < self.n_t - 1)
            def _():
                self.hop(piece, 0, 0).wait_send()

            @pl.when(self.z > 0)
            def _():
                self.hop(piece, 1, 0).wait_send()
        else:
            direction = (piece > self.z).astype(jnp.int32)
            on = jnp.where(direction == 0, self.z < self.n_t - 1, self.z > 0)

            @pl.when(on)
            def _():
                self.hop(piece, direction, hops).wait_send()


class Climb:
    def __init__(self, n_t, me, z, own, kept, sems):
        self.n_t, self.me, self.z, self.own, self.kept = n_t, me, z, own, kept
        self.send, self.recv = sems

    def hop(self, r):
        source = self.own if r == 0 else self.kept[r - 1]
        return pltpu.make_async_remote_copy(
            source,
            self.kept[r],
            self.send.at[r],
            self.recv.at[r],
            device_id=(self.me, jnp.minimum(self.z + 1, self.n_t - 1)),
            device_id_type=MESH,
        )

    def start(self, r):
        @pl.when((self.z >= r) & (self.z < self.n_t - 1))
        def _():
            self.hop(r).start()

    def arrive(self, r):
        @pl.when(self.z >= r)
        def _():
            self.hop(r - 1).wait_recv()

    def finish(self, r):
        @pl.when((self.z >= r) & (self.z < self.n_t - 1))
        def _():
            self.hop(r).wait_send()


def gather_kernel(n_dp, n_t, count, climbs, *refs):
    shards, refs = refs[:count], refs[count:]
    if climbs:
        own, refs = refs[0], refs[1:]
    wholes, refs = refs[:count], refs[count:]
    if climbs:
        kept, refs = refs[: n_t - 1], refs[n_t - 1 :]
    sems, refs = refs[:5], refs[5:]
    me, z = lax.axis_index("dp"), lax.axis_index("tensor")
    neighbours(n_dp, n_t, me, z)
    works = [
        Gather(n_dp, n_t, me, z, c, shards[c], wholes[c], sems) for c in range(count)
    ]
    climb = Climb(n_t, me, z, own, kept, refs) if climbs else None
    stages = log2(n_dp)
    works[0].send_own()
    if climbs:
        climb.start(0)
    total = count * n_t
    passed = 0
    for n in range(total + 2 * (stages - 1)):
        if n < total:
            c, k = divmod(n, n_t)
            works[c].arrive(k)
            works[c].spread(k, 0)
            if k == 0 and c + 1 < count:
                works[c + 1].send_own()
            if climbs and n in (5, 9, 13)[: n_t - 1]:
                passed += 1
                climb.arrive(passed)
                if passed < n_t - 1:
                    climb.start(passed)
        for stage in range(1, stages):
            at = n - 2 * stage
            if 0 <= at < total:
                works[at // n_t].spread(at % n_t, stage)
    for c in range(count):
        for k in range(n_t):
            works[c].finish(k)
    if climbs:
        for r in range(n_t - 1):
            climb.finish(r)


def gather(shards, n_dp, n_t, collective_id, own=None):
    count = len(shards)
    shapes = [
        jax.ShapeDtypeStruct((n_t, n_dp) + s.shape, s.dtype) for s in shards
    ]
    args = list(shards)
    scratch = [
        pltpu.SemaphoreType.DMA((count,)),
        pltpu.SemaphoreType.DMA((count, 2, n_t)),
        pltpu.SemaphoreType.DMA((count, 2, n_t)),
        pltpu.SemaphoreType.DMA((count, n_t, n_dp - 1)),
        pltpu.SemaphoreType.DMA((count, n_t, n_dp - 1)),
    ]
    if own is not None:
        args.append(own)
        shapes += [jax.ShapeDtypeStruct(own.shape, own.dtype)] * (n_t - 1)
        scratch += [pltpu.SemaphoreType.DMA((n_t,))] * 2
    anywhere = pl.BlockSpec(memory_space=pl.ANY)
    return pl.pallas_call(
        functools.partial(gather_kernel, n_dp, n_t, count, own is not None),
        in_specs=[anywhere] * len(args),
        out_specs=[anywhere] * len(shapes),
        out_shape=shapes,
        scratch_shapes=scratch,
        compiler_params=pltpu.CompilerParams(collective_id=collective_id, has_side_effects=True),
        name="gather_weights",
    )(*args)


def greet_all(n_dp, n_t, me, z):
    barrier = pltpu.get_barrier_semaphore()
    masks = [1 << b for b in range(log2(n_dp))]
    for mask in masks:
        pl.semaphore_signal(barrier, 1, device_id=(me ^ mask, z), device_id_type=MESH)
    for other in range(1, n_t):
        pl.semaphore_signal(barrier, 1, device_id=(me, z ^ other), device_id_type=MESH)
    pl.semaphore_wait(barrier, len(masks) + n_t - 1)


def count_of(shape):
    return math.prod(shape)


def add_blocks(target, source, dtype=bf16):
    lead = target.shape[:-2]

    def body(i, _):
        at = []
        for extent in lead[::-1]:
            at.append(lax.rem(i, extent))
            i = i // extent
        at = tuple(at[::-1])
        target[at] = (target[at].astype(f32) + source[at].astype(f32)).astype(dtype)
        return 0

    lax.fori_loop(0, count_of(lead), body, 0)


class Scatter:
    def __init__(self, n_dp, n_t, me, z, index, keep, send, land, out, held, tile, landings, sems):
        self.n_t, self.me, self.z, self.index = n_t, me, z, index
        self.keep, self.send, self.land, self.out, self.held = keep, send, land, out, held
        self.tile, self.landings, self.sems = tile, landings, sems
        self.bits, self.t_bits = log2(n_dp) - 1, log2(n_t)
        self.stages = 2 + self.bits + self.t_bits
        self.cols = held.shape[-1]

    def remote(self, source, target, slot, dp, z):
        send, recv = self.sems[0], self.sems[1]
        return pltpu.make_async_remote_copy(
            source,
            target,
            send.at[self.index, slot],
            recv.at[self.index, slot],
            device_id=(dp, z),
            device_id_type=MESH,
        )

    def load(self):
        return pltpu.make_async_copy(self.keep, self.held, self.sems[2].at[self.index])

    def core(self):
        return self.remote(self.send, self.land, 0, self.me ^ 1, self.z)

    def part(self, half, stage, bit):
        rest = (slice(None),) * (self.bits - 1 - stage)
        done = (0,) * stage
        if half == 0:
            return self.held.at[(slice(0, self.n_t // 2),) + rest + (bit,) + done]
        return self.held.at[(slice(self.n_t // 2, self.n_t),) + done + (bit,) + rest]

    def landing(self, which):
        ref = self.landings[which]
        at = (self.index % 2,) + (slice(None),) * (len(ref.shape) - 2) + (slice(0, self.cols),)
        return ref.at[at]

    def plane(self, half, stage):
        mask = 2 << stage if half == 0 else 1 << (self.bits - stage)
        return self.remote(
            self.part(half, stage, 1),
            self.landing(2 * stage + half),
            1 + 2 * stage + half,
            self.me ^ mask,
            self.z,
        )

    def column(self, stage, first, count):
        return self.held.at[(slice(first, first + count),) + (0,) * self.bits]

    def along(self, stage):
        count = self.n_t >> (stage + 1)
        return self.remote(
            self.column(stage, count, count),
            self.landing(2 * self.bits + stage),
            1 + 2 * self.bits + stage,
            self.me,
            self.z ^ count,
        )

    def start(self, stage):
        if stage < self.bits:
            self.plane(0, stage).start()
            self.plane(1, stage).start()
        elif stage < self.bits + self.t_bits:
            self.along(stage - self.bits).start()

    def event(self, number):
        if number == 0:
            self.core().start()
            self.load().start()
        elif number == 1:
            self.load().wait()
            self.core().wait_recv()
            self.add_land()
            self.start(0)
        elif number <= 1 + self.bits:
            stage = number - 2
            for half in (0, 1):
                self.plane(half, stage).wait_recv()
                add_blocks(self.part(half, stage, 0), self.landing(2 * stage + half))
            self.start(stage + 1)
        else:
            stage = number - 2 - self.bits
            self.along(stage).wait_recv()
            count = self.n_t >> (stage + 1)
            if stage < self.t_bits - 1:
                add_blocks(
                    self.column(stage, 0, count), self.landing(2 * self.bits + stage)
                )
                self.start(number - 1)
            else:
                mine = self.held[(0,) * (1 + self.bits)].astype(f32)
                got = self.landing(2 * self.bits + stage)[0].astype(f32)
                self.out[...] = mine + got

    def add_land(self):
        lead = self.held.shape[:-2]

        def at_of(i):
            at = []
            for extent in lead[::-1]:
                at.append(lax.rem(i, extent))
                i = i // extent
            return tuple(at[::-1])

        def fetch(i):
            return pltpu.make_async_copy(
                self.land.at[at_of(i)],
                self.tile.at[lax.rem(i, 2), :, pl.ds(0, self.cols)],
                self.sems[3].at[lax.rem(i, 2)],
            )

        total = count_of(lead)
        fetch(0).start()

        def body(i, _):
            @pl.when(i + 1 < total)
            def _():
                fetch(i + 1).start()

            fetch(i).wait()
            at = at_of(i)
            got = self.tile[lax.rem(i, 2), :, pl.ds(0, self.cols)].astype(f32)
            self.held[at] = (self.held[at].astype(f32) + got).astype(bf16)
            return 0

        lax.fori_loop(0, total, body, 0)

    def finish(self):
        self.core().wait_send()
        for stage in range(self.bits):
            for half in (0, 1):
                self.plane(half, stage).wait_send()
        for stage in range(self.t_bits):
            self.along(stage).wait_send()


class Descend:
    def __init__(self, n_t, me, z, sums, landed, sems):
        self.n_t, self.me, self.z = n_t, me, z
        self.sums, self.landed, self.send, self.recv = sums, landed, sems[0], sems[1]

    def hop(self, r):
        return pltpu.make_async_remote_copy(
            self.sums[r],
            self.landed[r - 1],
            self.send.at[r],
            self.recv.at[r],
            device_id=(self.me, jnp.maximum(self.z - 1, 0)),
            device_id_type=MESH,
        )

    def start(self, r):
        @pl.when(self.z >= r)
        def _():
            self.hop(r).start()

    def finish(self, r):
        @pl.when(self.z >= r)
        def _():
            self.hop(r).wait_send()


def attention_part(r, group, n_t, z, length, q_ref, do_ref, lse_ref, delta_ref, kv_ref, got_ref, dq_ref, sum_ref):
    rows = q_ref.shape[1]
    groups = lse_ref.shape[0]
    per = group * HEAD_SIZE
    first = z * rows
    active = z >= r
    fresh = r == n_t - 1

    def beside(ref, base):
        return jnp.concatenate(
            [ref[pl.ds(base + a * HEAD_SIZE, HEAD_SIZE), :] for a in range(group)], axis=1
        )

    @pl.when(active)
    def _():
        def body(g, _):
            base = pl.multiple_of(g * per, 32)
            at = pl.multiple_of(g * HEAD_SIZE, 32)
            q = beside(q_ref, base)
            do = beside(do_ref, base)
            delta, lse = delta_ref[g], lse_ref[g]
            dq = jnp.zeros(q.shape, f32)
            for j in range(rows // KEY_TILE):
                part = slice(j * KEY_TILE, (j + 1) * KEY_TILE)
                k, v = kv_ref[0, pl.ds(at, HEAD_SIZE), part], kv_ref[1, pl.ds(at, HEAD_SIZE), part]
                s = dot(k, q, ((0,), (0,)))
                ok = key_mask(s, first - r * rows + j * KEY_TILE, first, length, rows, r == 0)
                p = jnp.where(ok, jnp.exp2(s * SCALE2 - lse), 0.0)
                dp = dot(v, do, ((0,), (0,)))
                ds = (p * (dp - delta)).astype(bf16)
                dv = dot(do, p.astype(bf16), ((1,), (1,)))
                dk = dot(q, ds, ((1,), (1,))) * SCALE
                sum_ref[0, pl.ds(at, HEAD_SIZE), part] = dk.astype(bf16)
                sum_ref[1, pl.ds(at, HEAD_SIZE), part] = dv.astype(bf16)
                dq += dot(k, ds)
            for a in range(group):
                own = pl.ds(base + a * HEAD_SIZE, HEAD_SIZE)
                term = dq[:, a * rows : (a + 1) * rows] * SCALE
                if fresh:
                    dq_ref[own, :] = term
                else:
                    dq_ref[own, :] += term
            return 0

        lax.fori_loop(0, groups, body, 0)

    @pl.when(jnp.logical_not(active))
    def _():
        sum_ref[...] = jnp.zeros_like(sum_ref)
        if fresh:
            dq_ref[...] = jnp.zeros_like(dq_ref)


def scatter_kernel(n_dp, n_t, count, group, *refs):
    refs = list(refs)

    def take(k):
        out = refs[:k]
        del refs[:k]
        return out

    attention = group > 0
    keeps, sends = take(count), take(count)
    if attention:
        (sc_ref, q_ref, do_ref, lse_ref, delta_ref) = take(5)
        kvs = take(n_t)
    lands, outs = take(count), take(count)
    if attention:
        dq_ref, dkv_ref = take(2)
    helds = take(count)
    (tile,) = take(1)
    landings = take(2 * (log2(n_dp) - 1) + log2(n_t))
    sems = take(4)
    me, z = lax.axis_index("dp"), lax.axis_index("tensor")
    greet_all(n_dp, n_t, me, z)
    works = [
        Scatter(
            n_dp, n_t, me, z, c, keeps[c], sends[c], lands[c], outs[c], helds[c], tile, landings, sems
        )
        for c in range(count)
    ]
    stages = works[0].stages

    def tick(k):
        for number in range(stages - 1, 0, -1):
            c = k - (number - 1)
            if 0 <= c < count:
                works[c].event(number)
        if k + 2 < count:
            works[k + 2].event(0)

    works[0].event(0)
    if count > 1:
        works[1].event(0)
    ticks = list(range(count + stages - 2))
    if attention:
        sums = take(n_t - 1)
        landed = take(n_t - 1)
        chain_sems = take(2)
        length = sc_ref[1]
        descend = Descend(n_t, me, z, [dkv_ref] + sums, landed, chain_sems)
        for r in range(n_t - 1, -1, -1):
            target = dkv_ref if r == 0 else sums[r - 1]
            attention_part(
                r, group, n_t, z, length, q_ref, do_ref, lse_ref, delta_ref, kvs[r], None, dq_ref, target
            )
            if r < n_t - 1:
                @pl.when((z + 1 < n_t) & (z >= r))
                def _():
                    descend.hop(r + 1).wait_recv()
                    add_blocks(target, landed[r])

            if r > 0:
                descend.start(r)
            tick(ticks.pop(0))
    for k in ticks:
        tick(k)
    for work in works:
        work.finish()
    if attention:
        for r in range(1, n_t):
            descend.finish(r)


def scatter(keeps, sends, n_dp, n_t, collective_id, attention=None):
    count = len(keeps)
    bits = log2(n_dp) - 1
    block = keeps[0].shape[1] >> bits
    widest = max(k.shape[2] for k in keeps)
    shapes = [(n_t,) + (2,) * bits + (block, k.shape[2]) for k in keeps]
    args = [k.reshape(s) for k, s in zip(keeps, shapes)] + [
        k.reshape(s) for k, s in zip(sends, shapes)
    ]
    anywhere = pl.BlockSpec(memory_space=pl.ANY)
    vmem = pl.BlockSpec(memory_space=pltpu.VMEM)
    smem = pl.BlockSpec(memory_space=pltpu.SMEM)
    in_specs = [anywhere] * len(args)
    out_shape = [jax.ShapeDtypeStruct(s, bf16) for s in shapes] + [
        jax.ShapeDtypeStruct((block, s[-1]), f32) for s in shapes
    ]
    out_specs = [anywhere] * count + [vmem] * count
    scratch = [pltpu.VMEM(s, bf16) for s in shapes]
    scratch.append(pltpu.VMEM((2, block, widest), bf16))
    for stage in range(bits):
        for _ in (0, 1):
            scratch.append(
                pltpu.VMEM((2, n_t // 2) + (2,) * (bits - 1 - stage) + (block, widest), bf16)
            )
    for stage in range(log2(n_t)):
        scratch.append(pltpu.VMEM((2, n_t >> (stage + 1), block, widest), bf16))
    copies = 1 + 2 * bits + log2(n_t)
    scratch += [
        pltpu.SemaphoreType.DMA((count, copies)),
        pltpu.SemaphoreType.DMA((count, copies)),
        pltpu.SemaphoreType.DMA((count,)),
        pltpu.SemaphoreType.DMA((2,)),
    ]
    group = 0
    if attention is not None:
        sc, q, do, lse, delta, kvs = attention
        args += [sc, q, do, lse, delta] + list(kvs)
        in_specs += [smem] + [vmem] * (4 + n_t)
        group = q.shape[0] // kvs[0].shape[1]
        out_shape += [jax.ShapeDtypeStruct(q.shape, f32), jax.ShapeDtypeStruct(kvs[0].shape, bf16)]
        out_specs += [vmem, vmem]
        scratch += [pltpu.VMEM(kvs[0].shape, bf16)] * (2 * (n_t - 1))
        scratch += [pltpu.SemaphoreType.DMA((n_t,))] * 2
    outs = pl.pallas_call(
        functools.partial(scatter_kernel, n_dp, n_t, count, group),
        in_specs=in_specs,
        out_specs=out_specs,
        out_shape=out_shape,
        scratch_shapes=scratch,
        compiler_params=pltpu.CompilerParams(
            collective_id=collective_id, has_side_effects=True, vmem_limit_bytes=62 * 1024 * 1024
        ),
        name="scatter_grads",
    )(*args)
    return outs[count:]


def local(
    n_dp,
    n_t,
    tokens,
    lengths,
    cotangent,
    attn_gain,
    query_weight,
    key_matrix,
    value_matrix,
    out_weight,
    mlp_gain,
    gate_weight,
    up_weight,
    down_weight,
):
    rows, width = tokens.shape
    block = query_weight.shape[0]
    nq, nk = query_weight.shape[1], key_matrix.shape[1]
    no = out_weight.shape[0]
    units = gate_weight.shape[1]
    tile = units // CHUNKS
    me_dp = lax.axis_index("dp")
    me_t = lax.axis_index("tensor")
    length = lengths[0]
    me = jnp.stack([me_t, me_t]).astype(jnp.int32)
    sc = jnp.stack([me_t.astype(jnp.int32), length])

    gains = jnp.stack([attn_gain, mlp_gain], axis=1)
    gains = jnp.pad(gains, ((0, 0), (0, GAIN_LANES - 2)))
    shard_qkv = jnp.concatenate([query_weight, key_matrix, value_matrix, gains], axis=1)
    down_t = down_weight.T
    shard_mlp = []
    for c in range(CHUNKS):
        cols = slice(c * tile, (c + 1) * tile)
        shard_mlp.append(
            jnp.concatenate([gate_weight[:, cols], up_weight[:, cols], down_t[:, cols]], axis=1)
        )
    (w_qkv,) = gather([shard_qkv], n_dp, n_t, 0)
    w_qkv = w_qkv.reshape(n_t, width, shard_qkv.shape[1])
    gain_cols = w_qkv[0, :, nq + 2 * nk : nq + 2 * nk + 2].astype(f32)
    gain_one, gain_two = gain_cols[:, 0], gain_cols[:, 1]

    position = (me_t * rows + jnp.arange(rows, dtype=jnp.int32)).astype(f32)
    freqs = rope_base ** (-(jnp.arange(HALF, dtype=f32) * 2.0) / HEAD_SIZE)
    angles = freqs[:, None] * position[None, :]
    cosine, sine = jnp.cos(angles), jnp.sin(angles)
    live = (me_t * rows + jnp.arange(rows, dtype=jnp.int32) < length).astype(f32)[:, None]
    x = tokens.astype(f32)
    inv_one = lax.rsqrt(jnp.mean(x * x, axis=1, keepdims=True) + eps_norm)
    g32 = cotangent.astype(f32) * live
    g = g32.astype(bf16)
    gt = to_relative(g.T, me_dp, n_dp)
    n1 = (x * inv_one * gain_one).astype(bf16)
    q, kv = qkv_project(n1, w_qkv, cosine, sine, nq, nk)
    q = q.reshape(n_t * nq, rows)

    *w_all, = gather([out_weight.T] + shard_mlp, n_dp, n_t, 1, kv)
    kvs = [kv] + w_all[1 + CHUNKS :]
    w_all = w_all[: 1 + CHUNKS]
    w_out, *w_mlp = [w.reshape(n_t, width, w.shape[-1]) for w in w_all]
    att, lse = attend(sc, q, kvs)
    att_z = att.reshape(n_t, no, rows)
    h_one = out_project(att_z, w_out, tokens, no, 0)

    inv_two = lax.rsqrt(jnp.mean(h_one * h_one, axis=1, keepdims=True) + eps_norm)
    n2 = (h_one * inv_two * gain_two).astype(bf16)
    n2t = to_relative(n2.T, me_dp, n_dp)
    carry = None
    shares = []
    for c in range(CHUNKS):
        out_sum, dn_sum, keep, send = mlp(me, n2, n2t, g, gt, w_mlp[c], 0, tile, carry)
        carry = (out_sum, dn_sum)
        shares.append((keep, send))
    mlp_out, d_n2 = carry
    block_out = (live * (h_one + mlp_out)).astype(bf16)

    scaled = d_n2 * gain_two
    inner = jnp.mean(scaled * h_one, axis=1, keepdims=True)
    gain_two_part = jnp.sum(d_n2 * h_one * inv_two, axis=0)
    d_h = g32 + inv_two * scaled - h_one * (inv_two * inv_two * inv_two * inner)
    d_h_low = d_h.astype(bf16)
    d_h_t = to_relative(d_h_low.T, me_dp, n_dp)
    d_att, keep, send = out_back(me, d_h_low, d_h_t, att_z, w_out, no, 0)
    shares.append((keep, send))

    d_att = d_att.reshape(n_t * no, rows)
    groups, _, lanes = lse.shape
    delta = (d_att.astype(f32) * att.astype(f32)).reshape(groups, -1, HEAD_SIZE, rows).sum(axis=2)
    delta = delta.reshape(groups, 1, lanes)
    *grads, out_share, d_q, d_kv = scatter(
        [s[0] for s in shares],
        [s[1] for s in shares],
        n_dp,
        n_t,
        2,
        (sc, q, d_att, lse, delta, kvs),
    )
    n1t = to_relative(n1.T, me_dp, n_dp)
    d_n1, keep, send = qkv_back(
        me, d_q.reshape(n_t, nq, rows), d_kv, cosine, sine, n1t, w_qkv, nq, nk
    )
    middle = nq
    q_share, kv_share = scatter(
        [keep[:, :, :middle], keep[:, :, middle:]], [send[:, :, :middle], send[:, :, middle:]], n_dp, n_t, 3
    )

    scaled = d_n1 * gain_one
    inner = jnp.mean(scaled * x, axis=1, keepdims=True)
    gain_one_part = jnp.sum(d_n1 * x * inv_one, axis=0)
    d_x = inv_one * scaled - x * (inv_one * inv_one * inv_one * inner)
    tokens_grad = (d_h + d_x).astype(bf16)

    gain_parts = jnp.stack([gain_one_part.reshape(n_dp, block), gain_two_part.reshape(n_dp, block)], 1)
    gain_parts = to_relative(gain_parts, me_dp, n_dp)
    gain_share = reduce_small(gain_parts, me_dp, n_dp, n_t)

    gate_share = jnp.concatenate([s[:, :tile] for s in grads], axis=1)
    up_share = jnp.concatenate([s[:, tile : 2 * tile] for s in grads], axis=1)
    down_share = jnp.concatenate([s[:, 2 * tile :].T for s in grads], axis=0)
    return (
        block_out,
        tokens_grad,
        gain_share[0],
        q_share,
        kv_share[:, :nk],
        kv_share[:, nk:],
        out_share.T,
        gain_share[1],
        gate_share,
        up_share,
        down_share,
    )


def solution(mesh):
    in_specs = (
        P(("dp", "tensor"), None),
        P("dp"),
        P(("dp", "tensor"), None),
        P("dp"),
        P("dp", "tensor"),
        P("dp", "tensor"),
        P("dp", "tensor"),
        P("tensor", "dp"),
        P("dp"),
        P("dp", "tensor"),
        P("dp", "tensor"),
        P("tensor", "dp"),
    )
    out_specs = (
        P(("dp", "tensor"), None),
        P(("dp", "tensor"), None),
        P("dp"),
        P("dp", "tensor"),
        P("dp", "tensor"),
        P("dp", "tensor"),
        P("tensor", "dp"),
        P("dp"),
        P("dp", "tensor"),
        P("dp", "tensor"),
        P("tensor", "dp"),
    )
    fn = functools.partial(local, mesh.shape["dp"], mesh.shape["tensor"])
    return jax.shard_map(fn, mesh=mesh, in_specs=in_specs, out_specs=out_specs, check_vma=False)
```

```python
import functools
import math

import jax
import jax.numpy as jnp
from jax import lax
from jax.experimental import pallas as pl
from jax.experimental.pallas import tpu as pltpu
from jax.sharding import PartitionSpec as P

HEAD_SIZE = 96
HALF = HEAD_SIZE // 2
GAIN_LANES = 128
CHUNKS = 4
CLIMB_AT = 8
CLIMB_STEP = 5
KEY_TILE = 256
NEG = -1e30

eps_norm = 1e-05
rope_base = 100000.0
SCALE = 1.0 / math.sqrt(HEAD_SIZE)
SCALE2 = SCALE * math.log2(math.e)

f32 = jnp.float32
bf16 = jnp.bfloat16
VMEM_LIMIT = 56 * 1024 * 1024


def dot(a, b, dims=((1,), (0,))):
    return lax.dot_general(a, b, (dims, ((), ())), preferred_element_type=f32)


def params(*semantics):
    return pltpu.CompilerParams(dimension_semantics=semantics, vmem_limit_bytes=VMEM_LIMIT)


def cost(flops, nbytes, trans=0):
    return pl.CostEstimate(flops=int(flops), bytes_accessed=int(nbytes), transcendentals=int(trans))


def place(ref, me_ref, grad, col=0):
    count, block = ref.shape[1], ref.shape[2]
    for d in range(count):
        r = me_ref[1] ^ d
        at = (r & 1) * (count // 2) + (r >> 1)
        ref[0, at, :, col : col + grad.shape[1]] = grad[d * block : (d + 1) * block]


def turn(y, cosine, sine, sign):
    parts = []
    for h in range(y.shape[0] // HEAD_SIZE):
        a = y[h * HEAD_SIZE : h * HEAD_SIZE + HALF]
        b = y[h * HEAD_SIZE + HALF : (h + 1) * HEAD_SIZE]
        parts.append(a * cosine - sign * (b * sine))
        parts.append(b * cosine + sign * (a * sine))
    return jnp.concatenate(parts, axis=0)


def qkv_kernel(nq, nk, n1_ref, w_ref, cos_ref, sin_ref, q_ref, kv_ref):
    w = w_ref[0, :, : nq + 2 * nk]
    y = dot(n1_ref[...], w).T
    cosine, sine = cos_ref[...], sin_ref[...]
    q_ref[0] = turn(y[:nq], cosine, sine, 1.0).astype(bf16)
    kv_ref[0] = turn(y[nq : nq + nk], cosine, sine, 1.0).astype(bf16)
    kv_ref[1] = y[nq + nk :].astype(bf16)


def qkv_project(n1, w, cosine, sine, nq, nk):
    rows, width = n1.shape
    zs, _, cols = w.shape
    return pl.pallas_call(
        functools.partial(qkv_kernel, nq, nk),
        grid=(zs,),
        in_specs=[
            pl.BlockSpec((rows, width), lambda z: (0, 0)),
            pl.BlockSpec((1, width, cols), lambda z: (z, 0, 0)),
            pl.BlockSpec((HALF, rows), lambda z: (0, 0)),
            pl.BlockSpec((HALF, rows), lambda z: (0, 0)),
        ],
        out_specs=[
            pl.BlockSpec((1, nq, rows), lambda z: (z, 0, 0)),
            pl.BlockSpec((2, nk, rows), lambda z: (0, z, 0)),
        ],
        out_shape=[
            jax.ShapeDtypeStruct((zs, nq, rows), bf16),
            jax.ShapeDtypeStruct((2, zs * nk, rows), bf16),
        ],
        compiler_params=params("arbitrary"),
        cost_estimate=cost(2 * rows * width * cols * zs, 2 * zs * width * cols + 8 * rows * width),
        name="qkv_project",
    )(n1, w, cosine, sine)


def out_kernel(att_ref, w_ref, x_ref, h_ref):
    z = pl.program_id(0)

    @pl.when(z == 0)
    def _():
        h_ref[...] = x_ref[...].astype(f32)

    h_ref[...] += dot(att_ref[0].T, w_ref[0], ((1,), (1,)))


def out_project(att, w, x, no, col):
    zs, _, rows = att.shape
    width = x.shape[1]
    return pl.pallas_call(
        out_kernel,
        grid=(zs,),
        in_specs=[
            pl.BlockSpec((1, no, rows), lambda z: (z, 0, 0)),
            pl.BlockSpec((1, width, no), lambda z: (z, 0, col)),
            pl.BlockSpec((rows, width), lambda z: (0, 0)),
        ],
        out_specs=pl.BlockSpec((rows, width), lambda z: (0, 0)),
        out_shape=jax.ShapeDtypeStruct((rows, width), f32),
        compiler_params=params("arbitrary"),
        cost_estimate=cost(2 * rows * width * no * zs, 2 * zs * width * no + 8 * rows * width),
        name="out_project",
    )(att, w, x)


def out_back_kernel(me_ref, dh_ref, dht_ref, att_ref, w_ref, da_ref, grad_ref):
    w = w_ref[0]
    da_ref[0] = dot(dh_ref[...], w).T.astype(bf16)
    place(grad_ref, me_ref, dot(dht_ref[...], att_ref[0].T).astype(bf16))


def out_back(me, dh, dht, att, w, no, col, n_dp):
    zs, _, rows = att.shape
    width = dh.shape[1]
    block = width // n_dp
    return pl.pallas_call(
        out_back_kernel,
        grid_spec=pltpu.PrefetchScalarGridSpec(
            num_scalar_prefetch=1,
            grid=(zs,),
            in_specs=[
                pl.BlockSpec((rows, width), lambda z, m: (0, 0)),
                pl.BlockSpec((width, rows), lambda z, m: (0, 0)),
                pl.BlockSpec((1, no, rows), lambda z, m: (z, 0, 0)),
                pl.BlockSpec((1, width, no), lambda z, m: (z, 0, col)),
            ],
            out_specs=[
                pl.BlockSpec((1, no, rows), lambda z, m: (z, 0, 0)),
                pl.BlockSpec((1, n_dp, block, no), lambda z, m: (z ^ m[0], 0, 0, 0)),
            ],
        ),
        out_shape=[
            jax.ShapeDtypeStruct((zs, no, rows), bf16),
            jax.ShapeDtypeStruct((zs, n_dp, block, no), bf16),
        ],
        compiler_params=params("arbitrary"),
        cost_estimate=cost(4 * rows * width * no * zs, 4 * zs * width * no + 8 * rows * width),
        name="out_back",
    )(me, dh, dht, att, w)


def qkv_back_kernel(
    nq, nk, me_ref, dq_ref, dkv_ref, cos_ref, sin_ref, n1t_ref, w_ref, dn_ref, dwq_ref, dwkv_ref
):
    z = pl.program_id(0)

    @pl.when(z == 0)
    def _():
        dn_ref[...] = jnp.zeros_like(dn_ref)

    cosine, sine = cos_ref[...], sin_ref[...]
    dq = turn(dq_ref[0], cosine, sine, -1.0).astype(bf16)
    dk = turn(dkv_ref[0].astype(f32), cosine, sine, -1.0).astype(bf16)
    d = jnp.concatenate([dq, dk, dkv_ref[1]], axis=0).T
    w = w_ref[0, :, : nq + 2 * nk]
    dn_ref[...] += dot(d, w, ((1,), (1,)))
    grad = dot(n1t_ref[...], d).astype(bf16)
    place(dwq_ref, me_ref, grad[:, :nq])
    place(dwkv_ref, me_ref, grad[:, nq:])


def qkv_back(me, dq, dkv, cosine, sine, n1t, w, nq, nk, n_dp):
    zs, _, rows = dq.shape
    width = n1t.shape[0]
    block = width // n_dp
    cols = w.shape[2]
    out = nq + 2 * nk
    return pl.pallas_call(
        functools.partial(qkv_back_kernel, nq, nk),
        grid_spec=pltpu.PrefetchScalarGridSpec(
            num_scalar_prefetch=1,
            grid=(zs,),
            in_specs=[
                pl.BlockSpec((1, nq, rows), lambda z, m: (z, 0, 0)),
                pl.BlockSpec((2, nk, rows), lambda z, m: (0, z, 0)),
                pl.BlockSpec((HALF, rows), lambda z, m: (0, 0)),
                pl.BlockSpec((HALF, rows), lambda z, m: (0, 0)),
                pl.BlockSpec((width, rows), lambda z, m: (0, 0)),
                pl.BlockSpec((1, width, cols), lambda z, m: (z, 0, 0)),
            ],
            out_specs=[
                pl.BlockSpec((rows, width), lambda z, m: (0, 0)),
                pl.BlockSpec((1, n_dp, block, nq), lambda z, m: (z ^ m[0], 0, 0, 0)),
                pl.BlockSpec((1, n_dp, block, 2 * nk), lambda z, m: (z ^ m[0], 0, 0, 0)),
            ],
        ),
        out_shape=[
            jax.ShapeDtypeStruct((rows, width), f32),
            jax.ShapeDtypeStruct((zs, n_dp, block, nq), bf16),
            jax.ShapeDtypeStruct((zs, n_dp, block, 2 * nk), bf16),
        ],
        compiler_params=params("arbitrary"),
        cost_estimate=cost(4 * rows * width * out * zs, 4 * zs * width * cols + 8 * rows * width),
        name="qkv_back",
    )(me, dq, dkv, cosine, sine, n1t, w)


def key_mask(s, key_first, query_first, length, rows, diagonal):
    key = key_first + lax.broadcasted_iota(jnp.int32, (s.shape[0], 1), 0)
    ok = key < length
    if diagonal:
        lane = lax.broadcasted_iota(jnp.int32, s.shape, 1)
        query = query_first + lax.rem(lane, rows)
        ok = ok & (key <= query)
    return jnp.broadcast_to(ok, s.shape)


def mlp_kernel(
    tile, first, me_ref, n2_ref, n2t_ref, g_ref, gt_ref, w_ref, *refs
):
    if first:
        out_ref, dn_ref, grad_ref = refs
    else:
        out_in, dn_in, out_ref, dn_ref, grad_ref = refs
    z = pl.program_id(0)

    @pl.when(z == 0)
    def _():
        if first:
            out_ref[...] = jnp.zeros_like(out_ref)
            dn_ref[...] = jnp.zeros_like(dn_ref)
        else:
            out_ref[...] = out_in[...]
            dn_ref[...] = dn_in[...]

    wg = w_ref[0, :, :tile]
    wu = w_ref[0, :, tile : 2 * tile]
    wd = w_ref[0, :, 2 * tile : 3 * tile]
    n2, g = n2_ref[...], g_ref[...]
    gate = dot(n2, wg)
    up = dot(n2, wu)
    d_hidden = dot(g, wd)
    sigma = 1.0 / (1.0 + jnp.exp(-gate))
    active = gate * sigma
    hidden = (active * up).astype(bf16)
    d_gate = (d_hidden * up * (sigma * (1.0 + gate * (1.0 - sigma)))).astype(bf16)
    d_up = (d_hidden * active).astype(bf16)
    out_ref[...] += dot(hidden, wd, ((1,), (1,)))
    dn_ref[...] += dot(d_gate, wg, ((1,), (1,))) + dot(d_up, wu, ((1,), (1,)))
    place(grad_ref, me_ref, dot(n2t_ref[...], d_gate).astype(bf16), 0)
    place(grad_ref, me_ref, dot(n2t_ref[...], d_up).astype(bf16), tile)
    place(grad_ref, me_ref, dot(gt_ref[...], hidden).astype(bf16), 2 * tile)


def mlp(me, n2, n2t, g, gt, w, chunk, tile, carry, n_dp):
    rows, width = n2.shape
    zs = w.shape[0]
    block = width // n_dp
    full = pl.BlockSpec((rows, width), lambda z, m: (0, 0))
    full_t = pl.BlockSpec((width, rows), lambda z, m: (0, 0))
    grad_spec = pl.BlockSpec((1, n_dp, block, 3 * tile), lambda z, m: (z ^ m[0], 0, 0, 0))
    first = carry is None
    in_specs = [
        full,
        full_t,
        full,
        full_t,
        pl.BlockSpec((1, width, 3 * tile), lambda z, m: (z, 0, chunk)),
    ]
    args = [me, n2, n2t, g, gt, w]
    aliases = {}
    if not first:
        in_specs += [full, full]
        aliases = {6: 0, 7: 1}
        args += list(carry)
    return pl.pallas_call(
        functools.partial(mlp_kernel, tile, first),
        grid_spec=pltpu.PrefetchScalarGridSpec(
            num_scalar_prefetch=1,
            grid=(zs,),
            in_specs=in_specs,
            out_specs=[full, full, grad_spec],
        ),
        out_shape=[
            jax.ShapeDtypeStruct((rows, width), f32),
            jax.ShapeDtypeStruct((rows, width), f32),
            jax.ShapeDtypeStruct((zs, n_dp, block, 3 * tile), bf16),
        ],
        input_output_aliases=aliases,
        compiler_params=params("arbitrary"),
        cost_estimate=cost(
            18 * rows * width * tile * zs, 4 * zs * width * 3 * tile + 24 * rows * width
        ),
        name="mlp",
    )(*args)


def pairs(count, mask):
    return [(i, i ^ mask) for i in range(count)]


def bits_of(count):
    return [1 << b for b in range(count.bit_length() - 1)]


def relative_order(count):
    return [r for low in (0, 1) for r in range(count) if (r & 1) == low]


def to_relative(rows_first, me, count):
    block = rows_first.shape[0] // count
    parts = [
        lax.dynamic_slice_in_dim(rows_first, (me ^ r) * block, block, axis=0)
        for r in relative_order(count)
    ]
    return jnp.concatenate(parts, axis=0)


def reduce_small(values, me, n_dp, n_t):
    order = relative_order(n_dp)
    buf = values
    left = n_dp
    buf = buf[: left // 2] + lax.ppermute(buf[left // 2 :], "dp", pairs(n_dp, 1))
    left //= 2
    for bit in [b for b in bits_of(n_dp) if b > 1][::-1]:
        buf = buf[: left // 2] + lax.ppermute(buf[left // 2 :], "dp", pairs(n_dp, bit))
        left //= 2
    buf = buf[0]
    for bit in bits_of(n_t):
        buf = buf + lax.ppermute(buf, "tensor", pairs(n_t, bit))
    return buf


MESH = pl.DeviceIdType.MESH


def log2(n):
    return n.bit_length() - 1


def nearest_first(n_t):
    return [sorted(range(n_t), key=lambda p: (abs(p - z), p)) for z in range(n_t)]


def pick(values, z):
    out = jnp.int32(values[0])
    for i in range(1, len(values)):
        out = jnp.where(z == i, jnp.int32(values[i]), out)
    return out


def neighbours(n_dp, n_t, me, z):
    barrier = pltpu.get_barrier_semaphore()
    masks = [1 << b for b in range(log2(n_dp))]
    for mask in masks:
        pl.semaphore_signal(barrier, 1, device_id=(me ^ mask, z), device_id_type=MESH)

    @pl.when(z > 0)
    def _():
        pl.semaphore_signal(barrier, 1, device_id=(me, z - 1), device_id_type=MESH)

    @pl.when(z < n_t - 1)
    def _():
        pl.semaphore_signal(barrier, 1, device_id=(me, z + 1), device_id_type=MESH)

    count = len(masks) + (z > 0).astype(jnp.int32) + (z < n_t - 1).astype(jnp.int32)
    pl.semaphore_wait(barrier, count)


class Gather:
    def __init__(self, n_dp, n_t, me, z, index, shard, whole, sems):
        self.n_dp, self.n_t, self.me, self.z = n_dp, n_t, me, z
        self.index, self.shard, self.whole = index, shard, whole
        self.own, self.z_send, self.z_recv, self.x_send, self.x_recv = sems
        self.bits = log2(n_dp) - 1

    def local(self):
        return pltpu.make_async_copy(
            self.shard, self.whole.at[self.z, self.me], self.own.at[self.index]
        )

    def hop(self, piece, direction, hops):
        source = self.whole.at[piece, self.me]
        step = 1 - 2 * direction
        return pltpu.make_async_remote_copy(
            source,
            source,
            self.z_send.at[self.index, direction, hops],
            self.z_recv.at[self.index, direction, hops],
            device_id=(self.me, jnp.clip(self.z + step, 0, self.n_t - 1)),
            device_id_type=MESH,
        )

    def send_own(self):
        local = self.local()
        local.start()
        local.wait()

        @pl.when(self.z < self.n_t - 1)
        def _():
            self.hop(self.z, 0, 0).start()

        @pl.when(self.z > 0)
        def _():
            self.hop(self.z, 1, 0).start()

    def order(self, k):
        return pick([row[k] for row in nearest_first(self.n_t)], self.z)

    def arrive(self, k):
        if k == 0:
            return
        piece = self.order(k)
        direction = (piece > self.z).astype(jnp.int32)
        hops = jnp.abs(piece - self.z)
        self.hop(piece, direction, hops - 1).wait_recv()
        on = jnp.where(direction == 0, self.z < self.n_t - 1, self.z > 0)

        @pl.when(on)
        def _():
            self.hop(piece, direction, hops).start()

    def doubling(self, k, stage, i, incoming=False):
        piece = self.order(k)
        odd = (piece & 1) == 1
        bit = jnp.where(odd, 1 << (self.bits - stage), 2 << stage)
        shift = jnp.where(odd, self.bits - stage + 1, 1)
        partner = self.me ^ bit
        origin = partner if incoming else self.me
        held = self.whole.at[piece, origin ^ (i << shift)]
        at = (1 << stage) - 1 + i
        return pltpu.make_async_remote_copy(
            held,
            held,
            self.x_send.at[self.index, k, at],
            self.x_recv.at[self.index, k, at],
            device_id=(partner, self.z),
            device_id_type=MESH,
        )

    def core(self, k, i, incoming=False):
        piece = self.order(k)
        partner = self.me ^ 1
        origin = partner if incoming else self.me
        held = self.whole.at[piece, origin ^ (i << 1)]
        at = (1 << self.bits) - 1 + i
        return pltpu.make_async_remote_copy(
            held,
            held,
            self.x_send.at[self.index, k, at],
            self.x_recv.at[self.index, k, at],
            device_id=(partner, self.z),
            device_id_type=MESH,
        )

    def each(self, count, body):
        if count <= 4:
            for i in range(count):
                body(i)
        else:
            lax.fori_loop(0, count, lambda i, _: (body(i), 0)[1], 0)

    def spread(self, k, stage):
        if stage > 0:
            self.each(1 << (stage - 1), lambda i: self.doubling(k, stage - 1, i, True).wait_recv())
        if stage < self.bits:
            self.each(1 << stage, lambda i: self.doubling(k, stage, i).start())
        else:
            self.each(1 << self.bits, lambda i: self.core(k, i).start())

    def finish(self, k):
        self.each(1 << self.bits, lambda i: self.core(k, i, True).wait_recv())
        for stage in range(self.bits):
            self.each(1 << stage, lambda i: self.doubling(k, stage, i).wait_send())
        self.each(1 << self.bits, lambda i: self.core(k, i).wait_send())
        piece = self.order(k)
        hops = jnp.abs(piece - self.z)
        if k == 0:

            @pl.when(self.z < self.n_t - 1)
            def _():
                self.hop(piece, 0, 0).wait_send()

            @pl.when(self.z > 0)
            def _():
                self.hop(piece, 1, 0).wait_send()
        else:
            direction = (piece > self.z).astype(jnp.int32)
            on = jnp.where(direction == 0, self.z < self.n_t - 1, self.z > 0)

            @pl.when(on)
            def _():
                self.hop(piece, direction, hops).wait_send()


class Climb:
    def __init__(self, n_t, me, z, own, kept, sems):
        self.n_t, self.me, self.z, self.own, self.kept = n_t, me, z, own, kept
        self.send, self.recv = sems

    def hop(self, r):
        source = self.own if r == 0 else self.kept[r - 1]
        return pltpu.make_async_remote_copy(
            source,
            self.kept[r],
            self.send.at[r],
            self.recv.at[r],
            device_id=(self.me, jnp.minimum(self.z + 1, self.n_t - 1)),
            device_id_type=MESH,
        )

    def start(self, r):
        @pl.when((self.z >= r) & (self.z < self.n_t - 1))
        def _():
            self.hop(r).start()

    def arrive(self, r):
        @pl.when(self.z >= r)
        def _():
            self.hop(r - 1).wait_recv()

    def finish(self, r):
        @pl.when((self.z >= r) & (self.z < self.n_t - 1))
        def _():
            self.hop(r).wait_send()


def attend_part(r, z, length, q_ref, kv_ref, m_ref, l_ref, acc_ref):
    rows = q_ref.shape[1]
    groups = m_ref.shape[0]
    group = q_ref.shape[0] // (groups * HEAD_SIZE)
    first = z * rows

    @pl.when(z >= r)
    def _():
        def body(g, _):
            base = pl.multiple_of(g * (group * HEAD_SIZE), 32)
            at = pl.multiple_of(g * HEAD_SIZE, 32)
            q = jnp.concatenate(
                [q_ref[pl.ds(base + a * HEAD_SIZE, HEAD_SIZE), :] for a in range(group)], axis=1
            )
            if r == 0:
                m = jnp.full((1, group * rows), NEG, f32)
                total = jnp.zeros((1, group * rows), f32)
                acc = jnp.zeros((HEAD_SIZE, group * rows), f32)
            else:
                m, total, acc = m_ref[g], l_ref[g], acc_ref[g]
            for j in range(rows // KEY_TILE):
                part = slice(j * KEY_TILE, (j + 1) * KEY_TILE)
                k = kv_ref[0, pl.ds(at, HEAD_SIZE), part]
                v = kv_ref[1, pl.ds(at, HEAD_SIZE), part]
                s = dot(k, q, ((0,), (0,)))
                ok = key_mask(s, first - r * rows + j * KEY_TILE, first, length, rows, r == 0)
                s = jnp.where(ok, s, NEG)
                new = jnp.maximum(m, jnp.max(s, axis=0, keepdims=True))
                shrink = jnp.exp2((m - new) * SCALE2)
                p = jnp.exp2(s * SCALE2 - new * SCALE2)
                total = total * shrink + jnp.sum(p, axis=0, keepdims=True)
                acc = acc * shrink + dot(v, p.astype(bf16))
                m = new
            m_ref[g], l_ref[g], acc_ref[g] = m, total, acc
            return 0

        lax.fori_loop(0, groups, body, 0)


def attend_end(q_shape, m_ref, l_ref, acc_ref, att_ref):
    groups = m_ref.shape[0]
    rows = q_shape[1]
    group = q_shape[0] // (groups * HEAD_SIZE)

    def body(g, _):
        out = acc_ref[g] / l_ref[g]
        for a in range(group):
            own = pl.ds(pl.multiple_of((g * group + a) * HEAD_SIZE, 32), HEAD_SIZE)
            att_ref[own, :] = out[:, a * rows : (a + 1) * rows].astype(bf16)
        m_ref[g] = m_ref[g] * SCALE2 + jnp.log2(l_ref[g])
        return 0

    lax.fori_loop(0, groups, body, 0)


def gather_kernel(n_dp, n_t, count, climbs, *refs):
    refs = list(refs)

    def take(k):
        out = refs[:k]
        del refs[:k]
        return out

    shards = take(count)
    if climbs:
        own, q_ref, length_ref = take(3)
    wholes = take(count)
    if climbs:
        kept = take(n_t - 1)
        att_ref, lse_ref = take(2)
    sems = take(5)
    me, z = lax.axis_index("dp"), lax.axis_index("tensor")
    neighbours(n_dp, n_t, me, z)
    works = [
        Gather(n_dp, n_t, me, z, c, shards[c], wholes[c], sems) for c in range(count)
    ]
    if climbs:
        climb_sems = take(2)
        l_ref, acc_ref, kv_ref, kv_sem = take(4)
        climb = Climb(n_t, me, z, own, kept, climb_sems)
        climb.start(0)
        length = length_ref[0]

    def attend_step(r):
        if r > 0:
            climb.arrive(r)
            if r < n_t - 1:
                climb.start(r)

        @pl.when(z >= r)
        def _():
            fetch = pltpu.make_async_copy(own if r == 0 else kept[r - 1], kv_ref, kv_sem)
            fetch.start()
            fetch.wait()

        attend_part(r, z, length, q_ref, kv_ref, lse_ref, l_ref, acc_ref)

    stages = log2(n_dp)
    works[0].send_own()
    total = count * n_t
    todo = list(range(n_t)) if climbs else []
    for n in range(total + 2 * (stages - 1)):
        if n < total:
            c, k = divmod(n, n_t)
            works[c].arrive(k)
            works[c].spread(k, 0)
            if k == 0 and c + 1 < count:
                works[c + 1].send_own()
        for stage in range(1, stages):
            at = n - 2 * stage
            if 0 <= at < total:
                works[at // n_t].spread(at % n_t, stage)
        if todo and (n == 2 if todo[0] == 0 else n == CLIMB_AT + CLIMB_STEP * (todo[0] - 1)):
            attend_step(todo.pop(0))
    for r in todo:
        attend_step(r)
    if climbs:
        attend_end(q_ref.shape, lse_ref, l_ref, acc_ref, att_ref)
    for c in range(count):
        for k in range(n_t):
            works[c].finish(k)
    if climbs:
        for r in range(n_t - 1):
            climb.finish(r)


def gather(shards, n_dp, n_t, collective_id, attention=None):
    count = len(shards)
    shapes = [
        jax.ShapeDtypeStruct((n_t, n_dp) + s.shape, s.dtype) for s in shards
    ]
    args = list(shards)
    anywhere = pl.BlockSpec(memory_space=pl.ANY)
    vmem = pl.BlockSpec(memory_space=pltpu.VMEM)
    in_specs = [anywhere] * count
    out_specs = [anywhere] * count
    scratch = [
        pltpu.SemaphoreType.DMA((count,)),
        pltpu.SemaphoreType.DMA((count, 2, n_t)),
        pltpu.SemaphoreType.DMA((count, 2, n_t)),
        pltpu.SemaphoreType.DMA((count, n_t, n_dp - 1)),
        pltpu.SemaphoreType.DMA((count, n_t, n_dp - 1)),
    ]
    if attention is not None:
        kv, q, length = attention
        rows = q.shape[1]
        groups = kv.shape[1] // HEAD_SIZE
        lanes = q.shape[0] // (groups * HEAD_SIZE) * rows
        args += [kv, q, length.reshape(1)]
        in_specs += [anywhere, vmem, pl.BlockSpec(memory_space=pltpu.SMEM)]
        shapes += [jax.ShapeDtypeStruct(kv.shape, kv.dtype)] * (n_t - 1)
        shapes += [
            jax.ShapeDtypeStruct(q.shape, bf16),
            jax.ShapeDtypeStruct((groups, 1, lanes), f32),
        ]
        out_specs += [anywhere] * (n_t - 1) + [vmem, vmem]
        scratch += [pltpu.SemaphoreType.DMA((n_t,))] * 2
        scratch += [
            pltpu.VMEM((groups, 1, lanes), f32),
            pltpu.VMEM((groups, HEAD_SIZE, lanes), f32),
            pltpu.VMEM(kv.shape, bf16),
            pltpu.SemaphoreType.DMA,
        ]
    return pl.pallas_call(
        functools.partial(gather_kernel, n_dp, n_t, count, attention is not None),
        in_specs=in_specs,
        out_specs=out_specs,
        out_shape=shapes,
        scratch_shapes=scratch,
        compiler_params=pltpu.CompilerParams(
            collective_id=collective_id, has_side_effects=True, vmem_limit_bytes=VMEM_LIMIT
        ),
        name="gather_weights",
    )(*args)


def greet_all(n_dp, n_t, me, z):
    barrier = pltpu.get_barrier_semaphore()
    masks = [1 << b for b in range(log2(n_dp))]
    for mask in masks:
        pl.semaphore_signal(barrier, 1, device_id=(me ^ mask, z), device_id_type=MESH)
    for other in range(1, n_t):
        pl.semaphore_signal(barrier, 1, device_id=(me, z ^ other), device_id_type=MESH)
    pl.semaphore_wait(barrier, len(masks) + n_t - 1)


def count_of(shape):
    return math.prod(shape)


def add_blocks(target, source, dtype=bf16):
    lead = target.shape[:-2]

    def body(i, _):
        at = []
        for extent in lead[::-1]:
            at.append(lax.rem(i, extent))
            i = i // extent
        at = tuple(at[::-1])
        target[at] = (target[at].astype(f32) + source[at].astype(f32)).astype(dtype)
        return 0

    lax.fori_loop(0, count_of(lead), body, 0)


class Scatter:
    def __init__(self, n_dp, n_t, me, z, index, grad, land, out, held, tile, landings, sems):
        self.n_t, self.me, self.z, self.index = n_t, me, z, index
        self.keep, self.send = grad.at[:, 0], grad.at[:, 1]
        self.land, self.out, self.held = land, out, held
        self.tile, self.landings, self.sems = tile, landings, sems
        self.bits, self.t_bits = log2(n_dp) - 1, log2(n_t)
        self.stages = 2 + self.bits + self.t_bits
        self.cols = held.shape[-1]

    def remote(self, source, target, slot, dp, z):
        send, recv = self.sems[0], self.sems[1]
        return pltpu.make_async_remote_copy(
            source,
            target,
            send.at[self.index, slot],
            recv.at[self.index, slot],
            device_id=(dp, z),
            device_id_type=MESH,
        )

    def load(self):
        return pltpu.make_async_copy(self.keep, self.held, self.sems[2].at[self.index])

    def core(self):
        return self.remote(self.send, self.land, 0, self.me ^ 1, self.z)

    def part(self, half, stage, bit):
        rest = (slice(None),) * (self.bits - 1 - stage)
        done = (0,) * stage
        if half == 0:
            return self.held.at[(slice(0, self.n_t // 2),) + rest + (bit,) + done]
        return self.held.at[(slice(self.n_t // 2, self.n_t),) + done + (bit,) + rest]

    def landing(self, which):
        ref = self.landings[which]
        at = (self.index % 2,) + (slice(None),) * (len(ref.shape) - 2) + (slice(0, self.cols),)
        return ref.at[at]

    def plane(self, half, stage):
        mask = 2 << stage if half == 0 else 1 << (self.bits - stage)
        return self.remote(
            self.part(half, stage, 1),
            self.landing(2 * stage + half),
            1 + 2 * stage + half,
            self.me ^ mask,
            self.z,
        )

    def column(self, stage, first, count):
        return self.held.at[(slice(first, first + count),) + (0,) * self.bits]

    def along(self, stage):
        count = self.n_t >> (stage + 1)
        return self.remote(
            self.column(stage, count, count),
            self.landing(2 * self.bits + stage),
            1 + 2 * self.bits + stage,
            self.me,
            self.z ^ count,
        )

    def start(self, stage):
        if stage < self.bits:
            self.plane(0, stage).start()
            self.plane(1, stage).start()
        elif stage < self.bits + self.t_bits:
            self.along(stage - self.bits).start()

    def event(self, number):
        if number == 0:
            self.core().start()
            self.load().start()
        elif number == 1:
            self.load().wait()
            self.core().wait_recv()
            self.add_land()
            self.start(0)
        elif number <= 1 + self.bits:
            stage = number - 2
            for half in (0, 1):
                self.plane(half, stage).wait_recv()
                add_blocks(self.part(half, stage, 0), self.landing(2 * stage + half))
            self.start(stage + 1)
        else:
            stage = number - 2 - self.bits
            self.along(stage).wait_recv()
            count = self.n_t >> (stage + 1)
            if stage < self.t_bits - 1:
                add_blocks(
                    self.column(stage, 0, count), self.landing(2 * self.bits + stage)
                )
                self.start(number - 1)
            else:
                mine = self.held[(0,) * (1 + self.bits)].astype(f32)
                got = self.landing(2 * self.bits + stage)[0].astype(f32)
                self.out[...] = mine + got

    def add_land(self):
        lead = self.held.shape[:-2]

        def at_of(i):
            at = []
            for extent in lead[::-1]:
                at.append(lax.rem(i, extent))
                i = i // extent
            return tuple(at[::-1])

        def fetch(i):
            return pltpu.make_async_copy(
                self.land.at[at_of(i)],
                self.tile.at[lax.rem(i, 2), :, pl.ds(0, self.cols)],
                self.sems[3].at[lax.rem(i, 2)],
            )

        total = count_of(lead)
        fetch(0).start()

        def body(i, _):
            @pl.when(i + 1 < total)
            def _():
                fetch(i + 1).start()

            fetch(i).wait()
            at = at_of(i)
            got = self.tile[lax.rem(i, 2), :, pl.ds(0, self.cols)].astype(f32)
            self.held[at] = (self.held[at].astype(f32) + got).astype(bf16)
            return 0

        lax.fori_loop(0, total, body, 0)

    def finish(self):
        self.core().wait_send()
        for stage in range(self.bits):
            for half in (0, 1):
                self.plane(half, stage).wait_send()
        for stage in range(self.t_bits):
            self.along(stage).wait_send()


class Descend:
    def __init__(self, n_t, me, z, sums, landed, sems):
        self.n_t, self.me, self.z = n_t, me, z
        self.sums, self.landed, self.send, self.recv = sums, landed, sems[0], sems[1]

    def hop(self, r):
        return pltpu.make_async_remote_copy(
            self.sums[r],
            self.landed[r - 1],
            self.send.at[r],
            self.recv.at[r],
            device_id=(self.me, jnp.maximum(self.z - 1, 0)),
            device_id_type=MESH,
        )

    def start(self, r):
        @pl.when(self.z >= r)
        def _():
            self.hop(r).start()

    def finish(self, r):
        @pl.when(self.z >= r)
        def _():
            self.hop(r).wait_send()


def attention_part(r, group, n_t, z, length, q_ref, do_ref, lse_ref, delta_ref, kv_ref, got_ref, dq_ref, sum_ref):
    rows = q_ref.shape[1]
    groups = lse_ref.shape[0]
    per = group * HEAD_SIZE
    first = z * rows
    active = z >= r
    fresh = r == n_t - 1

    def beside(ref, base):
        return jnp.concatenate(
            [ref[pl.ds(base + a * HEAD_SIZE, HEAD_SIZE), :] for a in range(group)], axis=1
        )

    @pl.when(active)
    def _():
        def body(g, _):
            base = pl.multiple_of(g * per, 32)
            at = pl.multiple_of(g * HEAD_SIZE, 32)
            q = beside(q_ref, base)
            do = beside(do_ref, base)
            delta, lse = delta_ref[g], lse_ref[g]
            dq = jnp.zeros(q.shape, f32)
            for j in range(rows // KEY_TILE):
                part = slice(j * KEY_TILE, (j + 1) * KEY_TILE)
                k, v = kv_ref[0, pl.ds(at, HEAD_SIZE), part], kv_ref[1, pl.ds(at, HEAD_SIZE), part]
                s = dot(k, q, ((0,), (0,)))
                ok = key_mask(s, first - r * rows + j * KEY_TILE, first, length, rows, r == 0)
                p = jnp.where(ok, jnp.exp2(s * SCALE2 - lse), 0.0)
                dp = dot(v, do, ((0,), (0,)))
                ds = (p * (dp - delta)).astype(bf16)
                dv = dot(do, p.astype(bf16), ((1,), (1,)))
                dk = dot(q, ds, ((1,), (1,))) * SCALE
                sum_ref[0, pl.ds(at, HEAD_SIZE), part] = dk.astype(bf16)
                sum_ref[1, pl.ds(at, HEAD_SIZE), part] = dv.astype(bf16)
                dq += dot(k, ds)
            for a in range(group):
                own = pl.ds(base + a * HEAD_SIZE, HEAD_SIZE)
                term = dq[:, a * rows : (a + 1) * rows] * SCALE
                if fresh:
                    dq_ref[own, :] = term
                else:
                    dq_ref[own, :] += term
            return 0

        lax.fori_loop(0, groups, body, 0)

    @pl.when(jnp.logical_not(active))
    def _():
        sum_ref[...] = jnp.zeros_like(sum_ref)
        if fresh:
            dq_ref[...] = jnp.zeros_like(dq_ref)


def scatter_kernel(n_dp, n_t, count, group, *refs):
    refs = list(refs)

    def take(k):
        out = refs[:k]
        del refs[:k]
        return out

    attention = group > 0
    grads = take(count)
    if attention:
        (sc_ref, q_ref, do_ref, lse_ref, delta_ref) = take(5)
        kvs = take(n_t)
    lands, outs = take(count), take(count)
    if attention:
        dq_ref, dkv_ref = take(2)
    helds = take(count)
    (tile,) = take(1)
    landings = take(2 * (log2(n_dp) - 1) + log2(n_t))
    sems = take(4)
    me, z = lax.axis_index("dp"), lax.axis_index("tensor")
    greet_all(n_dp, n_t, me, z)
    works = [
        Scatter(
            n_dp, n_t, me, z, c, grads[c], lands[c], outs[c], helds[c], tile, landings, sems
        )
        for c in range(count)
    ]
    stages = works[0].stages

    def tick(k):
        for number in range(stages - 1, 0, -1):
            c = k - (number - 1)
            if 0 <= c < count:
                works[c].event(number)
        if k + 2 < count:
            works[k + 2].event(0)

    works[0].event(0)
    if count > 1:
        works[1].event(0)
    ticks = list(range(count + stages - 2))
    if attention:
        sums = take(n_t - 1)
        landed = take(n_t - 1)
        chain_sems = take(2)
        length = sc_ref[1]
        descend = Descend(n_t, me, z, [dkv_ref] + sums, landed, chain_sems)
        for r in range(n_t - 1, -1, -1):
            target = dkv_ref if r == 0 else sums[r - 1]
            attention_part(
                r, group, n_t, z, length, q_ref, do_ref, lse_ref, delta_ref, kvs[r], None, dq_ref, target
            )
            if r < n_t - 1:
                @pl.when((z + 1 < n_t) & (z >= r))
                def _():
                    descend.hop(r + 1).wait_recv()
                    add_blocks(target, landed[r])

            if r > 0:
                descend.start(r)
            tick(ticks.pop(0))
    for k in ticks:
        tick(k)
    for work in works:
        work.finish()
    if attention:
        for r in range(1, n_t):
            descend.finish(r)


def scatter(grads, n_dp, n_t, collective_id, attention=None):
    count = len(grads)
    bits = log2(n_dp) - 1
    block = grads[0].shape[2]
    widest = max(k.shape[3] for k in grads)
    shapes = [(n_t,) + (2,) * bits + (block, k.shape[3]) for k in grads]
    args = [k.reshape(s[:1] + (2,) + s[1:]) for k, s in zip(grads, shapes)]
    anywhere = pl.BlockSpec(memory_space=pl.ANY)
    vmem = pl.BlockSpec(memory_space=pltpu.VMEM)
    smem = pl.BlockSpec(memory_space=pltpu.SMEM)
    in_specs = [anywhere] * len(args)
    out_shape = [jax.ShapeDtypeStruct(s, bf16) for s in shapes] + [
        jax.ShapeDtypeStruct((block, s[-1]), f32) for s in shapes
    ]
    out_specs = [anywhere] * count + [vmem] * count
    scratch = [pltpu.VMEM(s, bf16) for s in shapes]
    scratch.append(pltpu.VMEM((2, block, widest), bf16))
    for stage in range(bits):
        for _ in (0, 1):
            scratch.append(
                pltpu.VMEM((2, n_t // 2) + (2,) * (bits - 1 - stage) + (block, widest), bf16)
            )
    for stage in range(log2(n_t)):
        scratch.append(pltpu.VMEM((2, n_t >> (stage + 1), block, widest), bf16))
    copies = 1 + 2 * bits + log2(n_t)
    scratch += [
        pltpu.SemaphoreType.DMA((count, copies)),
        pltpu.SemaphoreType.DMA((count, copies)),
        pltpu.SemaphoreType.DMA((count,)),
        pltpu.SemaphoreType.DMA((2,)),
    ]
    group = 0
    if attention is not None:
        sc, q, do, lse, delta, kvs = attention
        args += [sc, q, do, lse, delta] + list(kvs)
        in_specs += [smem] + [vmem] * (4 + n_t)
        group = q.shape[0] // kvs[0].shape[1]
        out_shape += [jax.ShapeDtypeStruct(q.shape, f32), jax.ShapeDtypeStruct(kvs[0].shape, bf16)]
        out_specs += [vmem, vmem]
        scratch += [pltpu.VMEM(kvs[0].shape, bf16)] * (2 * (n_t - 1))
        scratch += [pltpu.SemaphoreType.DMA((n_t,))] * 2
    outs = pl.pallas_call(
        functools.partial(scatter_kernel, n_dp, n_t, count, group),
        in_specs=in_specs,
        out_specs=out_specs,
        out_shape=out_shape,
        scratch_shapes=scratch,
        compiler_params=pltpu.CompilerParams(
            collective_id=collective_id, has_side_effects=True, vmem_limit_bytes=62 * 1024 * 1024
        ),
        name="scatter_grads",
    )(*args)
    return outs[count:]


def local(
    n_dp,
    n_t,
    tokens,
    lengths,
    cotangent,
    attn_gain,
    query_weight,
    key_matrix,
    value_matrix,
    out_weight,
    mlp_gain,
    gate_weight,
    up_weight,
    down_weight,
):
    rows, width = tokens.shape
    block = query_weight.shape[0]
    nq, nk = query_weight.shape[1], key_matrix.shape[1]
    no = out_weight.shape[0]
    units = gate_weight.shape[1]
    tile = units // CHUNKS
    me_dp = lax.axis_index("dp")
    me_t = lax.axis_index("tensor")
    length = lengths[0]
    me = jnp.stack([me_t, me_dp]).astype(jnp.int32)
    sc = jnp.stack([me_t.astype(jnp.int32), length])

    gains = jnp.stack([attn_gain, mlp_gain], axis=1)
    gains = jnp.pad(gains, ((0, 0), (0, GAIN_LANES - 2)))
    shard_qkv = jnp.concatenate([query_weight, key_matrix, value_matrix, gains], axis=1)
    down_t = down_weight.T
    shard_mlp = []
    for c in range(CHUNKS):
        cols = slice(c * tile, (c + 1) * tile)
        shard_mlp.append(
            jnp.concatenate([gate_weight[:, cols], up_weight[:, cols], down_t[:, cols]], axis=1)
        )
    (w_qkv,) = gather([shard_qkv], n_dp, n_t, 0)
    w_qkv = w_qkv.reshape(n_t, width, shard_qkv.shape[1])
    gain_cols = w_qkv[0, :, nq + 2 * nk : nq + 2 * nk + 2].astype(f32)
    gain_one, gain_two = gain_cols[:, 0], gain_cols[:, 1]

    position = (me_t * rows + jnp.arange(rows, dtype=jnp.int32)).astype(f32)
    freqs = rope_base ** (-(jnp.arange(HALF, dtype=f32) * 2.0) / HEAD_SIZE)
    angles = freqs[:, None] * position[None, :]
    cosine, sine = jnp.cos(angles), jnp.sin(angles)
    live = (me_t * rows + jnp.arange(rows, dtype=jnp.int32) < length).astype(f32)[:, None]
    x = tokens.astype(f32)
    inv_one = lax.rsqrt(jnp.mean(x * x, axis=1, keepdims=True) + eps_norm)
    g32 = cotangent.astype(f32) * live
    g = g32.astype(bf16)
    gt = g.T
    n1 = (x * inv_one * gain_one).astype(bf16)
    q, kv = qkv_project(n1, w_qkv, cosine, sine, nq, nk)
    q = q.reshape(n_t * nq, rows)

    *gathered, att, lse = gather([out_weight.T] + shard_mlp, n_dp, n_t, 1, (kv, q, length))
    w_out, *w_mlp = [w.reshape(n_t, width, w.shape[-1]) for w in gathered[: 1 + CHUNKS]]
    kvs = [kv] + gathered[1 + CHUNKS :]
    att_z = att.reshape(n_t, no, rows)
    h_one = out_project(att_z, w_out, tokens, no, 0)

    inv_two = lax.rsqrt(jnp.mean(h_one * h_one, axis=1, keepdims=True) + eps_norm)
    n2 = (h_one * inv_two * gain_two).astype(bf16)
    n2t = n2.T
    carry = None
    shares = []
    for c in range(CHUNKS):
        out_sum, dn_sum, share = mlp(
            me, n2, n2t, g, gt, w_mlp[c], 0, tile, carry, n_dp
        )
        carry = (out_sum, dn_sum)
        shares.append(share)
    mlp_out, d_n2 = carry
    block_out = (live * (h_one + mlp_out)).astype(bf16)

    scaled = d_n2 * gain_two
    inner = jnp.mean(scaled * h_one, axis=1, keepdims=True)
    gain_two_part = jnp.sum(d_n2 * h_one * inv_two, axis=0)
    d_h = g32 + inv_two * scaled - h_one * (inv_two * inv_two * inv_two * inner)
    d_h_low = d_h.astype(bf16)
    d_h_t = d_h_low.T
    d_att, share = out_back(me, d_h_low, d_h_t, att_z, w_out, no, 0, n_dp)
    shares.append(share)

    d_att = d_att.reshape(n_t * no, rows)
    groups, _, lanes = lse.shape
    delta = (d_att.astype(f32) * att.astype(f32)).reshape(groups, -1, HEAD_SIZE, rows).sum(axis=2)
    delta = delta.reshape(groups, 1, lanes)
    *grads, out_share, d_q, d_kv = scatter(
        shares,
        n_dp,
        n_t,
        2,
        (sc, q, d_att, lse, delta, kvs),
    )
    n1t = n1.T
    d_n1, q_part, kv_part = qkv_back(
        me, d_q.reshape(n_t, nq, rows), d_kv, cosine, sine, n1t, w_qkv, nq, nk, n_dp
    )
    q_share, kv_share = scatter([q_part, kv_part], n_dp, n_t, 3)

    scaled = d_n1 * gain_one
    inner = jnp.mean(scaled * x, axis=1, keepdims=True)
    gain_one_part = jnp.sum(d_n1 * x * inv_one, axis=0)
    d_x = inv_one * scaled - x * (inv_one * inv_one * inv_one * inner)
    tokens_grad = (d_h + d_x).astype(bf16)

    gain_parts = jnp.stack([gain_one_part.reshape(n_dp, block), gain_two_part.reshape(n_dp, block)], 1)
    gain_parts = to_relative(gain_parts, me_dp, n_dp)
    gain_share = reduce_small(gain_parts, me_dp, n_dp, n_t)

    gate_share = jnp.concatenate([s[:, :tile] for s in grads], axis=1)
    up_share = jnp.concatenate([s[:, tile : 2 * tile] for s in grads], axis=1)
    down_share = jnp.concatenate([s[:, 2 * tile :].T for s in grads], axis=0)
    return (
        block_out,
        tokens_grad,
        gain_share[0],
        q_share,
        kv_share[:, :nk],
        kv_share[:, nk:],
        out_share.T,
        gain_share[1],
        gate_share,
        up_share,
        down_share,
    )


def solution(mesh):
    in_specs = (
        P(("dp", "tensor"), None),
        P("dp"),
        P(("dp", "tensor"), None),
        P("dp"),
        P("dp", "tensor"),
        P("dp", "tensor"),
        P("dp", "tensor"),
        P("tensor", "dp"),
        P("dp"),
        P("dp", "tensor"),
        P("dp", "tensor"),
        P("tensor", "dp"),
    )
    out_specs = (
        P(("dp", "tensor"), None),
        P(("dp", "tensor"), None),
        P("dp"),
        P("dp", "tensor"),
        P("dp", "tensor"),
        P("dp", "tensor"),
        P("tensor", "dp"),
        P("dp"),
        P("dp", "tensor"),
        P("dp", "tensor"),
        P("tensor", "dp"),
    )
    fn = functools.partial(local, mesh.shape["dp"], mesh.shape["tensor"])
    return jax.shard_map(fn, mesh=mesh, in_specs=in_specs, out_specs=out_specs, check_vma=False)
```

```python
import functools
import math

import jax
import jax.numpy as jnp
from jax import lax
from jax.experimental import pallas as pl
from jax.experimental.pallas import tpu as pltpu
from jax.sharding import PartitionSpec as P

HEAD_SIZE = 96
HALF = HEAD_SIZE // 2
GAIN_LANES = 128
CHUNKS = 4
MERGED = CHUNKS - 1
CLIMB_AT = 7
CLIMB_STEP = 4
KEY_TILE = 256
NEG = -1e30

eps_norm = 1e-05
rope_base = 100000.0
SCALE = 1.0 / math.sqrt(HEAD_SIZE)
SCALE2 = SCALE * math.log2(math.e)

f32 = jnp.float32
bf16 = jnp.bfloat16
VMEM_LIMIT = 56 * 1024 * 1024


def dot(a, b, dims=((1,), (0,))):
    return lax.dot_general(a, b, (dims, ((), ())), preferred_element_type=f32)


def params(*semantics):
    return pltpu.CompilerParams(dimension_semantics=semantics, vmem_limit_bytes=VMEM_LIMIT)


def cost(flops, nbytes, trans=0):
    return pl.CostEstimate(flops=int(flops), bytes_accessed=int(nbytes), transcendentals=int(trans))


def place(ref, me, grad, col=0):
    count, block = ref.shape[1], ref.shape[2]
    for d in range(count):
        r = me ^ d
        at = (r & 1) * (count // 2) + (r >> 1)
        ref[0, at, :, col : col + grad.shape[1]] = grad[d * block : (d + 1) * block]


def turn(y, cosine, sine, sign):
    parts = []
    for h in range(y.shape[0] // HEAD_SIZE):
        a = y[h * HEAD_SIZE : h * HEAD_SIZE + HALF]
        b = y[h * HEAD_SIZE + HALF : (h + 1) * HEAD_SIZE]
        parts.append(a * cosine - sign * (b * sine))
        parts.append(b * cosine + sign * (a * sine))
    return jnp.concatenate(parts, axis=0)


def qkv_kernel(nq, nk, n1_ref, w_ref, cos_ref, sin_ref, q_ref, kv_ref):
    w = w_ref[0, :, : nq + 2 * nk]
    y = dot(n1_ref[...], w).T
    cosine, sine = cos_ref[...], sin_ref[...]
    q_ref[0] = turn(y[:nq], cosine, sine, 1.0).astype(bf16)
    kv_ref[0] = turn(y[nq : nq + nk], cosine, sine, 1.0).astype(bf16)
    kv_ref[1] = y[nq + nk :].astype(bf16)


def qkv_project(n1, w, cosine, sine, nq, nk):
    rows, width = n1.shape
    zs, _, cols = w.shape
    return pl.pallas_call(
        functools.partial(qkv_kernel, nq, nk),
        grid=(zs,),
        in_specs=[
            pl.BlockSpec((rows, width), lambda z: (0, 0)),
            pl.BlockSpec((1, width, cols), lambda z: (z, 0, 0)),
            pl.BlockSpec((HALF, rows), lambda z: (0, 0)),
            pl.BlockSpec((HALF, rows), lambda z: (0, 0)),
        ],
        out_specs=[
            pl.BlockSpec((1, nq, rows), lambda z: (z, 0, 0)),
            pl.BlockSpec((2, nk, rows), lambda z: (0, z, 0)),
        ],
        out_shape=[
            jax.ShapeDtypeStruct((zs, nq, rows), bf16),
            jax.ShapeDtypeStruct((2, zs * nk, rows), bf16),
        ],
        compiler_params=params("arbitrary"),
        cost_estimate=cost(2 * rows * width * cols * zs, 2 * zs * width * cols + 8 * rows * width),
        name="qkv_project",
    )(n1, w, cosine, sine)


def out_kernel(att_ref, w_ref, x_ref, h_ref):
    z = pl.program_id(0)

    @pl.when(z == 0)
    def _():
        h_ref[...] = x_ref[...].astype(f32)

    h_ref[...] += dot(att_ref[0].T, w_ref[0], ((1,), (1,)))


def out_project(att, w, x, no, col):
    zs, _, rows = att.shape
    width = x.shape[1]
    return pl.pallas_call(
        out_kernel,
        grid=(zs,),
        in_specs=[
            pl.BlockSpec((1, no, rows), lambda z: (z, 0, 0)),
            pl.BlockSpec((1, width, no), lambda z: (z, 0, col)),
            pl.BlockSpec((rows, width), lambda z: (0, 0)),
        ],
        out_specs=pl.BlockSpec((rows, width), lambda z: (0, 0)),
        out_shape=jax.ShapeDtypeStruct((rows, width), f32),
        compiler_params=params("arbitrary"),
        cost_estimate=cost(2 * rows * width * no * zs, 2 * zs * width * no + 8 * rows * width),
        name="out_project",
    )(att, w, x)


def out_back_kernel(me_ref, dh_ref, dht_ref, att_ref, w_ref, da_ref, grad_ref):
    w = w_ref[0]
    da_ref[0] = dot(dh_ref[...], w).T.astype(bf16)
    place(grad_ref, me_ref[1], dot(dht_ref[...], att_ref[0].T).astype(bf16))


def out_back(me, dh, dht, att, w, no, col, n_dp):
    zs, _, rows = att.shape
    width = dh.shape[1]
    block = width // n_dp
    return pl.pallas_call(
        out_back_kernel,
        grid_spec=pltpu.PrefetchScalarGridSpec(
            num_scalar_prefetch=1,
            grid=(zs,),
            in_specs=[
                pl.BlockSpec((rows, width), lambda z, m: (0, 0)),
                pl.BlockSpec((width, rows), lambda z, m: (0, 0)),
                pl.BlockSpec((1, no, rows), lambda z, m: (z, 0, 0)),
                pl.BlockSpec((1, width, no), lambda z, m: (z, 0, col)),
            ],
            out_specs=[
                pl.BlockSpec((1, no, rows), lambda z, m: (z, 0, 0)),
                pl.BlockSpec((1, n_dp, block, no), lambda z, m: (z ^ m[0], 0, 0, 0)),
            ],
        ),
        out_shape=[
            jax.ShapeDtypeStruct((zs, no, rows), bf16),
            jax.ShapeDtypeStruct((zs, n_dp, block, no), bf16),
        ],
        compiler_params=params("arbitrary"),
        cost_estimate=cost(4 * rows * width * no * zs, 4 * zs * width * no + 8 * rows * width),
        name="out_back",
    )(me, dh, dht, att, w)


def qkv_back_kernel(
    nq, nk, me_ref, dq_ref, dkv_ref, cos_ref, sin_ref, n1t_ref, w_ref, dn_ref, dwq_ref, dwkv_ref
):
    z = pl.program_id(0)

    @pl.when(z == 0)
    def _():
        dn_ref[...] = jnp.zeros_like(dn_ref)

    cosine, sine = cos_ref[...], sin_ref[...]
    dq = turn(dq_ref[0], cosine, sine, -1.0).astype(bf16)
    dk = turn(dkv_ref[0].astype(f32), cosine, sine, -1.0).astype(bf16)
    d = jnp.concatenate([dq, dk, dkv_ref[1]], axis=0).T
    w = w_ref[0, :, : nq + 2 * nk]
    dn_ref[...] += dot(d, w, ((1,), (1,)))
    grad = dot(n1t_ref[...], d).astype(bf16)
    place(dwq_ref, me_ref[1], grad[:, :nq])
    place(dwkv_ref, me_ref[1], grad[:, nq:])


def qkv_back(me, dq, dkv, cosine, sine, n1t, w, nq, nk, n_dp):
    zs, _, rows = dq.shape
    width = n1t.shape[0]
    block = width // n_dp
    cols = w.shape[2]
    out = nq + 2 * nk
    return pl.pallas_call(
        functools.partial(qkv_back_kernel, nq, nk),
        grid_spec=pltpu.PrefetchScalarGridSpec(
            num_scalar_prefetch=1,
            grid=(zs,),
            in_specs=[
                pl.BlockSpec((1, nq, rows), lambda z, m: (z, 0, 0)),
                pl.BlockSpec((2, nk, rows), lambda z, m: (0, z, 0)),
                pl.BlockSpec((HALF, rows), lambda z, m: (0, 0)),
                pl.BlockSpec((HALF, rows), lambda z, m: (0, 0)),
                pl.BlockSpec((width, rows), lambda z, m: (0, 0)),
                pl.BlockSpec((1, width, cols), lambda z, m: (z, 0, 0)),
            ],
            out_specs=[
                pl.BlockSpec((rows, width), lambda z, m: (0, 0)),
                pl.BlockSpec((1, n_dp, block, nq), lambda z, m: (z ^ m[0], 0, 0, 0)),
                pl.BlockSpec((1, n_dp, block, 2 * nk), lambda z, m: (z ^ m[0], 0, 0, 0)),
            ],
        ),
        out_shape=[
            jax.ShapeDtypeStruct((rows, width), f32),
            jax.ShapeDtypeStruct((zs, n_dp, block, nq), bf16),
            jax.ShapeDtypeStruct((zs, n_dp, block, 2 * nk), bf16),
        ],
        compiler_params=params("arbitrary"),
        cost_estimate=cost(4 * rows * width * out * zs, 4 * zs * width * cols + 8 * rows * width),
        name="qkv_back",
    )(me, dq, dkv, cosine, sine, n1t, w)


def key_mask(s, key_first, query_first, length, rows, diagonal):
    key = key_first + lax.broadcasted_iota(jnp.int32, (s.shape[0], 1), 0)
    ok = key < length
    if diagonal:
        lane = lax.broadcasted_iota(jnp.int32, s.shape, 1)
        query = query_first + lax.rem(lane, rows)
        ok = ok & (key <= query)
    return jnp.broadcast_to(ok, s.shape)


def mlp_step(tile, me, n2_ref, n2t_ref, g_ref, gt_ref, w_ref, out_ref, dn_ref, grad_ref):
    pair = w_ref[0, :, : 2 * tile]
    wd = w_ref[0, :, 2 * tile :]
    both = dot(n2_ref[...], pair)
    gate, up = both[:, :tile], both[:, tile:]
    d_hidden = dot(g_ref[...], wd)
    sigma = 1.0 / (1.0 + jnp.exp(-gate))
    active = gate * sigma
    hidden = (active * up).astype(bf16)
    d_gate = (d_hidden * up * (sigma * (1.0 + gate * (1.0 - sigma)))).astype(bf16)
    d_up = (d_hidden * active).astype(bf16)
    d_both = jnp.concatenate([d_gate, d_up], axis=1)
    out_ref[...] += dot(hidden, wd, ((1,), (1,)))
    dn_ref[...] += dot(d_both, pair, ((1,), (1,)))
    place(grad_ref, me, dot(n2t_ref[...], d_both).astype(bf16), 0)
    place(grad_ref, me, dot(gt_ref[...], hidden).astype(bf16), 2 * tile)


def mlp_kernel(
    tile, first, me_ref, n2_ref, n2t_ref, g_ref, gt_ref, w_ref, *refs
):
    if first:
        out_ref, dn_ref, grad_ref = refs
    else:
        out_in, dn_in, out_ref, dn_ref, grad_ref = refs
    z = pl.program_id(0)

    @pl.when(z == 0)
    def _():
        if first:
            out_ref[...] = jnp.zeros_like(out_ref)
            dn_ref[...] = jnp.zeros_like(dn_ref)
        else:
            out_ref[...] = out_in[...]
            dn_ref[...] = dn_in[...]

    mlp_step(tile, me_ref[1], n2_ref, n2t_ref, g_ref, gt_ref, w_ref, out_ref, dn_ref, grad_ref)


def mlp(me, n2, n2t, g, gt, w, chunk, tile, carry, n_dp):
    rows, width = n2.shape
    zs = w.shape[0]
    block = width // n_dp
    full = pl.BlockSpec((rows, width), lambda z, m: (0, 0))
    full_t = pl.BlockSpec((width, rows), lambda z, m: (0, 0))
    grad_spec = pl.BlockSpec((1, n_dp, block, 3 * tile), lambda z, m: (z ^ m[0], 0, 0, 0))
    first = carry is None
    in_specs = [
        full,
        full_t,
        full,
        full_t,
        pl.BlockSpec((1, width, 3 * tile), lambda z, m: (z, 0, chunk)),
    ]
    args = [me, n2, n2t, g, gt, w]
    aliases = {}
    if not first:
        in_specs += [full, full]
        aliases = {6: 0, 7: 1}
        args += list(carry)
    return pl.pallas_call(
        functools.partial(mlp_kernel, tile, first),
        grid_spec=pltpu.PrefetchScalarGridSpec(
            num_scalar_prefetch=1,
            grid=(zs,),
            in_specs=in_specs,
            out_specs=[full, full, grad_spec],
        ),
        out_shape=[
            jax.ShapeDtypeStruct((rows, width), f32),
            jax.ShapeDtypeStruct((rows, width), f32),
            jax.ShapeDtypeStruct((zs, n_dp, block, 3 * tile), bf16),
        ],
        input_output_aliases=aliases,
        compiler_params=params("arbitrary"),
        cost_estimate=cost(
            18 * rows * width * tile * zs, 4 * zs * width * 3 * tile + 24 * rows * width
        ),
        name="mlp",
    )(*args)


def pairs(count, mask):
    return [(i, i ^ mask) for i in range(count)]


def bits_of(count):
    return [1 << b for b in range(count.bit_length() - 1)]


def relative_order(count):
    return [r for low in (0, 1) for r in range(count) if (r & 1) == low]


def to_relative(rows_first, me, count):
    block = rows_first.shape[0] // count
    parts = [
        lax.dynamic_slice_in_dim(rows_first, (me ^ r) * block, block, axis=0)
        for r in relative_order(count)
    ]
    return jnp.concatenate(parts, axis=0)


def reduce_small(values, me, n_dp, n_t):
    order = relative_order(n_dp)
    buf = values
    left = n_dp
    buf = buf[: left // 2] + lax.ppermute(buf[left // 2 :], "dp", pairs(n_dp, 1))
    left //= 2
    for bit in [b for b in bits_of(n_dp) if b > 1][::-1]:
        buf = buf[: left // 2] + lax.ppermute(buf[left // 2 :], "dp", pairs(n_dp, bit))
        left //= 2
    buf = buf[0]
    for bit in bits_of(n_t):
        buf = buf + lax.ppermute(buf, "tensor", pairs(n_t, bit))
    return buf


MESH = pl.DeviceIdType.MESH


def log2(n):
    return n.bit_length() - 1


def nearest_first(n_t):
    return [sorted(range(n_t), key=lambda p: (abs(p - z), p)) for z in range(n_t)]


def pick(values, z):
    out = jnp.int32(values[0])
    for i in range(1, len(values)):
        out = jnp.where(z == i, jnp.int32(values[i]), out)
    return out


def neighbours(n_dp, n_t, me, z):
    barrier = pltpu.get_barrier_semaphore()
    masks = [1 << b for b in range(log2(n_dp))]
    for mask in masks:
        pl.semaphore_signal(barrier, 1, device_id=(me ^ mask, z), device_id_type=MESH)

    @pl.when(z > 0)
    def _():
        pl.semaphore_signal(barrier, 1, device_id=(me, z - 1), device_id_type=MESH)

    @pl.when(z < n_t - 1)
    def _():
        pl.semaphore_signal(barrier, 1, device_id=(me, z + 1), device_id_type=MESH)

    count = len(masks) + (z > 0).astype(jnp.int32) + (z < n_t - 1).astype(jnp.int32)
    pl.semaphore_wait(barrier, count)


class Gather:
    def __init__(self, n_dp, n_t, me, z, index, shard, whole, sems, lanes=None):
        self.n_dp, self.n_t, self.me, self.z = n_dp, n_t, me, z
        self.index, self.shard, self.whole, self.lanes = index, shard, whole, lanes
        self.own, self.z_send, self.z_recv, self.x_send, self.x_recv = sems
        self.bits = log2(n_dp) - 1

    def place_of(self, piece, d):
        if self.lanes is None:
            return self.whole.at[piece, d]
        return self.whole.at[piece, d, :, self.lanes]

    def local(self):
        return pltpu.make_async_copy(
            self.shard, self.place_of(self.z, self.me), self.own.at[self.index]
        )

    def hop(self, piece, direction, hops):
        source = self.place_of(piece, self.me)
        step = 1 - 2 * direction
        return pltpu.make_async_remote_copy(
            source,
            source,
            self.z_send.at[self.index, direction, hops],
            self.z_recv.at[self.index, direction, hops],
            device_id=(self.me, jnp.clip(self.z + step, 0, self.n_t - 1)),
            device_id_type=MESH,
        )

    def send_own(self):
        local = self.local()
        local.start()
        local.wait()

        @pl.when(self.z < self.n_t - 1)
        def _():
            self.hop(self.z, 0, 0).start()

        @pl.when(self.z > 0)
        def _():
            self.hop(self.z, 1, 0).start()

    def order(self, k):
        return pick([row[k] for row in nearest_first(self.n_t)], self.z)

    def arrive(self, k):
        if k == 0:
            return
        piece = self.order(k)
        direction = (piece > self.z).astype(jnp.int32)
        hops = jnp.abs(piece - self.z)
        self.hop(piece, direction, hops - 1).wait_recv()
        on = jnp.where(direction == 0, self.z < self.n_t - 1, self.z > 0)

        @pl.when(on)
        def _():
            self.hop(piece, direction, hops).start()

    def doubling(self, k, stage, i, incoming=False):
        piece = self.order(k)
        odd = (piece & 1) == 1
        bit = jnp.where(odd, 1 << (self.bits - stage), 2 << stage)
        shift = jnp.where(odd, self.bits - stage + 1, 1)
        partner = self.me ^ bit
        origin = partner if incoming else self.me
        held = self.place_of(piece, origin ^ (i << shift))
        at = (1 << stage) - 1 + i
        return pltpu.make_async_remote_copy(
            held,
            held,
            self.x_send.at[self.index, k, at],
            self.x_recv.at[self.index, k, at],
            device_id=(partner, self.z),
            device_id_type=MESH,
        )

    def core(self, k, i, incoming=False):
        piece = self.order(k)
        partner = self.me ^ 1
        origin = partner if incoming else self.me
        held = self.place_of(piece, origin ^ (i << 1))
        at = (1 << self.bits) - 1 + i
        return pltpu.make_async_remote_copy(
            held,
            held,
            self.x_send.at[self.index, k, at],
            self.x_recv.at[self.index, k, at],
            device_id=(partner, self.z),
            device_id_type=MESH,
        )

    def each(self, count, body):
        if count <= 4:
            for i in range(count):
                body(i)
        else:
            lax.fori_loop(0, count, lambda i, _: (body(i), 0)[1], 0)

    def spread(self, k, stage):
        if stage > 0:
            self.each(1 << (stage - 1), lambda i: self.doubling(k, stage - 1, i, True).wait_recv())
        if stage < self.bits:
            self.each(1 << stage, lambda i: self.doubling(k, stage, i).start())
        else:
            self.each(1 << self.bits, lambda i: self.core(k, i).start())

    def finish(self, k):
        self.each(1 << self.bits, lambda i: self.core(k, i, True).wait_recv())
        for stage in range(self.bits):
            self.each(1 << stage, lambda i: self.doubling(k, stage, i).wait_send())
        self.each(1 << self.bits, lambda i: self.core(k, i).wait_send())
        piece = self.order(k)
        hops = jnp.abs(piece - self.z)
        if k == 0:

            @pl.when(self.z < self.n_t - 1)
            def _():
                self.hop(piece, 0, 0).wait_send()

            @pl.when(self.z > 0)
            def _():
                self.hop(piece, 1, 0).wait_send()
        else:
            direction = (piece > self.z).astype(jnp.int32)
            on = jnp.where(direction == 0, self.z < self.n_t - 1, self.z > 0)

            @pl.when(on)
            def _():
                self.hop(piece, direction, hops).wait_send()


class Climb:
    def __init__(self, n_t, me, z, own, kept, sems):
        self.n_t, self.me, self.z, self.own, self.kept = n_t, me, z, own, kept
        self.send, self.recv = sems

    def hop(self, r):
        source = self.own if r == 0 else self.kept[r - 1]
        return pltpu.make_async_remote_copy(
            source,
            self.kept[r],
            self.send.at[r],
            self.recv.at[r],
            device_id=(self.me, jnp.minimum(self.z + 1, self.n_t - 1)),
            device_id_type=MESH,
        )

    def start(self, r):
        @pl.when((self.z >= r) & (self.z < self.n_t - 1))
        def _():
            self.hop(r).start()

    def arrive(self, r):
        @pl.when(self.z >= r)
        def _():
            self.hop(r - 1).wait_recv()

    def finish(self, r):
        @pl.when((self.z >= r) & (self.z < self.n_t - 1))
        def _():
            self.hop(r).wait_send()


def attend_part(r, z, length, q_ref, kv_ref, m_ref, l_ref, acc_ref):
    rows = q_ref.shape[1]
    groups = m_ref.shape[0]
    group = q_ref.shape[0] // (groups * HEAD_SIZE)
    first = z * rows

    @pl.when(z >= r)
    def _():
        def body(g, _):
            base = pl.multiple_of(g * (group * HEAD_SIZE), 32)
            at = pl.multiple_of(g * HEAD_SIZE, 32)
            q = jnp.concatenate(
                [q_ref[pl.ds(base + a * HEAD_SIZE, HEAD_SIZE), :] for a in range(group)], axis=1
            )
            if r == 0:
                m = jnp.full((1, group * rows), NEG, f32)
                total = jnp.zeros((1, group * rows), f32)
                acc = jnp.zeros((HEAD_SIZE, group * rows), f32)
            else:
                m, total, acc = m_ref[g], l_ref[g], acc_ref[g]
            for j in range(rows // KEY_TILE):
                part = slice(j * KEY_TILE, (j + 1) * KEY_TILE)
                k = kv_ref[0, pl.ds(at, HEAD_SIZE), part]
                v = kv_ref[1, pl.ds(at, HEAD_SIZE), part]
                s = dot(k, q, ((0,), (0,)))
                ok = key_mask(s, first - r * rows + j * KEY_TILE, first, length, rows, r == 0)
                s = jnp.where(ok, s, NEG)
                new = jnp.maximum(m, jnp.max(s, axis=0, keepdims=True))
                shrink = jnp.exp2((m - new) * SCALE2)
                p = jnp.exp2(s * SCALE2 - new * SCALE2)
                total = total * shrink + jnp.sum(p, axis=0, keepdims=True)
                acc = acc * shrink + dot(v, p.astype(bf16))
                m = new
            m_ref[g], l_ref[g], acc_ref[g] = m, total, acc
            return 0

        lax.fori_loop(0, groups, body, 0)


def attend_end(q_shape, m_ref, l_ref, acc_ref, att_ref):
    groups = m_ref.shape[0]
    rows = q_shape[1]
    group = q_shape[0] // (groups * HEAD_SIZE)

    def body(g, _):
        out = acc_ref[g] / l_ref[g]
        for a in range(group):
            own = pl.ds(pl.multiple_of((g * group + a) * HEAD_SIZE, 32), HEAD_SIZE)
            att_ref[own, :] = out[:, a * rows : (a + 1) * rows].astype(bf16)
        m_ref[g] = m_ref[g] * SCALE2 + jnp.log2(l_ref[g])
        return 0

    lax.fori_loop(0, groups, body, 0)


def gather_kernel(n_dp, n_t, count, merged, climbs, *refs):
    refs = list(refs)

    def take(k):
        out = refs[:k]
        del refs[:k]
        return out

    shards = take(count)
    if climbs:
        own, q_ref, length_ref = take(3)
    wholes = [(ref, None) for ref in take(count - merged)]
    if merged:
        (ref,) = take(1)
        wide = shards[-1].shape[1]
        wholes += [(ref, slice(i * wide, (i + 1) * wide)) for i in range(merged)]
    if climbs:
        kept = take(n_t - 1)
        att_ref, lse_ref = take(2)
    sems = take(5)
    me, z = lax.axis_index("dp"), lax.axis_index("tensor")
    neighbours(n_dp, n_t, me, z)
    works = [
        Gather(n_dp, n_t, me, z, c, shards[c], wholes[c][0], sems, wholes[c][1])
        for c in range(count)
    ]
    if climbs:
        climb_sems = take(2)
        l_ref, acc_ref, kv_ref, kv_sem = take(4)
        climb = Climb(n_t, me, z, own, kept, climb_sems)
        climb.start(0)
        length = length_ref[0]

    def attend_step(r):
        if r > 0:
            climb.arrive(r)
            if r < n_t - 1:
                climb.start(r)

        @pl.when(z >= r)
        def _():
            fetch = pltpu.make_async_copy(own if r == 0 else kept[r - 1], kv_ref, kv_sem)
            fetch.start()
            fetch.wait()

        attend_part(r, z, length, q_ref, kv_ref, lse_ref, l_ref, acc_ref)

    stages = log2(n_dp)
    works[0].send_own()
    total = count * n_t
    todo = list(range(n_t)) if climbs else []
    for n in range(total + 2 * (stages - 1)):
        if n < total:
            c, k = divmod(n, n_t)
            works[c].arrive(k)
            works[c].spread(k, 0)
            if k == 0 and c + 1 < count:
                works[c + 1].send_own()
        for stage in range(1, stages):
            at = n - 2 * stage
            if 0 <= at < total:
                works[at // n_t].spread(at % n_t, stage)
        if todo and (n == 2 if todo[0] == 0 else n == CLIMB_AT + CLIMB_STEP * (todo[0] - 1)):
            attend_step(todo.pop(0))
    for r in todo:
        attend_step(r)
    if climbs:
        attend_end(q_ref.shape, lse_ref, l_ref, acc_ref, att_ref)
    for c in range(count):
        for k in range(n_t):
            works[c].finish(k)
    if climbs:
        for r in range(n_t - 1):
            climb.finish(r)


def gather(shards, n_dp, n_t, collective_id, attention=None, merged=0):
    count = len(shards)
    shapes = [
        jax.ShapeDtypeStruct((n_t, n_dp) + s.shape, s.dtype) for s in shards[: count - merged]
    ]
    if merged:
        block, wide = shards[-1].shape
        shapes.append(jax.ShapeDtypeStruct((n_t, n_dp, block, merged * wide), bf16))
    args = list(shards)
    anywhere = pl.BlockSpec(memory_space=pl.ANY)
    vmem = pl.BlockSpec(memory_space=pltpu.VMEM)
    in_specs = [anywhere] * count
    out_specs = [anywhere] * len(shapes)
    scratch = [
        pltpu.SemaphoreType.DMA((count,)),
        pltpu.SemaphoreType.DMA((count, 2, n_t)),
        pltpu.SemaphoreType.DMA((count, 2, n_t)),
        pltpu.SemaphoreType.DMA((count, n_t, n_dp - 1)),
        pltpu.SemaphoreType.DMA((count, n_t, n_dp - 1)),
    ]
    if attention is not None:
        kv, q, length = attention
        rows = q.shape[1]
        groups = kv.shape[1] // HEAD_SIZE
        lanes = q.shape[0] // (groups * HEAD_SIZE) * rows
        args += [kv, q, length.reshape(1)]
        in_specs += [anywhere, vmem, pl.BlockSpec(memory_space=pltpu.SMEM)]
        shapes += [jax.ShapeDtypeStruct(kv.shape, kv.dtype)] * (n_t - 1)
        shapes += [
            jax.ShapeDtypeStruct(q.shape, bf16),
            jax.ShapeDtypeStruct((groups, 1, lanes), f32),
        ]
        out_specs += [anywhere] * (n_t - 1) + [vmem, vmem]
        scratch += [pltpu.SemaphoreType.DMA((n_t,))] * 2
        scratch += [
            pltpu.VMEM((groups, 1, lanes), f32),
            pltpu.VMEM((groups, HEAD_SIZE, lanes), f32),
            pltpu.VMEM(kv.shape, bf16),
            pltpu.SemaphoreType.DMA,
        ]
    return pl.pallas_call(
        functools.partial(gather_kernel, n_dp, n_t, count, merged, attention is not None),
        in_specs=in_specs,
        out_specs=out_specs,
        out_shape=shapes,
        scratch_shapes=scratch,
        compiler_params=pltpu.CompilerParams(
            collective_id=collective_id, has_side_effects=True, vmem_limit_bytes=VMEM_LIMIT
        ),
        name="gather_weights",
    )(*args)


def mlp_gather_kernel(
    n_dp, n_t, tile, n2_ref, n2t_ref, g_ref, gt_ref, w_ref, shard_ref,
    out_ref, dn_ref, grad_ref, whole_ref, *sems
):
    me, z = lax.axis_index("dp"), lax.axis_index("tensor")
    step = pl.program_id(0) * pl.num_programs(1) + pl.program_id(1)
    steps = w_ref.shape[0] * MERGED * n_t
    work = Gather(n_dp, n_t, me, z, 0, shard_ref, whole_ref, sems)
    stages = log2(n_dp)

    @pl.when(step == 0)
    def _():
        neighbours(n_dp, n_t, me, z)
        work.send_own()
        out_ref[...] = jnp.zeros_like(out_ref)
        dn_ref[...] = jnp.zeros_like(dn_ref)

    for n in range(n_t + 2 * (stages - 1)):

        @pl.when(step == min(n, steps - 1))
        def _():
            if n < n_t:
                work.arrive(n)
                work.spread(n, 0)
            for stage in range(1, stages):
                at = n - 2 * stage
                if 0 <= at < n_t:
                    work.spread(at, stage)

    mlp_step(
        tile, me, n2_ref, n2t_ref, g_ref, gt_ref, w_ref, out_ref, dn_ref, grad_ref.at[0]
    )

    @pl.when(step == steps - 1)
    def _():
        for k in range(n_t):
            work.finish(k)


def mlp_gather(n2, n2t, g, gt, w, shard, tile, n_dp, n_t, collective_id):
    rows, width = n2.shape
    block = width // n_dp
    full = pl.BlockSpec((rows, width), lambda c, i: (0, 0))
    full_t = pl.BlockSpec((width, rows), lambda c, i: (0, 0))
    anywhere = pl.BlockSpec(memory_space=pl.ANY)
    cols = 3 * tile
    return pl.pallas_call(
        functools.partial(mlp_gather_kernel, n_dp, n_t, tile),
        grid=(MERGED, n_t),
        in_specs=[
            full,
            full_t,
            full,
            full_t,
            pl.BlockSpec((1, width, cols), lambda c, i: (i, 0, c)),
            anywhere,
        ],
        out_specs=[
            full,
            full,
            pl.BlockSpec(
                (1, 1, n_dp, block, cols),
                lambda c, i: (c, i ^ lax.axis_index("tensor"), 0, 0, 0),
            ),
            anywhere,
        ],
        out_shape=[
            jax.ShapeDtypeStruct((rows, width), f32),
            jax.ShapeDtypeStruct((rows, width), f32),
            jax.ShapeDtypeStruct((MERGED, n_t, n_dp, block, cols), bf16),
            jax.ShapeDtypeStruct((n_t, n_dp, block, cols), bf16),
        ],
        scratch_shapes=[
            pltpu.SemaphoreType.DMA((1,)),
            pltpu.SemaphoreType.DMA((1, 2, n_t)),
            pltpu.SemaphoreType.DMA((1, 2, n_t)),
            pltpu.SemaphoreType.DMA((1, n_t, n_dp - 1)),
            pltpu.SemaphoreType.DMA((1, n_t, n_dp - 1)),
        ],
        compiler_params=pltpu.CompilerParams(
            dimension_semantics=("arbitrary", "arbitrary"),
            collective_id=collective_id,
            has_side_effects=True,
            vmem_limit_bytes=VMEM_LIMIT,
        ),
        name="mlp_gather",
    )(n2, n2t, g, gt, w, shard)


def greet_all(n_dp, n_t, me, z):
    barrier = pltpu.get_barrier_semaphore()
    masks = [1 << b for b in range(log2(n_dp))]
    for mask in masks:
        pl.semaphore_signal(barrier, 1, device_id=(me ^ mask, z), device_id_type=MESH)
    for other in range(1, n_t):
        pl.semaphore_signal(barrier, 1, device_id=(me, z ^ other), device_id_type=MESH)
    pl.semaphore_wait(barrier, len(masks) + n_t - 1)


def count_of(shape):
    return math.prod(shape)


def add_blocks(target, source, dtype=bf16):
    lead = target.shape[:-2]

    def body(i, _):
        at = []
        for extent in lead[::-1]:
            at.append(lax.rem(i, extent))
            i = i // extent
        at = tuple(at[::-1])
        target[at] = (target[at].astype(f32) + source[at].astype(f32)).astype(dtype)
        return 0

    lax.fori_loop(0, count_of(lead), body, 0)


class Scatter:
    def __init__(self, n_dp, n_t, me, z, index, grad, land, out, held, tile, landings, sems):
        self.n_t, self.me, self.z, self.index = n_t, me, z, index
        ref, lead = grad
        self.keep, self.send = ref.at[lead + (slice(None), 0)], ref.at[lead + (slice(None), 1)]
        self.land, self.out, self.held = land, out, held
        self.tile, self.landings, self.sems = tile, landings, sems
        self.bits, self.t_bits = log2(n_dp) - 1, log2(n_t)
        self.stages = 2 + self.bits + self.t_bits
        self.cols = held.shape[-1]

    def remote(self, source, target, slot, dp, z):
        send, recv = self.sems[0], self.sems[1]
        return pltpu.make_async_remote_copy(
            source,
            target,
            send.at[self.index, slot],
            recv.at[self.index, slot],
            device_id=(dp, z),
            device_id_type=MESH,
        )

    def load(self):
        return pltpu.make_async_copy(self.keep, self.held, self.sems[2].at[self.index])

    def core(self):
        return self.remote(self.send, self.land, 0, self.me ^ 1, self.z)

    def part(self, half, stage, bit):
        rest = (slice(None),) * (self.bits - 1 - stage)
        done = (0,) * stage
        if half == 0:
            return self.held.at[(slice(0, self.n_t // 2),) + rest + (bit,) + done]
        return self.held.at[(slice(self.n_t // 2, self.n_t),) + done + (bit,) + rest]

    def landing(self, which):
        ref = self.landings[which]
        at = (self.index % 2,) + (slice(None),) * (len(ref.shape) - 2) + (slice(0, self.cols),)
        return ref.at[at]

    def plane(self, half, stage):
        mask = 2 << stage if half == 0 else 1 << (self.bits - stage)
        return self.remote(
            self.part(half, stage, 1),
            self.landing(2 * stage + half),
            1 + 2 * stage + half,
            self.me ^ mask,
            self.z,
        )

    def column(self, stage, first, count):
        return self.held.at[(slice(first, first + count),) + (0,) * self.bits]

    def along(self, stage):
        count = self.n_t >> (stage + 1)
        return self.remote(
            self.column(stage, count, count),
            self.landing(2 * self.bits + stage),
            1 + 2 * self.bits + stage,
            self.me,
            self.z ^ count,
        )

    def start(self, stage):
        if stage < self.bits:
            self.plane(0, stage).start()
            self.plane(1, stage).start()
        elif stage < self.bits + self.t_bits:
            self.along(stage - self.bits).start()

    def event(self, number):
        if number == 0:
            self.core().start()
            self.load().start()
        elif number == 1:
            self.load().wait()
            self.core().wait_recv()
            self.add_land()
            self.start(0)
        elif number <= 1 + self.bits:
            stage = number - 2
            for half in (0, 1):
                self.plane(half, stage).wait_recv()
                add_blocks(self.part(half, stage, 0), self.landing(2 * stage + half))
            self.start(stage + 1)
        else:
            stage = number - 2 - self.bits
            self.along(stage).wait_recv()
            count = self.n_t >> (stage + 1)
            if stage < self.t_bits - 1:
                add_blocks(
                    self.column(stage, 0, count), self.landing(2 * self.bits + stage)
                )
                self.start(number - 1)
            else:
                mine = self.held[(0,) * (1 + self.bits)].astype(f32)
                got = self.landing(2 * self.bits + stage)[0].astype(f32)
                self.out[...] = mine + got

    def add_land(self):
        lead = self.held.shape[:-2]

        def at_of(i):
            at = []
            for extent in lead[::-1]:
                at.append(lax.rem(i, extent))
                i = i // extent
            return tuple(at[::-1])

        def fetch(i):
            return pltpu.make_async_copy(
                self.land.at[at_of(i)],
                self.tile.at[lax.rem(i, 2), :, pl.ds(0, self.cols)],
                self.sems[3].at[lax.rem(i, 2)],
            )

        total = count_of(lead)
        fetch(0).start()

        def body(i, _):
            @pl.when(i + 1 < total)
            def _():
                fetch(i + 1).start()

            fetch(i).wait()
            at = at_of(i)
            got = self.tile[lax.rem(i, 2), :, pl.ds(0, self.cols)].astype(f32)
            self.held[at] = (self.held[at].astype(f32) + got).astype(bf16)
            return 0

        lax.fori_loop(0, total, body, 0)

    def finish(self):
        self.core().wait_send()
        for stage in range(self.bits):
            for half in (0, 1):
                self.plane(half, stage).wait_send()
        for stage in range(self.t_bits):
            self.along(stage).wait_send()


class Descend:
    def __init__(self, n_t, me, z, sums, landed, sems):
        self.n_t, self.me, self.z = n_t, me, z
        self.sums, self.landed, self.send, self.recv = sums, landed, sems[0], sems[1]

    def hop(self, r):
        return pltpu.make_async_remote_copy(
            self.sums[r],
            self.landed[r - 1],
            self.send.at[r],
            self.recv.at[r],
            device_id=(self.me, jnp.maximum(self.z - 1, 0)),
            device_id_type=MESH,
        )

    def start(self, r):
        @pl.when(self.z >= r)
        def _():
            self.hop(r).start()

    def finish(self, r):
        @pl.when(self.z >= r)
        def _():
            self.hop(r).wait_send()


def attention_part(r, group, n_t, z, length, q_ref, do_ref, lse_ref, delta_ref, kv_ref, got_ref, dq_ref, sum_ref):
    rows = q_ref.shape[1]
    groups = lse_ref.shape[0]
    per = group * HEAD_SIZE
    first = z * rows
    active = z >= r
    fresh = r == n_t - 1

    def beside(ref, base):
        return jnp.concatenate(
            [ref[pl.ds(base + a * HEAD_SIZE, HEAD_SIZE), :] for a in range(group)], axis=1
        )

    @pl.when(active)
    def _():
        def body(g, _):
            base = pl.multiple_of(g * per, 32)
            at = pl.multiple_of(g * HEAD_SIZE, 32)
            q = beside(q_ref, base)
            do = beside(do_ref, base)
            delta, lse = delta_ref[g], lse_ref[g]
            dq = jnp.zeros(q.shape, f32)
            for j in range(rows // KEY_TILE):
                part = slice(j * KEY_TILE, (j + 1) * KEY_TILE)
                k, v = kv_ref[0, pl.ds(at, HEAD_SIZE), part], kv_ref[1, pl.ds(at, HEAD_SIZE), part]
                s = dot(k, q, ((0,), (0,)))
                ok = key_mask(s, first - r * rows + j * KEY_TILE, first, length, rows, r == 0)
                p = jnp.where(ok, jnp.exp2(s * SCALE2 - lse), 0.0)
                dp = dot(v, do, ((0,), (0,)))
                ds = (p * (dp - delta)).astype(bf16)
                dv = dot(do, p.astype(bf16), ((1,), (1,)))
                dk = dot(q, ds, ((1,), (1,))) * SCALE
                sum_ref[0, pl.ds(at, HEAD_SIZE), part] = dk.astype(bf16)
                sum_ref[1, pl.ds(at, HEAD_SIZE), part] = dv.astype(bf16)
                dq += dot(k, ds)
            for a in range(group):
                own = pl.ds(base + a * HEAD_SIZE, HEAD_SIZE)
                term = dq[:, a * rows : (a + 1) * rows] * SCALE
                if fresh:
                    dq_ref[own, :] = term
                else:
                    dq_ref[own, :] += term
            return 0

        lax.fori_loop(0, groups, body, 0)

    @pl.when(jnp.logical_not(active))
    def _():
        sum_ref[...] = jnp.zeros_like(sum_ref)
        if fresh:
            dq_ref[...] = jnp.zeros_like(dq_ref)


def scatter_kernel(n_dp, n_t, stacked, group, *refs):
    refs = list(refs)

    def take(k):
        out = refs[:k]
        del refs[:k]
        return out

    attention = group > 0
    grads = []
    for ref, depth in zip(take(len(stacked)), stacked):
        grads += [(ref, (c,)) for c in range(depth)] if depth else [(ref, ())]
    count = len(grads)
    if attention:
        (sc_ref, q_ref, do_ref, lse_ref, delta_ref) = take(5)
        kvs = take(n_t)
    lands, outs = take(count), take(count)
    if attention:
        dq_ref, dkv_ref = take(2)
    helds = take(count)
    (tile,) = take(1)
    landings = take(2 * (log2(n_dp) - 1) + log2(n_t))
    sems = take(4)
    me, z = lax.axis_index("dp"), lax.axis_index("tensor")
    greet_all(n_dp, n_t, me, z)
    works = [
        Scatter(
            n_dp, n_t, me, z, c, grads[c], lands[c], outs[c], helds[c], tile, landings, sems
        )
        for c in range(count)
    ]
    stages = works[0].stages

    def tick(k):
        for number in range(stages - 1, 0, -1):
            c = k - (number - 1)
            if 0 <= c < count:
                works[c].event(number)
        if k + 2 < count:
            works[k + 2].event(0)

    works[0].event(0)
    if count > 1:
        works[1].event(0)
    ticks = list(range(count + stages - 2))
    if attention:
        sums = take(n_t - 1)
        landed = take(n_t - 1)
        chain_sems = take(2)
        length = sc_ref[1]
        descend = Descend(n_t, me, z, [dkv_ref] + sums, landed, chain_sems)
        for r in range(n_t - 1, -1, -1):
            target = dkv_ref if r == 0 else sums[r - 1]
            attention_part(
                r, group, n_t, z, length, q_ref, do_ref, lse_ref, delta_ref, kvs[r], None, dq_ref, target
            )
            if r < n_t - 1:
                @pl.when((z + 1 < n_t) & (z >= r))
                def _():
                    descend.hop(r + 1).wait_recv()
                    add_blocks(target, landed[r])

            if r > 0:
                descend.start(r)
            tick(ticks.pop(0))
    for k in ticks:
        tick(k)
    for work in works:
        work.finish()
    if attention:
        for r in range(1, n_t):
            descend.finish(r)


def scatter(grads, n_dp, n_t, collective_id, attention=None):
    bits = log2(n_dp) - 1
    block = grads[0].shape[-2]
    widest = max(k.shape[-1] for k in grads)
    stacked = [k.shape[0] if k.ndim == 5 else 0 for k in grads]
    shapes = []
    for k, depth in zip(grads, stacked):
        shapes += [(n_t,) + (2,) * bits + (block, k.shape[-1])] * max(depth, 1)
    count = len(shapes)
    args = [
        k.reshape(k.shape[: k.ndim - 3] + (2,) * (bits + 1) + k.shape[-2:]) for k in grads
    ]
    anywhere = pl.BlockSpec(memory_space=pl.ANY)
    vmem = pl.BlockSpec(memory_space=pltpu.VMEM)
    smem = pl.BlockSpec(memory_space=pltpu.SMEM)
    in_specs = [anywhere] * len(args)
    out_shape = [jax.ShapeDtypeStruct(s, bf16) for s in shapes] + [
        jax.ShapeDtypeStruct((block, s[-1]), f32) for s in shapes
    ]
    out_specs = [anywhere] * count + [vmem] * count
    scratch = [pltpu.VMEM(s, bf16) for s in shapes]
    scratch.append(pltpu.VMEM((2, block, widest), bf16))
    for stage in range(bits):
        for _ in (0, 1):
            scratch.append(
                pltpu.VMEM((2, n_t // 2) + (2,) * (bits - 1 - stage) + (block, widest), bf16)
            )
    for stage in range(log2(n_t)):
        scratch.append(pltpu.VMEM((2, n_t >> (stage + 1), block, widest), bf16))
    copies = 1 + 2 * bits + log2(n_t)
    scratch += [
        pltpu.SemaphoreType.DMA((count, copies)),
        pltpu.SemaphoreType.DMA((count, copies)),
        pltpu.SemaphoreType.DMA((count,)),
        pltpu.SemaphoreType.DMA((2,)),
    ]
    group = 0
    if attention is not None:
        sc, q, do, lse, delta, kvs = attention
        args += [sc, q, do, lse, delta] + list(kvs)
        in_specs += [smem] + [vmem] * (4 + n_t)
        group = q.shape[0] // kvs[0].shape[1]
        out_shape += [jax.ShapeDtypeStruct(q.shape, f32), jax.ShapeDtypeStruct(kvs[0].shape, bf16)]
        out_specs += [vmem, vmem]
        scratch += [pltpu.VMEM(kvs[0].shape, bf16)] * (2 * (n_t - 1))
        scratch += [pltpu.SemaphoreType.DMA((n_t,))] * 2
    outs = pl.pallas_call(
        functools.partial(scatter_kernel, n_dp, n_t, stacked, group),
        in_specs=in_specs,
        out_specs=out_specs,
        out_shape=out_shape,
        scratch_shapes=scratch,
        compiler_params=pltpu.CompilerParams(
            collective_id=collective_id, has_side_effects=True, vmem_limit_bytes=62 * 1024 * 1024
        ),
        name="scatter_grads",
    )(*args)
    return outs[count:]


def local(
    n_dp,
    n_t,
    tokens,
    lengths,
    cotangent,
    attn_gain,
    query_weight,
    key_matrix,
    value_matrix,
    out_weight,
    mlp_gain,
    gate_weight,
    up_weight,
    down_weight,
):
    rows, width = tokens.shape
    block = query_weight.shape[0]
    nq, nk = query_weight.shape[1], key_matrix.shape[1]
    no = out_weight.shape[0]
    units = gate_weight.shape[1]
    tile = units // CHUNKS
    me_dp = lax.axis_index("dp")
    me_t = lax.axis_index("tensor")
    length = lengths[0]
    me = jnp.stack([me_t, me_dp]).astype(jnp.int32)
    sc = jnp.stack([me_t.astype(jnp.int32), length])

    gains = jnp.stack([attn_gain, mlp_gain], axis=1)
    gains = jnp.pad(gains, ((0, 0), (0, GAIN_LANES - 2)))
    shard_qkv = jnp.concatenate([query_weight, key_matrix, value_matrix, gains], axis=1)
    down_t = down_weight.T
    shard_mlp = []
    for c in range(CHUNKS):
        cols = slice(c * tile, (c + 1) * tile)
        shard_mlp.append(
            jnp.concatenate([gate_weight[:, cols], up_weight[:, cols], down_t[:, cols]], axis=1)
        )
    (w_qkv,) = gather([shard_qkv], n_dp, n_t, 0)
    w_qkv = w_qkv.reshape(n_t, width, shard_qkv.shape[1])
    gain_cols = w_qkv[0, :, nq + 2 * nk : nq + 2 * nk + 2].astype(f32)
    gain_one, gain_two = gain_cols[:, 0], gain_cols[:, 1]

    position = (me_t * rows + jnp.arange(rows, dtype=jnp.int32)).astype(f32)
    freqs = rope_base ** (-(jnp.arange(HALF, dtype=f32) * 2.0) / HEAD_SIZE)
    angles = freqs[:, None] * position[None, :]
    cosine, sine = jnp.cos(angles), jnp.sin(angles)
    live = (me_t * rows + jnp.arange(rows, dtype=jnp.int32) < length).astype(f32)[:, None]
    x = tokens.astype(f32)
    inv_one = lax.rsqrt(jnp.mean(x * x, axis=1, keepdims=True) + eps_norm)
    g32 = cotangent.astype(f32) * live
    g = g32.astype(bf16)
    gt = g.T
    n1 = (x * inv_one * gain_one).astype(bf16)
    q, kv = qkv_project(n1, w_qkv, cosine, sine, nq, nk)
    q = q.reshape(n_t * nq, rows)

    w_out, w_mlp, *above, att, lse = gather(
        [out_weight.T] + shard_mlp[:MERGED], n_dp, n_t, 1, (kv, q, length), MERGED
    )
    w_out = w_out.reshape(n_t, width, no)
    w_mlp = w_mlp.reshape(n_t, width, 3 * tile * MERGED)
    kvs = [kv] + above
    att_z = att.reshape(n_t, no, rows)
    h_one = out_project(att_z, w_out, tokens, no, 0)

    inv_two = lax.rsqrt(jnp.mean(h_one * h_one, axis=1, keepdims=True) + eps_norm)
    n2 = (h_one * inv_two * gain_two).astype(bf16)
    n2t = n2.T
    out_sum, dn_sum, share, w_last = mlp_gather(
        n2, n2t, g, gt, w_mlp, shard_mlp[MERGED], tile, n_dp, n_t, 4
    )
    w_last = w_last.reshape(n_t, width, 3 * tile)
    shares = [share]
    out_sum, dn_sum, share = mlp(
        me, n2, n2t, g, gt, w_last, 0, tile, (out_sum, dn_sum), n_dp
    )
    shares.append(share)
    carry = (out_sum, dn_sum)
    mlp_out, d_n2 = carry
    block_out = (live * (h_one + mlp_out)).astype(bf16)

    scaled = d_n2 * gain_two
    inner = jnp.mean(scaled * h_one, axis=1, keepdims=True)
    gain_two_part = jnp.sum(d_n2 * h_one * inv_two, axis=0)
    d_h = g32 + inv_two * scaled - h_one * (inv_two * inv_two * inv_two * inner)
    d_h_low = d_h.astype(bf16)
    d_h_t = d_h_low.T
    d_att, share = out_back(me, d_h_low, d_h_t, att_z, w_out, no, 0, n_dp)
    shares.append(share)

    d_att = d_att.reshape(n_t * no, rows)
    groups, _, lanes = lse.shape
    delta = (d_att.astype(f32) * att.astype(f32)).reshape(groups, -1, HEAD_SIZE, rows).sum(axis=2)
    delta = delta.reshape(groups, 1, lanes)
    *grads, out_share, d_q, d_kv = scatter(
        shares,
        n_dp,
        n_t,
        2,
        (sc, q, d_att, lse, delta, kvs),
    )
    n1t = n1.T
    d_n1, q_part, kv_part = qkv_back(
        me, d_q.reshape(n_t, nq, rows), d_kv, cosine, sine, n1t, w_qkv, nq, nk, n_dp
    )
    q_share, kv_share = scatter([q_part, kv_part], n_dp, n_t, 3)

    scaled = d_n1 * gain_one
    inner = jnp.mean(scaled * x, axis=1, keepdims=True)
    gain_one_part = jnp.sum(d_n1 * x * inv_one, axis=0)
    d_x = inv_one * scaled - x * (inv_one * inv_one * inv_one * inner)
    tokens_grad = (d_h + d_x).astype(bf16)

    gain_parts = jnp.stack([gain_one_part.reshape(n_dp, block), gain_two_part.reshape(n_dp, block)], 1)
    gain_parts = to_relative(gain_parts, me_dp, n_dp)
    gain_share = reduce_small(gain_parts, me_dp, n_dp, n_t)

    gate_share = jnp.concatenate([s[:, :tile] for s in grads], axis=1)
    up_share = jnp.concatenate([s[:, tile : 2 * tile] for s in grads], axis=1)
    down_share = jnp.concatenate([s[:, 2 * tile :].T for s in grads], axis=0)
    return (
        block_out,
        tokens_grad,
        gain_share[0],
        q_share,
        kv_share[:, :nk],
        kv_share[:, nk:],
        out_share.T,
        gain_share[1],
        gate_share,
        up_share,
        down_share,
    )


def solution(mesh):
    in_specs = (
        P(("dp", "tensor"), None),
        P("dp"),
        P(("dp", "tensor"), None),
        P("dp"),
        P("dp", "tensor"),
        P("dp", "tensor"),
        P("dp", "tensor"),
        P("tensor", "dp"),
        P("dp"),
        P("dp", "tensor"),
        P("dp", "tensor"),
        P("tensor", "dp"),
    )
    out_specs = (
        P(("dp", "tensor"), None),
        P(("dp", "tensor"), None),
        P("dp"),
        P("dp", "tensor"),
        P("dp", "tensor"),
        P("dp", "tensor"),
        P("tensor", "dp"),
        P("dp"),
        P("dp", "tensor"),
        P("dp", "tensor"),
        P("tensor", "dp"),
    )
    fn = functools.partial(local, mesh.shape["dp"], mesh.shape["tensor"])
    return jax.shard_map(fn, mesh=mesh, in_specs=in_specs, out_specs=out_specs, check_vma=False)
```

```python
import functools
import math

import jax
import jax.numpy as jnp
from jax import lax
from jax.experimental import pallas as pl
from jax.experimental.pallas import tpu as pltpu
from jax.sharding import PartitionSpec as P

HEAD_SIZE = 96
HALF = HEAD_SIZE // 2
GAIN_LANES = 128
CHUNKS = 4
MERGED = CHUNKS - 1
CLIMB_AT = 7
CLIMB_STEP = 4
KEY_TILE = 256
NEG = -1e30

eps_norm = 1e-05
rope_base = 100000.0
SCALE = 1.0 / math.sqrt(HEAD_SIZE)
SCALE2 = SCALE * math.log2(math.e)

f32 = jnp.float32
bf16 = jnp.bfloat16
VMEM_LIMIT = 56 * 1024 * 1024


def dot(a, b, dims=((1,), (0,))):
    return lax.dot_general(a, b, (dims, ((), ())), preferred_element_type=f32)


def params(*semantics):
    return pltpu.CompilerParams(dimension_semantics=semantics, vmem_limit_bytes=VMEM_LIMIT)


def cost(flops, nbytes, trans=0):
    return pl.CostEstimate(flops=int(flops), bytes_accessed=int(nbytes), transcendentals=int(trans))


def place(ref, me, grad, col=0):
    count, block = ref.shape[1], ref.shape[2]
    for d in range(count):
        r = me ^ d
        at = (r & 1) * (count // 2) + (r >> 1)
        ref[0, at, :, col : col + grad.shape[1]] = grad[d * block : (d + 1) * block]


def turn(y, cosine, sine, sign):
    parts = []
    for h in range(y.shape[0] // HEAD_SIZE):
        a = y[h * HEAD_SIZE : h * HEAD_SIZE + HALF]
        b = y[h * HEAD_SIZE + HALF : (h + 1) * HEAD_SIZE]
        parts.append(a * cosine - sign * (b * sine))
        parts.append(b * cosine + sign * (a * sine))
    return jnp.concatenate(parts, axis=0)


def qkv_kernel(nq, nk, n1_ref, w_ref, cos_ref, sin_ref, q_ref, kv_ref):
    w = w_ref[0, :, : nq + 2 * nk]
    y = dot(n1_ref[...], w).T
    cosine, sine = cos_ref[...], sin_ref[...]
    q_ref[0] = turn(y[:nq], cosine, sine, 1.0).astype(bf16)
    kv_ref[0] = turn(y[nq : nq + nk], cosine, sine, 1.0).astype(bf16)
    kv_ref[1] = y[nq + nk :].astype(bf16)


def qkv_project(n1, w, cosine, sine, nq, nk):
    rows, width = n1.shape
    zs, _, cols = w.shape
    return pl.pallas_call(
        functools.partial(qkv_kernel, nq, nk),
        grid=(zs,),
        in_specs=[
            pl.BlockSpec((rows, width), lambda z: (0, 0)),
            pl.BlockSpec((1, width, cols), lambda z: (z, 0, 0)),
            pl.BlockSpec((HALF, rows), lambda z: (0, 0)),
            pl.BlockSpec((HALF, rows), lambda z: (0, 0)),
        ],
        out_specs=[
            pl.BlockSpec((1, nq, rows), lambda z: (z, 0, 0)),
            pl.BlockSpec((2, nk, rows), lambda z: (0, z, 0)),
        ],
        out_shape=[
            jax.ShapeDtypeStruct((zs, nq, rows), bf16),
            jax.ShapeDtypeStruct((2, zs * nk, rows), bf16),
        ],
        compiler_params=params("arbitrary"),
        cost_estimate=cost(2 * rows * width * cols * zs, 2 * zs * width * cols + 8 * rows * width),
        name="qkv_project",
    )(n1, w, cosine, sine)


def out_kernel(att_ref, w_ref, x_ref, h_ref):
    z = pl.program_id(0)

    @pl.when(z == 0)
    def _():
        h_ref[...] = x_ref[...].astype(f32)

    h_ref[...] += dot(att_ref[0].T, w_ref[0], ((1,), (1,)))


def out_project(att, w, x, no, col):
    zs, _, rows = att.shape
    width = x.shape[1]
    return pl.pallas_call(
        out_kernel,
        grid=(zs,),
        in_specs=[
            pl.BlockSpec((1, no, rows), lambda z: (z, 0, 0)),
            pl.BlockSpec((1, width, no), lambda z: (z, 0, col)),
            pl.BlockSpec((rows, width), lambda z: (0, 0)),
        ],
        out_specs=pl.BlockSpec((rows, width), lambda z: (0, 0)),
        out_shape=jax.ShapeDtypeStruct((rows, width), f32),
        compiler_params=params("arbitrary"),
        cost_estimate=cost(2 * rows * width * no * zs, 2 * zs * width * no + 8 * rows * width),
        name="out_project",
    )(att, w, x)


def out_back_kernel(me_ref, dh_ref, dht_ref, att_ref, w_ref, da_ref, grad_ref):
    w = w_ref[0]
    da_ref[0] = dot(dh_ref[...], w).T.astype(bf16)
    place(grad_ref, me_ref[1], dot(dht_ref[...], att_ref[0].T).astype(bf16))


def out_back(me, dh, dht, att, w, no, col, n_dp):
    zs, _, rows = att.shape
    width = dh.shape[1]
    block = width // n_dp
    return pl.pallas_call(
        out_back_kernel,
        grid_spec=pltpu.PrefetchScalarGridSpec(
            num_scalar_prefetch=1,
            grid=(zs,),
            in_specs=[
                pl.BlockSpec((rows, width), lambda z, m: (0, 0)),
                pl.BlockSpec((width, rows), lambda z, m: (0, 0)),
                pl.BlockSpec((1, no, rows), lambda z, m: (z, 0, 0)),
                pl.BlockSpec((1, width, no), lambda z, m: (z, 0, col)),
            ],
            out_specs=[
                pl.BlockSpec((1, no, rows), lambda z, m: (z, 0, 0)),
                pl.BlockSpec((1, n_dp, block, no), lambda z, m: (z ^ m[0], 0, 0, 0)),
            ],
        ),
        out_shape=[
            jax.ShapeDtypeStruct((zs, no, rows), bf16),
            jax.ShapeDtypeStruct((zs, n_dp, block, no), bf16),
        ],
        compiler_params=params("arbitrary"),
        cost_estimate=cost(4 * rows * width * no * zs, 4 * zs * width * no + 8 * rows * width),
        name="out_back",
    )(me, dh, dht, att, w)


def key_mask(s, key_first, query_first, length, rows, diagonal):
    key = key_first + lax.broadcasted_iota(jnp.int32, (s.shape[0], 1), 0)
    ok = key < length
    if diagonal:
        lane = lax.broadcasted_iota(jnp.int32, s.shape, 1)
        query = query_first + lax.rem(lane, rows)
        ok = ok & (key <= query)
    return jnp.broadcast_to(ok, s.shape)


def mlp_step(tile, me, n2_ref, n2t_ref, g_ref, gt_ref, w_ref, out_ref, dn_ref, grad_ref):
    pair = w_ref[0, :, : 2 * tile]
    wd = w_ref[0, :, 2 * tile :]
    both = dot(n2_ref[...], pair)
    gate, up = both[:, :tile], both[:, tile:]
    d_hidden = dot(g_ref[...], wd)
    sigma = 1.0 / (1.0 + jnp.exp(-gate))
    active = gate * sigma
    hidden = (active * up).astype(bf16)
    d_gate = (d_hidden * up * (sigma * (1.0 + gate * (1.0 - sigma)))).astype(bf16)
    d_up = (d_hidden * active).astype(bf16)
    d_both = jnp.concatenate([d_gate, d_up], axis=1)
    out_ref[...] += dot(hidden, wd, ((1,), (1,)))
    dn_ref[...] += dot(d_both, pair, ((1,), (1,)))
    place(grad_ref, me, dot(n2t_ref[...], d_both).astype(bf16), 0)
    place(grad_ref, me, dot(gt_ref[...], hidden).astype(bf16), 2 * tile)


def mlp_kernel(
    tile, first, me_ref, n2_ref, n2t_ref, g_ref, gt_ref, w_ref, *refs
):
    if first:
        out_ref, dn_ref, grad_ref = refs
    else:
        out_in, dn_in, out_ref, dn_ref, grad_ref = refs
    z = pl.program_id(0)

    @pl.when(z == 0)
    def _():
        if first:
            out_ref[...] = jnp.zeros_like(out_ref)
            dn_ref[...] = jnp.zeros_like(dn_ref)
        else:
            out_ref[...] = out_in[...]
            dn_ref[...] = dn_in[...]

    mlp_step(tile, me_ref[1], n2_ref, n2t_ref, g_ref, gt_ref, w_ref, out_ref, dn_ref, grad_ref)


def mlp(me, n2, n2t, g, gt, w, chunk, tile, carry, n_dp):
    rows, width = n2.shape
    zs = w.shape[0]
    block = width // n_dp
    full = pl.BlockSpec((rows, width), lambda z, m: (0, 0))
    full_t = pl.BlockSpec((width, rows), lambda z, m: (0, 0))
    grad_spec = pl.BlockSpec((1, n_dp, block, 3 * tile), lambda z, m: (z ^ m[0], 0, 0, 0))
    first = carry is None
    in_specs = [
        full,
        full_t,
        full,
        full_t,
        pl.BlockSpec((1, width, 3 * tile), lambda z, m: (z, 0, chunk)),
    ]
    args = [me, n2, n2t, g, gt, w]
    aliases = {}
    if not first:
        in_specs += [full, full]
        aliases = {6: 0, 7: 1}
        args += list(carry)
    return pl.pallas_call(
        functools.partial(mlp_kernel, tile, first),
        grid_spec=pltpu.PrefetchScalarGridSpec(
            num_scalar_prefetch=1,
            grid=(zs,),
            in_specs=in_specs,
            out_specs=[full, full, grad_spec],
        ),
        out_shape=[
            jax.ShapeDtypeStruct((rows, width), f32),
            jax.ShapeDtypeStruct((rows, width), f32),
            jax.ShapeDtypeStruct((zs, n_dp, block, 3 * tile), bf16),
        ],
        input_output_aliases=aliases,
        compiler_params=params("arbitrary"),
        cost_estimate=cost(
            18 * rows * width * tile * zs, 4 * zs * width * 3 * tile + 24 * rows * width
        ),
        name="mlp",
    )(*args)


def pairs(count, mask):
    return [(i, i ^ mask) for i in range(count)]


def bits_of(count):
    return [1 << b for b in range(count.bit_length() - 1)]


def relative_order(count):
    return [r for low in (0, 1) for r in range(count) if (r & 1) == low]


def to_relative(rows_first, me, count):
    block = rows_first.shape[0] // count
    parts = [
        lax.dynamic_slice_in_dim(rows_first, (me ^ r) * block, block, axis=0)
        for r in relative_order(count)
    ]
    return jnp.concatenate(parts, axis=0)


def reduce_small(values, me, n_dp, n_t):
    order = relative_order(n_dp)
    buf = values
    left = n_dp
    buf = buf[: left // 2] + lax.ppermute(buf[left // 2 :], "dp", pairs(n_dp, 1))
    left //= 2
    for bit in [b for b in bits_of(n_dp) if b > 1][::-1]:
        buf = buf[: left // 2] + lax.ppermute(buf[left // 2 :], "dp", pairs(n_dp, bit))
        left //= 2
    buf = buf[0]
    for bit in bits_of(n_t):
        buf = buf + lax.ppermute(buf, "tensor", pairs(n_t, bit))
    return buf


MESH = pl.DeviceIdType.MESH


def log2(n):
    return n.bit_length() - 1


def nearest_first(n_t):
    return [sorted(range(n_t), key=lambda p: (abs(p - z), p)) for z in range(n_t)]


def pick(values, z):
    out = jnp.int32(values[0])
    for i in range(1, len(values)):
        out = jnp.where(z == i, jnp.int32(values[i]), out)
    return out


def neighbours(n_dp, n_t, me, z):
    barrier = pltpu.get_barrier_semaphore()
    masks = [1 << b for b in range(log2(n_dp))]
    for mask in masks:
        pl.semaphore_signal(barrier, 1, device_id=(me ^ mask, z), device_id_type=MESH)

    @pl.when(z > 0)
    def _():
        pl.semaphore_signal(barrier, 1, device_id=(me, z - 1), device_id_type=MESH)

    @pl.when(z < n_t - 1)
    def _():
        pl.semaphore_signal(barrier, 1, device_id=(me, z + 1), device_id_type=MESH)

    count = len(masks) + (z > 0).astype(jnp.int32) + (z < n_t - 1).astype(jnp.int32)
    pl.semaphore_wait(barrier, count)


class Gather:
    def __init__(self, n_dp, n_t, me, z, index, shard, whole, sems, lanes=None):
        self.n_dp, self.n_t, self.me, self.z = n_dp, n_t, me, z
        self.index, self.shard, self.whole, self.lanes = index, shard, whole, lanes
        self.own, self.z_send, self.z_recv, self.x_send, self.x_recv = sems
        self.bits = log2(n_dp) - 1

    def place_of(self, piece, d):
        if self.lanes is None:
            return self.whole.at[piece, d]
        return self.whole.at[piece, d, :, self.lanes]

    def local(self):
        return pltpu.make_async_copy(
            self.shard, self.place_of(self.z, self.me), self.own.at[self.index]
        )

    def hop(self, piece, direction, hops):
        source = self.place_of(piece, self.me)
        step = 1 - 2 * direction
        return pltpu.make_async_remote_copy(
            source,
            source,
            self.z_send.at[self.index, direction, hops],
            self.z_recv.at[self.index, direction, hops],
            device_id=(self.me, jnp.clip(self.z + step, 0, self.n_t - 1)),
            device_id_type=MESH,
        )

    def send_own(self):
        local = self.local()
        local.start()
        local.wait()

        @pl.when(self.z < self.n_t - 1)
        def _():
            self.hop(self.z, 0, 0).start()

        @pl.when(self.z > 0)
        def _():
            self.hop(self.z, 1, 0).start()

    def order(self, k):
        return pick([row[k] for row in nearest_first(self.n_t)], self.z)

    def arrive(self, k):
        if k == 0:
            return
        piece = self.order(k)
        direction = (piece > self.z).astype(jnp.int32)
        hops = jnp.abs(piece - self.z)
        self.hop(piece, direction, hops - 1).wait_recv()
        on = jnp.where(direction == 0, self.z < self.n_t - 1, self.z > 0)

        @pl.when(on)
        def _():
            self.hop(piece, direction, hops).start()

    def doubling(self, k, stage, i, incoming=False):
        piece = self.order(k)
        odd = (piece & 1) == 1
        bit = jnp.where(odd, 1 << (self.bits - stage), 2 << stage)
        shift = jnp.where(odd, self.bits - stage + 1, 1)
        partner = self.me ^ bit
        origin = partner if incoming else self.me
        held = self.place_of(piece, origin ^ (i << shift))
        at = (1 << stage) - 1 + i
        return pltpu.make_async_remote_copy(
            held,
            held,
            self.x_send.at[self.index, k, at],
            self.x_recv.at[self.index, k, at],
            device_id=(partner, self.z),
            device_id_type=MESH,
        )

    def core(self, k, i, incoming=False):
        piece = self.order(k)
        partner = self.me ^ 1
        origin = partner if incoming else self.me
        held = self.place_of(piece, origin ^ (i << 1))
        at = (1 << self.bits) - 1 + i
        return pltpu.make_async_remote_copy(
            held,
            held,
            self.x_send.at[self.index, k, at],
            self.x_recv.at[self.index, k, at],
            device_id=(partner, self.z),
            device_id_type=MESH,
        )

    def each(self, count, body):
        if count <= 4:
            for i in range(count):
                body(i)
        else:
            lax.fori_loop(0, count, lambda i, _: (body(i), 0)[1], 0)

    def spread(self, k, stage):
        if stage > 0:
            self.each(1 << (stage - 1), lambda i: self.doubling(k, stage - 1, i, True).wait_recv())
        if stage < self.bits:
            self.each(1 << stage, lambda i: self.doubling(k, stage, i).start())
        else:
            self.each(1 << self.bits, lambda i: self.core(k, i).start())

    def finish(self, k):
        self.each(1 << self.bits, lambda i: self.core(k, i, True).wait_recv())
        for stage in range(self.bits):
            self.each(1 << stage, lambda i: self.doubling(k, stage, i).wait_send())
        self.each(1 << self.bits, lambda i: self.core(k, i).wait_send())
        piece = self.order(k)
        hops = jnp.abs(piece - self.z)
        if k == 0:

            @pl.when(self.z < self.n_t - 1)
            def _():
                self.hop(piece, 0, 0).wait_send()

            @pl.when(self.z > 0)
            def _():
                self.hop(piece, 1, 0).wait_send()
        else:
            direction = (piece > self.z).astype(jnp.int32)
            on = jnp.where(direction == 0, self.z < self.n_t - 1, self.z > 0)

            @pl.when(on)
            def _():
                self.hop(piece, direction, hops).wait_send()


class Climb:
    def __init__(self, n_t, me, z, own, kept, sems):
        self.n_t, self.me, self.z, self.own, self.kept = n_t, me, z, own, kept
        self.send, self.recv = sems

    def hop(self, r):
        source = self.own if r == 0 else self.kept[r - 1]
        return pltpu.make_async_remote_copy(
            source,
            self.kept[r],
            self.send.at[r],
            self.recv.at[r],
            device_id=(self.me, jnp.minimum(self.z + 1, self.n_t - 1)),
            device_id_type=MESH,
        )

    def start(self, r):
        @pl.when((self.z >= r) & (self.z < self.n_t - 1))
        def _():
            self.hop(r).start()

    def arrive(self, r):
        @pl.when(self.z >= r)
        def _():
            self.hop(r - 1).wait_recv()

    def finish(self, r):
        @pl.when((self.z >= r) & (self.z < self.n_t - 1))
        def _():
            self.hop(r).wait_send()


def attend_part(r, z, length, q_ref, kv_ref, m_ref, l_ref, acc_ref):
    rows = q_ref.shape[1]
    groups = m_ref.shape[0]
    group = q_ref.shape[0] // (groups * HEAD_SIZE)
    first = z * rows

    @pl.when(z >= r)
    def _():
        def body(g, _):
            base = pl.multiple_of(g * (group * HEAD_SIZE), 32)
            at = pl.multiple_of(g * HEAD_SIZE, 32)
            q = jnp.concatenate(
                [q_ref[pl.ds(base + a * HEAD_SIZE, HEAD_SIZE), :] for a in range(group)], axis=1
            )
            if r == 0:
                m = jnp.full((1, group * rows), NEG, f32)
                total = jnp.zeros((1, group * rows), f32)
                acc = jnp.zeros((HEAD_SIZE, group * rows), f32)
            else:
                m, total, acc = m_ref[g], l_ref[g], acc_ref[g]
            for j in range(rows // KEY_TILE):
                part = slice(j * KEY_TILE, (j + 1) * KEY_TILE)
                k = kv_ref[0, pl.ds(at, HEAD_SIZE), part]
                v = kv_ref[1, pl.ds(at, HEAD_SIZE), part]
                s = dot(k, q, ((0,), (0,)))
                ok = key_mask(s, first - r * rows + j * KEY_TILE, first, length, rows, r == 0)
                s = jnp.where(ok, s, NEG)
                new = jnp.maximum(m, jnp.max(s, axis=0, keepdims=True))
                shrink = jnp.exp2((m - new) * SCALE2)
                p = jnp.exp2(s * SCALE2 - new * SCALE2)
                total = total * shrink + jnp.sum(p, axis=0, keepdims=True)
                acc = acc * shrink + dot(v, p.astype(bf16))
                m = new
            m_ref[g], l_ref[g], acc_ref[g] = m, total, acc
            return 0

        lax.fori_loop(0, groups, body, 0)


def attend_end(q_shape, m_ref, l_ref, acc_ref, att_ref):
    groups = m_ref.shape[0]
    rows = q_shape[1]
    group = q_shape[0] // (groups * HEAD_SIZE)

    def body(g, _):
        out = acc_ref[g] / l_ref[g]
        for a in range(group):
            own = pl.ds(pl.multiple_of((g * group + a) * HEAD_SIZE, 32), HEAD_SIZE)
            att_ref[own, :] = out[:, a * rows : (a + 1) * rows].astype(bf16)
        m_ref[g] = m_ref[g] * SCALE2 + jnp.log2(l_ref[g])
        return 0

    lax.fori_loop(0, groups, body, 0)


def gather_kernel(n_dp, n_t, count, merged, climbs, *refs):
    refs = list(refs)

    def take(k):
        out = refs[:k]
        del refs[:k]
        return out

    shards = take(count)
    if climbs:
        own, q_ref, length_ref = take(3)
    wholes = [(ref, None) for ref in take(count - merged)]
    if merged:
        (ref,) = take(1)
        wide = shards[-1].shape[1]
        wholes += [(ref, slice(i * wide, (i + 1) * wide)) for i in range(merged)]
    if climbs:
        kept = take(n_t - 1)
        att_ref, lse_ref = take(2)
    sems = take(5)
    me, z = lax.axis_index("dp"), lax.axis_index("tensor")
    neighbours(n_dp, n_t, me, z)
    works = [
        Gather(n_dp, n_t, me, z, c, shards[c], wholes[c][0], sems, wholes[c][1])
        for c in range(count)
    ]
    if climbs:
        climb_sems = take(2)
        l_ref, acc_ref, kv_ref, kv_sem = take(4)
        climb = Climb(n_t, me, z, own, kept, climb_sems)
        climb.start(0)
        length = length_ref[0]

    def attend_step(r):
        if r > 0:
            climb.arrive(r)
            if r < n_t - 1:
                climb.start(r)

        @pl.when(z >= r)
        def _():
            fetch = pltpu.make_async_copy(own if r == 0 else kept[r - 1], kv_ref, kv_sem)
            fetch.start()
            fetch.wait()

        attend_part(r, z, length, q_ref, kv_ref, lse_ref, l_ref, acc_ref)

    stages = log2(n_dp)
    works[0].send_own()
    total = count * n_t
    todo = list(range(n_t)) if climbs else []
    for n in range(total + 2 * (stages - 1)):
        if n < total:
            c, k = divmod(n, n_t)
            works[c].arrive(k)
            works[c].spread(k, 0)
            if k == 0 and c + 1 < count:
                works[c + 1].send_own()
        for stage in range(1, stages):
            at = n - 2 * stage
            if 0 <= at < total:
                works[at // n_t].spread(at % n_t, stage)
        if todo and (n == 2 if todo[0] == 0 else n == CLIMB_AT + CLIMB_STEP * (todo[0] - 1)):
            attend_step(todo.pop(0))
    for r in todo:
        attend_step(r)
    if climbs:
        attend_end(q_ref.shape, lse_ref, l_ref, acc_ref, att_ref)
    for c in range(count):
        for k in range(n_t):
            works[c].finish(k)
    if climbs:
        for r in range(n_t - 1):
            climb.finish(r)


def gather(shards, n_dp, n_t, collective_id, attention=None, merged=0):
    count = len(shards)
    shapes = [
        jax.ShapeDtypeStruct((n_t, n_dp) + s.shape, s.dtype) for s in shards[: count - merged]
    ]
    if merged:
        block, wide = shards[-1].shape
        shapes.append(jax.ShapeDtypeStruct((n_t, n_dp, block, merged * wide), bf16))
    args = list(shards)
    anywhere = pl.BlockSpec(memory_space=pl.ANY)
    vmem = pl.BlockSpec(memory_space=pltpu.VMEM)
    in_specs = [anywhere] * count
    out_specs = [anywhere] * len(shapes)
    scratch = [
        pltpu.SemaphoreType.DMA((count,)),
        pltpu.SemaphoreType.DMA((count, 2, n_t)),
        pltpu.SemaphoreType.DMA((count, 2, n_t)),
        pltpu.SemaphoreType.DMA((count, n_t, n_dp - 1)),
        pltpu.SemaphoreType.DMA((count, n_t, n_dp - 1)),
    ]
    if attention is not None:
        kv, q, length = attention
        rows = q.shape[1]
        groups = kv.shape[1] // HEAD_SIZE
        lanes = q.shape[0] // (groups * HEAD_SIZE) * rows
        args += [kv, q, length.reshape(1)]
        in_specs += [anywhere, vmem, pl.BlockSpec(memory_space=pltpu.SMEM)]
        shapes += [jax.ShapeDtypeStruct(kv.shape, kv.dtype)] * (n_t - 1)
        shapes += [
            jax.ShapeDtypeStruct(q.shape, bf16),
            jax.ShapeDtypeStruct((groups, 1, lanes), f32),
        ]
        out_specs += [anywhere] * (n_t - 1) + [vmem, vmem]
        scratch += [pltpu.SemaphoreType.DMA((n_t,))] * 2
        scratch += [
            pltpu.VMEM((groups, 1, lanes), f32),
            pltpu.VMEM((groups, HEAD_SIZE, lanes), f32),
            pltpu.VMEM(kv.shape, bf16),
            pltpu.SemaphoreType.DMA,
        ]
    return pl.pallas_call(
        functools.partial(gather_kernel, n_dp, n_t, count, merged, attention is not None),
        in_specs=in_specs,
        out_specs=out_specs,
        out_shape=shapes,
        scratch_shapes=scratch,
        compiler_params=pltpu.CompilerParams(
            collective_id=collective_id, has_side_effects=True, vmem_limit_bytes=VMEM_LIMIT
        ),
        name="gather_weights",
    )(*args)


def mlp_gather_kernel(
    n_dp, n_t, tile, n2_ref, n2t_ref, g_ref, gt_ref, w_ref, shard_ref,
    out_ref, dn_ref, grad_ref, whole_ref, *sems
):
    me, z = lax.axis_index("dp"), lax.axis_index("tensor")
    step = pl.program_id(0) * pl.num_programs(1) + pl.program_id(1)
    steps = w_ref.shape[0] * MERGED * n_t
    work = Gather(n_dp, n_t, me, z, 0, shard_ref, whole_ref, sems)
    stages = log2(n_dp)

    @pl.when(step == 0)
    def _():
        neighbours(n_dp, n_t, me, z)
        work.send_own()
        out_ref[...] = jnp.zeros_like(out_ref)
        dn_ref[...] = jnp.zeros_like(dn_ref)

    for n in range(n_t + 2 * (stages - 1)):

        @pl.when(step == min(n, steps - 1))
        def _():
            if n < n_t:
                work.arrive(n)
                work.spread(n, 0)
            for stage in range(1, stages):
                at = n - 2 * stage
                if 0 <= at < n_t:
                    work.spread(at, stage)

    mlp_step(
        tile, me, n2_ref, n2t_ref, g_ref, gt_ref, w_ref, out_ref, dn_ref, grad_ref.at[0]
    )

    @pl.when(step == steps - 1)
    def _():
        for k in range(n_t):
            work.finish(k)


def mlp_gather(n2, n2t, g, gt, w, shard, tile, n_dp, n_t, collective_id):
    rows, width = n2.shape
    block = width // n_dp
    full = pl.BlockSpec((rows, width), lambda c, i: (0, 0))
    full_t = pl.BlockSpec((width, rows), lambda c, i: (0, 0))
    anywhere = pl.BlockSpec(memory_space=pl.ANY)
    cols = 3 * tile
    return pl.pallas_call(
        functools.partial(mlp_gather_kernel, n_dp, n_t, tile),
        grid=(MERGED, n_t),
        in_specs=[
            full,
            full_t,
            full,
            full_t,
            pl.BlockSpec((1, width, cols), lambda c, i: (i, 0, c)),
            anywhere,
        ],
        out_specs=[
            full,
            full,
            pl.BlockSpec(
                (1, 1, n_dp, block, cols),
                lambda c, i: (c, i ^ lax.axis_index("tensor"), 0, 0, 0),
            ),
            anywhere,
        ],
        out_shape=[
            jax.ShapeDtypeStruct((rows, width), f32),
            jax.ShapeDtypeStruct((rows, width), f32),
            jax.ShapeDtypeStruct((MERGED, n_t, n_dp, block, cols), bf16),
            jax.ShapeDtypeStruct((n_t, n_dp, block, cols), bf16),
        ],
        scratch_shapes=[
            pltpu.SemaphoreType.DMA((1,)),
            pltpu.SemaphoreType.DMA((1, 2, n_t)),
            pltpu.SemaphoreType.DMA((1, 2, n_t)),
            pltpu.SemaphoreType.DMA((1, n_t, n_dp - 1)),
            pltpu.SemaphoreType.DMA((1, n_t, n_dp - 1)),
        ],
        compiler_params=pltpu.CompilerParams(
            dimension_semantics=("arbitrary", "arbitrary"),
            collective_id=collective_id,
            has_side_effects=True,
            vmem_limit_bytes=VMEM_LIMIT,
        ),
        name="mlp_gather",
    )(n2, n2t, g, gt, w, shard)


def greet_all(n_dp, n_t, me, z):
    barrier = pltpu.get_barrier_semaphore()
    masks = [1 << b for b in range(log2(n_dp))]
    for mask in masks:
        pl.semaphore_signal(barrier, 1, device_id=(me ^ mask, z), device_id_type=MESH)
    for other in range(1, n_t):
        pl.semaphore_signal(barrier, 1, device_id=(me, z ^ other), device_id_type=MESH)
    pl.semaphore_wait(barrier, len(masks) + n_t - 1)


def count_of(shape):
    return math.prod(shape)


def add_blocks(target, source, dtype=bf16):
    lead = target.shape[:-2]

    def body(i, _):
        at = []
        for extent in lead[::-1]:
            at.append(lax.rem(i, extent))
            i = i // extent
        at = tuple(at[::-1])
        target[at] = (target[at].astype(f32) + source[at].astype(f32)).astype(dtype)
        return 0

    lax.fori_loop(0, count_of(lead), body, 0)


class Scatter:
    def __init__(self, n_dp, n_t, me, z, index, grad, land, out, held, first, cols, tile, landings, sems):
        self.n_t, self.me, self.z, self.index = n_t, me, z, index
        ref, lead = grad
        self.keep, self.send = ref.at[lead + (slice(None), 0)], ref.at[lead + (slice(None), 1)]
        self.land, self.out, self.held = land, out, held
        self.tile, self.landings, self.sems = tile, landings, sems
        self.bits, self.t_bits = log2(n_dp) - 1, log2(n_t)
        self.stages = 2 + self.bits + self.t_bits
        self.cols, self.lanes = cols, slice(first, first + cols)
        self.lead = (n_t,) + (2,) * self.bits

    def remote(self, source, target, slot, dp, z):
        send, recv = self.sems[0], self.sems[1]
        return pltpu.make_async_remote_copy(
            source,
            target,
            send.at[self.index, slot],
            recv.at[self.index, slot],
            device_id=(dp, z),
            device_id_type=MESH,
        )

    def at(self, index=()):
        return index + (slice(None),) * (len(self.lead) - len(index) + 1) + (self.lanes,)

    def load(self):
        return pltpu.make_async_copy(
            self.keep, self.held.at[self.at()], self.sems[2].at[self.index]
        )

    def core(self):
        return self.remote(self.send, self.land, 0, self.me ^ 1, self.z)

    def part(self, half, stage, bit):
        rest = (slice(None),) * (self.bits - 1 - stage)
        done = (0,) * stage
        if half == 0:
            return self.held.at[self.at((slice(0, self.n_t // 2),) + rest + (bit,) + done)]
        return self.held.at[self.at((slice(self.n_t // 2, self.n_t),) + done + (bit,) + rest)]

    def landing(self, which):
        ref = self.landings[which]
        at = (self.index % 2,) + (slice(None),) * (len(ref.shape) - 2) + (slice(0, self.cols),)
        return ref.at[at]

    def plane(self, half, stage):
        mask = 2 << stage if half == 0 else 1 << (self.bits - stage)
        return self.remote(
            self.part(half, stage, 1),
            self.landing(2 * stage + half),
            1 + 2 * stage + half,
            self.me ^ mask,
            self.z,
        )

    def column(self, stage, first, count):
        return self.held.at[self.at((slice(first, first + count),) + (0,) * self.bits)]

    def along(self, stage):
        count = self.n_t >> (stage + 1)
        return self.remote(
            self.column(stage, count, count),
            self.landing(2 * self.bits + stage),
            1 + 2 * self.bits + stage,
            self.me,
            self.z ^ count,
        )

    def start(self, stage):
        if stage < self.bits:
            self.plane(0, stage).start()
            self.plane(1, stage).start()
        elif stage < self.bits + self.t_bits:
            self.along(stage - self.bits).start()

    def event(self, number):
        if number == 0:
            self.core().start()
            self.load().start()
        elif number == 1:
            self.load().wait()
            self.core().wait_recv()
            self.add_land()
            self.start(0)
        elif number <= 1 + self.bits:
            stage = number - 2
            for half in (0, 1):
                self.plane(half, stage).wait_recv()
                add_blocks(self.part(half, stage, 0), self.landing(2 * stage + half))
            self.start(stage + 1)
        else:
            stage = number - 2 - self.bits
            self.along(stage).wait_recv()
            count = self.n_t >> (stage + 1)
            if stage < self.t_bits - 1:
                add_blocks(
                    self.column(stage, 0, count), self.landing(2 * self.bits + stage)
                )
                self.start(number - 1)
            else:
                mine = self.held[self.at((0,) * (1 + self.bits))].astype(f32)
                got = self.landing(2 * self.bits + stage)[0].astype(f32)
                self.out[...] = mine + got

    def add_land(self):
        lead = self.lead

        def at_of(i):
            at = []
            for extent in lead[::-1]:
                at.append(lax.rem(i, extent))
                i = i // extent
            return tuple(at[::-1])

        def fetch(i):
            return pltpu.make_async_copy(
                self.land.at[at_of(i)],
                self.tile.at[lax.rem(i, 2), :, pl.ds(0, self.cols)],
                self.sems[3].at[lax.rem(i, 2)],
            )

        total = count_of(lead)
        fetch(0).start()

        def body(i, _):
            @pl.when(i + 1 < total)
            def _():
                fetch(i + 1).start()

            fetch(i).wait()
            at = self.at(at_of(i))
            got = self.tile[lax.rem(i, 2), :, pl.ds(0, self.cols)].astype(f32)
            self.held[at] = (self.held[at].astype(f32) + got).astype(bf16)
            return 0

        lax.fori_loop(0, total, body, 0)

    def finish(self):
        self.core().wait_send()
        for stage in range(self.bits):
            for half in (0, 1):
                self.plane(half, stage).wait_send()
        for stage in range(self.t_bits):
            self.along(stage).wait_send()


class Descend:
    def __init__(self, n_t, me, z, sums, landed, sems):
        self.n_t, self.me, self.z = n_t, me, z
        self.sums, self.landed, self.send, self.recv = sums, landed, sems[0], sems[1]

    def hop(self, r):
        return pltpu.make_async_remote_copy(
            self.sums[r],
            self.landed[r - 1],
            self.send.at[r],
            self.recv.at[r],
            device_id=(self.me, jnp.maximum(self.z - 1, 0)),
            device_id_type=MESH,
        )

    def start(self, r):
        @pl.when(self.z >= r)
        def _():
            self.hop(r).start()

    def finish(self, r):
        @pl.when(self.z >= r)
        def _():
            self.hop(r).wait_send()


def attention_part(r, group, n_t, z, length, q_ref, do_ref, lse_ref, delta_ref, kv_ref, dq_ref, sum_ref):
    rows = q_ref.shape[1]
    groups = lse_ref.shape[0]
    per = group * HEAD_SIZE
    first = z * rows
    active = z >= r
    fresh = r == n_t - 1

    def beside(ref, base):
        return jnp.concatenate(
            [ref[pl.ds(base + a * HEAD_SIZE, HEAD_SIZE), :] for a in range(group)], axis=1
        )

    @pl.when(active)
    def _():
        def body(g, _):
            base = pl.multiple_of(g * per, 32)
            at = pl.multiple_of(g * HEAD_SIZE, 32)
            q = beside(q_ref, base)
            do = beside(do_ref, base)
            delta, lse = delta_ref[g], lse_ref[g]
            dq = jnp.zeros(q.shape, f32)
            for j in range(rows // KEY_TILE):
                part = slice(j * KEY_TILE, (j + 1) * KEY_TILE)
                k, v = kv_ref[0, pl.ds(at, HEAD_SIZE), part], kv_ref[1, pl.ds(at, HEAD_SIZE), part]
                s = dot(k, q, ((0,), (0,)))
                ok = key_mask(s, first - r * rows + j * KEY_TILE, first, length, rows, r == 0)
                p = jnp.where(ok, jnp.exp2(s * SCALE2 - lse), 0.0)
                dp = dot(v, do, ((0,), (0,)))
                ds = (p * (dp - delta)).astype(bf16)
                dv = dot(do, p.astype(bf16), ((1,), (1,)))
                dk = dot(q, ds, ((1,), (1,))) * SCALE
                sum_ref[0, pl.ds(at, HEAD_SIZE), part] = dk.astype(bf16)
                sum_ref[1, pl.ds(at, HEAD_SIZE), part] = dv.astype(bf16)
                dq += dot(k, ds)
            for a in range(group):
                own = pl.ds(base + a * HEAD_SIZE, HEAD_SIZE)
                term = dq[:, a * rows : (a + 1) * rows] * SCALE
                if fresh:
                    dq_ref[own, :] = term
                else:
                    dq_ref[own, :] += term
            return 0

        lax.fori_loop(0, groups, body, 0)

    @pl.when(jnp.logical_not(active))
    def _():
        sum_ref[...] = jnp.zeros_like(sum_ref)
        if fresh:
            dq_ref[...] = jnp.zeros_like(dq_ref)


def back_part(
    n_dp, n_t, me, z, nq, nk, dq_ref, dkv_ref, cos_ref, sin_ref, n1t_ref, w_hbm, wq_ref, wkv_ref,
    dn_ref, gbufs, parts, sems
):
    width = n1t_ref.shape[0]
    block = width // n_dp
    bits = log2(n_dp) - 1
    step = width // 4
    cosine, sine = cos_ref[...], sin_ref[...]

    def body(i, _):
        copies = [
            pltpu.make_async_copy(w_hbm.at[i, :, 0:nq], wq_ref.at[:, 0:nq], sems.at[0]),
            pltpu.make_async_copy(w_hbm.at[i, :, nq : nq + 2 * nk], wkv_ref, sems.at[1]),
        ]
        for copy in copies:
            copy.start()
        q_rows = pl.ds(pl.multiple_of(i * nq, 32), nq)
        k_rows = pl.ds(pl.multiple_of(i * nk, 32), nk)
        dq = turn(dq_ref[q_rows, :], cosine, sine, -1.0).astype(bf16).T
        dk = turn(dkv_ref[0, k_rows, :].astype(f32), cosine, sine, -1.0).astype(bf16)
        dkv = jnp.concatenate([dk, dkv_ref[1, k_rows, :]], axis=0).T
        for copy in copies:
            copy.wait()
        for c in range(4):
            part = slice(c * step, (c + 1) * step)
            dn_ref[:, part] += dot(dq, wq_ref[part, 0:nq], ((1,), (1,))) + dot(
                dkv, wkv_ref[part, :], ((1,), (1,))
            )
            for d, gbuf in ((dq, gbufs[0]), (dkv, gbufs[1])):
                grad = dot(n1t_ref[part, :], d).astype(bf16)
                for b in range(step // block):
                    r = me ^ (c * (step // block) + b)
                    at = (r & 1,) + tuple((r >> bit) & 1 for bit in range(bits, 0, -1))
                    gbuf[at] = grad[b * block : (b + 1) * block]
        stores = [
            pltpu.make_async_copy(gbufs[k], parts[k].at[i ^ z], sems.at[2 + k]) for k in (0, 1)
        ]
        for store in stores:
            store.start()
        for store in stores:
            store.wait()
        return 0

    dn_ref[...] = jnp.zeros_like(dn_ref)
    lax.fori_loop(0, n_t, body, 0)


def scatter_kernel(n_dp, n_t, stacked, cols, nq, nk, *refs):
    refs = list(refs)

    def take(k):
        out = refs[:k]
        del refs[:k]
        return out

    grads = []
    for ref, depth in zip(take(len(stacked)), stacked):
        grads += [(ref, (c,)) for c in range(depth)] if depth else [(ref, ())]
    early = len(grads)
    count = early + 2
    sc_ref, q_hbm, do_hbm, lse_ref, delta_ref = take(5)
    kvs = take(n_t)
    cos_ref, sin_ref, n1t_hbm, w_hbm = take(4)
    lands, outs = take(count), take(count)
    dn_ref, q_part, kv_part = take(3)
    grads += [(q_part, ()), (kv_part, ())]
    helds = take(early)
    (tile,) = take(1)
    landings = take(2 * (log2(n_dp) - 1) + log2(n_t))
    sems = take(4)
    dq_ref, dkv_ref, q_ref, do_ref, kv_ref, wkv_ref, gbuf_q, gbuf_kv, own_sems = take(9)
    sums, landed = take(n_t - 1), take(n_t - 1)
    chain_sems = take(2)
    me, z = lax.axis_index("dp"), lax.axis_index("tensor")
    greet_all(n_dp, n_t, me, z)
    places = [(held, 0) for held in helds] + [(helds[0], 0), (helds[0], cols[early])]
    works = [
        Scatter(
            n_dp, n_t, me, z, c, grads[c], lands[c], outs[c], *places[c], cols[c], tile, landings, sems
        )
        for c in range(count)
    ]
    stages = works[0].stages

    shift = max(0, stages - 1 - early)
    turns = [c if c < early else c + shift for c in range(count)]

    def tick(k):
        for number in range(stages - 1, 0, -1):
            if k - (number - 1) in turns:
                works[turns.index(k - (number - 1))].event(number)
        if k + 2 < early:
            works[k + 2].event(0)

    works[0].event(0)
    works[1].event(0)
    loads = [
        pltpu.make_async_copy(q_hbm, q_ref, own_sems.at[0]),
        pltpu.make_async_copy(do_hbm, do_ref, own_sems.at[1]),
    ]
    for load in loads:
        load.start()
    for load in loads:
        load.wait()
    ticks = list(range(count + shift + stages - 2))
    length = sc_ref[1]
    descend = Descend(n_t, me, z, [dkv_ref] + sums, landed, chain_sems)
    for r in range(n_t - 1, -1, -1):
        target = dkv_ref if r == 0 else sums[r - 1]
        fetch = pltpu.make_async_copy(kvs[r], kv_ref, own_sems.at[2])
        fetch.start()
        fetch.wait()
        attention_part(
            r, nq // nk, n_t, z, length, q_ref, do_ref, lse_ref, delta_ref, kv_ref, dq_ref, target
        )
        if r < n_t - 1:
            @pl.when((z + 1 < n_t) & (z >= r))
            def _():
                descend.hop(r + 1).wait_recv()
                add_blocks(target, landed[r])

        if r > 0:
            descend.start(r)
        tick(ticks.pop(0))
    fetch = pltpu.make_async_copy(n1t_hbm, do_ref, own_sems.at[3])
    fetch.start()
    fetch.wait()
    back_part(
        n_dp, n_t, me, z, nq, nk, dq_ref, dkv_ref, cos_ref, sin_ref, do_ref, w_hbm, q_ref, wkv_ref,
        dn_ref, (gbuf_q, gbuf_kv), (q_part, kv_part), own_sems
    )
    while ticks[0] < stages - 1:
        tick(ticks.pop(0))
    works[0].finish()
    works[early].event(0)
    works[early + 1].event(0)
    for k in ticks:
        tick(k)
    for work in works[1:]:
        work.finish()
    for r in range(1, n_t):
        descend.finish(r)


def scatter(grads, n_dp, n_t, collective_id, attention, back):
    bits = log2(n_dp) - 1
    block = grads[0].shape[-2]
    widest = max(k.shape[-1] for k in grads)
    stacked = [k.shape[0] if k.ndim == 5 else 0 for k in grads]
    sc, q, do, lse, delta, kvs = attention
    cosine, sine, n1t, w, nq, nk = back
    cols = []
    for k, depth in zip(grads, stacked):
        cols += [k.shape[-1]] * max(depth, 1)
    early = len(cols)
    cols += [nq, 2 * nk]
    shapes = [(n_t,) + (2,) * bits + (block, c) for c in cols]
    args = [
        k.reshape(k.shape[: k.ndim - 3] + (2,) * (bits + 1) + k.shape[-2:]) for k in grads
    ]
    anywhere = pl.BlockSpec(memory_space=pl.ANY)
    vmem = pl.BlockSpec(memory_space=pltpu.VMEM)
    smem = pl.BlockSpec(memory_space=pltpu.SMEM)
    in_specs = [anywhere] * len(args) + [smem, anywhere, anywhere, vmem, vmem] + [anywhere] * n_t
    in_specs += [vmem, vmem, anywhere, anywhere]
    args += [sc, q, do, lse, delta] + list(kvs) + [cosine, sine, n1t, w]
    wide = [(2,) * (bits + 1) + (block, c) for c in cols[early:]]
    out_shape = [jax.ShapeDtypeStruct(s, bf16) for s in shapes] + [
        jax.ShapeDtypeStruct((block, c), f32) for c in cols
    ]
    out_shape.append(jax.ShapeDtypeStruct((n1t.shape[1], n1t.shape[0]), f32))
    out_shape += [jax.ShapeDtypeStruct((n_t,) + s, bf16) for s in wide]
    out_specs = [anywhere] * len(cols) + [vmem] * (len(cols) + 1) + [anywhere] * 2
    scratch = [pltpu.VMEM(s, bf16) for s in shapes[:early]]
    scratch.append(pltpu.VMEM((2, block, widest), bf16))
    for stage in range(bits):
        for _ in (0, 1):
            scratch.append(
                pltpu.VMEM((2, n_t // 2) + (2,) * (bits - 1 - stage) + (block, widest), bf16)
            )
    for stage in range(log2(n_t)):
        scratch.append(pltpu.VMEM((2, n_t >> (stage + 1), block, widest), bf16))
    copies = 1 + 2 * bits + log2(n_t)
    scratch += [
        pltpu.SemaphoreType.DMA((len(cols), copies)),
        pltpu.SemaphoreType.DMA((len(cols), copies)),
        pltpu.SemaphoreType.DMA((len(cols),)),
        pltpu.SemaphoreType.DMA((2,)),
        pltpu.VMEM(q.shape, f32),
        pltpu.VMEM(kvs[0].shape, bf16),
        pltpu.VMEM(q.shape, bf16),
        pltpu.VMEM(do.shape, bf16),
        pltpu.VMEM(kvs[0].shape, bf16),
        pltpu.VMEM((n1t.shape[0], 2 * nk), bf16),
        pltpu.VMEM(wide[0], bf16),
        pltpu.VMEM(wide[1], bf16),
        pltpu.SemaphoreType.DMA((4,)),
    ]
    scratch += [pltpu.VMEM(kvs[0].shape, bf16)] * (2 * (n_t - 1))
    scratch += [pltpu.SemaphoreType.DMA((n_t,))] * 2
    outs = pl.pallas_call(
        functools.partial(scatter_kernel, n_dp, n_t, stacked, cols, nq, nk),
        in_specs=in_specs,
        out_specs=out_specs,
        out_shape=out_shape,
        scratch_shapes=scratch,
        compiler_params=pltpu.CompilerParams(
            collective_id=collective_id, has_side_effects=True, vmem_limit_bytes=63 * 1024 * 1024
        ),
        name="scatter_grads",
    )(*args)
    return outs[len(cols) : 2 * len(cols) + 1]


def local(
    n_dp,
    n_t,
    tokens,
    lengths,
    cotangent,
    attn_gain,
    query_weight,
    key_matrix,
    value_matrix,
    out_weight,
    mlp_gain,
    gate_weight,
    up_weight,
    down_weight,
):
    rows, width = tokens.shape
    block = query_weight.shape[0]
    nq, nk = query_weight.shape[1], key_matrix.shape[1]
    no = out_weight.shape[0]
    units = gate_weight.shape[1]
    tile = units // CHUNKS
    me_dp = lax.axis_index("dp")
    me_t = lax.axis_index("tensor")
    length = lengths[0]
    me = jnp.stack([me_t, me_dp]).astype(jnp.int32)
    sc = jnp.stack([me_t.astype(jnp.int32), length])

    gains = jnp.stack([attn_gain, mlp_gain], axis=1)
    gains = jnp.pad(gains, ((0, 0), (0, GAIN_LANES - 2)))
    shard_qkv = jnp.concatenate([query_weight, key_matrix, value_matrix, gains], axis=1)
    down_t = down_weight.T
    shard_mlp = []
    for c in range(CHUNKS):
        cols = slice(c * tile, (c + 1) * tile)
        shard_mlp.append(
            jnp.concatenate([gate_weight[:, cols], up_weight[:, cols], down_t[:, cols]], axis=1)
        )
    (w_qkv,) = gather([shard_qkv], n_dp, n_t, 0)
    w_qkv = w_qkv.reshape(n_t, width, shard_qkv.shape[1])
    gain_cols = w_qkv[0, :, nq + 2 * nk : nq + 2 * nk + 2].astype(f32)
    gain_one, gain_two = gain_cols[:, 0], gain_cols[:, 1]

    position = (me_t * rows + jnp.arange(rows, dtype=jnp.int32)).astype(f32)
    freqs = rope_base ** (-(jnp.arange(HALF, dtype=f32) * 2.0) / HEAD_SIZE)
    angles = freqs[:, None] * position[None, :]
    cosine, sine = jnp.cos(angles), jnp.sin(angles)
    live = (me_t * rows + jnp.arange(rows, dtype=jnp.int32) < length).astype(f32)[:, None]
    x = tokens.astype(f32)
    inv_one = lax.rsqrt(jnp.mean(x * x, axis=1, keepdims=True) + eps_norm)
    g32 = cotangent.astype(f32) * live
    g = g32.astype(bf16)
    gt = g.T
    n1 = (x * inv_one * gain_one).astype(bf16)
    q, kv = qkv_project(n1, w_qkv, cosine, sine, nq, nk)
    q = q.reshape(n_t * nq, rows)

    w_out, w_mlp, *above, att, lse = gather(
        [out_weight.T] + shard_mlp[:MERGED], n_dp, n_t, 1, (kv, q, length), MERGED
    )
    w_out = w_out.reshape(n_t, width, no)
    w_mlp = w_mlp.reshape(n_t, width, 3 * tile * MERGED)
    kvs = [kv] + above
    att_z = att.reshape(n_t, no, rows)
    h_one = out_project(att_z, w_out, tokens, no, 0)

    inv_two = lax.rsqrt(jnp.mean(h_one * h_one, axis=1, keepdims=True) + eps_norm)
    n2 = (h_one * inv_two * gain_two).astype(bf16)
    n2t = n2.T
    out_sum, dn_sum, share, w_last = mlp_gather(
        n2, n2t, g, gt, w_mlp, shard_mlp[MERGED], tile, n_dp, n_t, 4
    )
    w_last = w_last.reshape(n_t, width, 3 * tile)
    shares = [share]
    out_sum, dn_sum, share = mlp(
        me, n2, n2t, g, gt, w_last, 0, tile, (out_sum, dn_sum), n_dp
    )
    shares.append(share)
    carry = (out_sum, dn_sum)
    mlp_out, d_n2 = carry
    block_out = (live * (h_one + mlp_out)).astype(bf16)

    scaled = d_n2 * gain_two
    inner = jnp.mean(scaled * h_one, axis=1, keepdims=True)
    gain_two_part = jnp.sum(d_n2 * h_one * inv_two, axis=0)
    d_h = g32 + inv_two * scaled - h_one * (inv_two * inv_two * inv_two * inner)
    d_h_low = d_h.astype(bf16)
    d_h_t = d_h_low.T
    d_att, share = out_back(me, d_h_low, d_h_t, att_z, w_out, no, 0, n_dp)
    shares.append(share)

    d_att = d_att.reshape(n_t * no, rows)
    groups, _, lanes = lse.shape
    delta = (d_att.astype(f32) * att.astype(f32)).reshape(groups, -1, HEAD_SIZE, rows).sum(axis=2)
    delta = delta.reshape(groups, 1, lanes)
    *grads, out_share, q_share, kv_share, d_n1 = scatter(
        shares,
        n_dp,
        n_t,
        2,
        (sc, q, d_att, lse, delta, kvs),
        (cosine, sine, n1.T, w_qkv, nq, nk),
    )

    scaled = d_n1 * gain_one
    inner = jnp.mean(scaled * x, axis=1, keepdims=True)
    gain_one_part = jnp.sum(d_n1 * x * inv_one, axis=0)
    d_x = inv_one * scaled - x * (inv_one * inv_one * inv_one * inner)
    tokens_grad = (d_h + d_x).astype(bf16)

    gain_parts = jnp.stack([gain_one_part.reshape(n_dp, block), gain_two_part.reshape(n_dp, block)], 1)
    gain_parts = to_relative(gain_parts, me_dp, n_dp)
    gain_share = reduce_small(gain_parts, me_dp, n_dp, n_t)

    gate_share = jnp.concatenate([s[:, :tile] for s in grads], axis=1)
    up_share = jnp.concatenate([s[:, tile : 2 * tile] for s in grads], axis=1)
    down_share = jnp.concatenate([s[:, 2 * tile :].T for s in grads], axis=0)
    return (
        block_out,
        tokens_grad,
        gain_share[0],
        q_share,
        kv_share[:, :nk],
        kv_share[:, nk:],
        out_share.T,
        gain_share[1],
        gate_share,
        up_share,
        down_share,
    )


def solution(mesh):
    in_specs = (
        P(("dp", "tensor"), None),
        P("dp"),
        P(("dp", "tensor"), None),
        P("dp"),
        P("dp", "tensor"),
        P("dp", "tensor"),
        P("dp", "tensor"),
        P("tensor", "dp"),
        P("dp"),
        P("dp", "tensor"),
        P("dp", "tensor"),
        P("tensor", "dp"),
    )
    out_specs = (
        P(("dp", "tensor"), None),
        P(("dp", "tensor"), None),
        P("dp"),
        P("dp", "tensor"),
        P("dp", "tensor"),
        P("dp", "tensor"),
        P("tensor", "dp"),
        P("dp"),
        P("dp", "tensor"),
        P("dp", "tensor"),
        P("tensor", "dp"),
    )
    fn = functools.partial(local, mesh.shape["dp"], mesh.shape["tensor"])
    return jax.shard_map(fn, mesh=mesh, in_specs=in_specs, out_specs=out_specs, check_vma=False)
```

```python
import functools
import math

import jax
import jax.numpy as jnp
from jax import lax
from jax.experimental import pallas as pl
from jax.experimental.pallas import tpu as pltpu
from jax.sharding import PartitionSpec as P

HEAD_SIZE = 96
HALF = HEAD_SIZE // 2
GAIN_LANES = 128
CHUNKS = 4
MERGED = CHUNKS - 1
CLIMB_AT = 7
CLIMB_STEP = 4
KEY_TILE = 256
NEG = -1e30

eps_norm = 1e-05
rope_base = 100000.0
SCALE = 1.0 / math.sqrt(HEAD_SIZE)
SCALE2 = SCALE * math.log2(math.e)

f32 = jnp.float32
bf16 = jnp.bfloat16
VMEM_LIMIT = 56 * 1024 * 1024


def dot(a, b, dims=((1,), (0,))):
    return lax.dot_general(a, b, (dims, ((), ())), preferred_element_type=f32)


def params(*semantics):
    return pltpu.CompilerParams(dimension_semantics=semantics, vmem_limit_bytes=VMEM_LIMIT)


def cost(flops, nbytes, trans=0):
    return pl.CostEstimate(flops=int(flops), bytes_accessed=int(nbytes), transcendentals=int(trans))


def place(ref, me, grad, col=0):
    count, block = ref.shape[1], ref.shape[2]
    for d in range(count):
        r = me ^ d
        at = (r & 1) * (count // 2) + (r >> 1)
        ref[0, at, :, col : col + grad.shape[1]] = grad[d * block : (d + 1) * block]


def turn(y, cosine, sine, sign):
    parts = []
    for h in range(y.shape[0] // HEAD_SIZE):
        a = y[h * HEAD_SIZE : h * HEAD_SIZE + HALF]
        b = y[h * HEAD_SIZE + HALF : (h + 1) * HEAD_SIZE]
        parts.append(a * cosine - sign * (b * sine))
        parts.append(b * cosine + sign * (a * sine))
    return jnp.concatenate(parts, axis=0)


def qkv_kernel(nq, nk, n1_ref, w_ref, cos_ref, sin_ref, q_ref, kv_ref, n1t_ref):
    @pl.when(pl.program_id(0) == 0)
    def _():
        n1t_ref[...] = n1_ref[...].T

    w = w_ref[0, :, : nq + 2 * nk]
    y = dot(n1_ref[...], w).T
    cosine, sine = cos_ref[...], sin_ref[...]
    q_ref[0] = turn(y[:nq], cosine, sine, 1.0).astype(bf16)
    kv_ref[0] = turn(y[nq : nq + nk], cosine, sine, 1.0).astype(bf16)
    kv_ref[1] = y[nq + nk :].astype(bf16)


def qkv_project(n1, w, cosine, sine, nq, nk):
    rows, width = n1.shape
    zs, _, cols = w.shape
    return pl.pallas_call(
        functools.partial(qkv_kernel, nq, nk),
        grid=(zs,),
        in_specs=[
            pl.BlockSpec((rows, width), lambda z: (0, 0)),
            pl.BlockSpec((1, width, cols), lambda z: (z, 0, 0)),
            pl.BlockSpec((HALF, rows), lambda z: (0, 0)),
            pl.BlockSpec((HALF, rows), lambda z: (0, 0)),
        ],
        out_specs=[
            pl.BlockSpec((1, nq, rows), lambda z: (z, 0, 0)),
            pl.BlockSpec((2, nk, rows), lambda z: (0, z, 0)),
            pl.BlockSpec((width, rows), lambda z: (0, 0)),
        ],
        out_shape=[
            jax.ShapeDtypeStruct((zs, nq, rows), bf16),
            jax.ShapeDtypeStruct((2, zs * nk, rows), bf16),
            jax.ShapeDtypeStruct((width, rows), bf16),
        ],
        compiler_params=params("arbitrary"),
        cost_estimate=cost(2 * rows * width * cols * zs, 2 * zs * width * cols + 8 * rows * width),
        name="qkv_project",
    )(n1, w, cosine, sine)


def out_kernel(att_ref, w_ref, x_ref, h_ref):
    z = pl.program_id(0)

    @pl.when(z == 0)
    def _():
        h_ref[...] = x_ref[...].astype(f32)

    h_ref[...] += dot(att_ref[0].T, w_ref[0], ((1,), (1,)))


def out_project(att, w, x, no, col):
    zs, _, rows = att.shape
    width = x.shape[1]
    return pl.pallas_call(
        out_kernel,
        grid=(zs,),
        in_specs=[
            pl.BlockSpec((1, no, rows), lambda z: (z, 0, 0)),
            pl.BlockSpec((1, width, no), lambda z: (z, 0, col)),
            pl.BlockSpec((rows, width), lambda z: (0, 0)),
        ],
        out_specs=pl.BlockSpec((rows, width), lambda z: (0, 0)),
        out_shape=jax.ShapeDtypeStruct((rows, width), f32),
        compiler_params=params("arbitrary"),
        cost_estimate=cost(2 * rows * width * no * zs, 2 * zs * width * no + 8 * rows * width),
        name="out_project",
    )(att, w, x)


def out_back_kernel(me_ref, dh_ref, att_ref, w_ref, da_ref, grad_ref, dht_ref):
    @pl.when(pl.program_id(0) == 0)
    def _():
        dht_ref[...] = dh_ref[...].T

    w = w_ref[0]
    da_ref[0] = dot(dh_ref[...], w).T.astype(bf16)
    place(grad_ref, me_ref[1], dot(dht_ref[...], att_ref[0].T).astype(bf16))


def out_back(me, dh, att, w, no, col, n_dp):
    zs, _, rows = att.shape
    width = dh.shape[1]
    block = width // n_dp
    return pl.pallas_call(
        out_back_kernel,
        grid_spec=pltpu.PrefetchScalarGridSpec(
            num_scalar_prefetch=1,
            grid=(zs,),
            in_specs=[
                pl.BlockSpec((rows, width), lambda z, m: (0, 0)),
                pl.BlockSpec((1, no, rows), lambda z, m: (z, 0, 0)),
                pl.BlockSpec((1, width, no), lambda z, m: (z, 0, col)),
            ],
            out_specs=[
                pl.BlockSpec((1, no, rows), lambda z, m: (z, 0, 0)),
                pl.BlockSpec((1, n_dp, block, no), lambda z, m: (z ^ m[0], 0, 0, 0)),
            ],
            scratch_shapes=[pltpu.VMEM((width, rows), bf16)],
        ),
        out_shape=[
            jax.ShapeDtypeStruct((zs, no, rows), bf16),
            jax.ShapeDtypeStruct((zs, n_dp, block, no), bf16),
        ],
        compiler_params=params("arbitrary"),
        cost_estimate=cost(4 * rows * width * no * zs, 4 * zs * width * no + 8 * rows * width),
        name="out_back",
    )(me, dh, att, w)


def key_mask(s, key_first, query_first, length, rows, diagonal):
    key = key_first + lax.broadcasted_iota(jnp.int32, (s.shape[0], 1), 0)
    ok = key < length
    if diagonal:
        lane = lax.broadcasted_iota(jnp.int32, s.shape, 1)
        query = query_first + lax.rem(lane, rows)
        ok = ok & (key <= query)
    return jnp.broadcast_to(ok, s.shape)


def mlp_step(tile, me, n2_ref, n2t_ref, g_ref, gt_ref, w_ref, out_ref, dn_ref, grad_ref):
    pair = w_ref[0, :, : 2 * tile]
    wd = w_ref[0, :, 2 * tile :]
    both = dot(n2_ref[...], pair)
    gate, up = both[:, :tile], both[:, tile:]
    d_hidden = dot(g_ref[...], wd)
    sigma = 1.0 / (1.0 + jnp.exp(-gate))
    active = gate * sigma
    hidden = (active * up).astype(bf16)
    d_gate = (d_hidden * up * (sigma * (1.0 + gate * (1.0 - sigma)))).astype(bf16)
    d_up = (d_hidden * active).astype(bf16)
    d_both = jnp.concatenate([d_gate, d_up], axis=1)
    out_ref[...] += dot(hidden, wd, ((1,), (1,)))
    dn_ref[...] += dot(d_both, pair, ((1,), (1,)))
    place(grad_ref, me, dot(n2t_ref[...], d_both).astype(bf16), 0)
    place(grad_ref, me, dot(gt_ref[...], hidden).astype(bf16), 2 * tile)


def mlp_kernel(
    tile, first, me_ref, n2_ref, n2t_ref, g_ref, gt_ref, w_ref, *refs
):
    if first:
        out_ref, dn_ref, grad_ref = refs
    else:
        out_in, dn_in, out_ref, dn_ref, grad_ref = refs
    z = pl.program_id(0)

    @pl.when(z == 0)
    def _():
        if first:
            out_ref[...] = jnp.zeros_like(out_ref)
            dn_ref[...] = jnp.zeros_like(dn_ref)
        else:
            out_ref[...] = out_in[...]
            dn_ref[...] = dn_in[...]

    mlp_step(tile, me_ref[1], n2_ref, n2t_ref, g_ref, gt_ref, w_ref, out_ref, dn_ref, grad_ref)


def mlp(me, n2, n2t, g, gt, w, chunk, tile, carry, n_dp):
    rows, width = n2.shape
    zs = w.shape[0]
    block = width // n_dp
    full = pl.BlockSpec((rows, width), lambda z, m: (0, 0))
    full_t = pl.BlockSpec((width, rows), lambda z, m: (0, 0))
    grad_spec = pl.BlockSpec((1, n_dp, block, 3 * tile), lambda z, m: (z ^ m[0], 0, 0, 0))
    first = carry is None
    in_specs = [
        full,
        full_t,
        full,
        full_t,
        pl.BlockSpec((1, width, 3 * tile), lambda z, m: (z, 0, chunk)),
    ]
    args = [me, n2, n2t, g, gt, w]
    aliases = {}
    if not first:
        in_specs += [full, full]
        aliases = {6: 0, 7: 1}
        args += list(carry)
    return pl.pallas_call(
        functools.partial(mlp_kernel, tile, first),
        grid_spec=pltpu.PrefetchScalarGridSpec(
            num_scalar_prefetch=1,
            grid=(zs,),
            in_specs=in_specs,
            out_specs=[full, full, grad_spec],
        ),
        out_shape=[
            jax.ShapeDtypeStruct((rows, width), f32),
            jax.ShapeDtypeStruct((rows, width), f32),
            jax.ShapeDtypeStruct((zs, n_dp, block, 3 * tile), bf16),
        ],
        input_output_aliases=aliases,
        compiler_params=params("arbitrary"),
        cost_estimate=cost(
            18 * rows * width * tile * zs, 4 * zs * width * 3 * tile + 24 * rows * width
        ),
        name="mlp",
    )(*args)


def pairs(count, mask):
    return [(i, i ^ mask) for i in range(count)]


def bits_of(count):
    return [1 << b for b in range(count.bit_length() - 1)]


def relative_order(count):
    return [r for low in (0, 1) for r in range(count) if (r & 1) == low]


def to_relative(rows_first, me, count):
    block = rows_first.shape[0] // count
    parts = [
        lax.dynamic_slice_in_dim(rows_first, (me ^ r) * block, block, axis=0)
        for r in relative_order(count)
    ]
    return jnp.concatenate(parts, axis=0)


def reduce_small(values, me, n_dp, n_t):
    order = relative_order(n_dp)
    buf = values
    left = n_dp
    buf = buf[: left // 2] + lax.ppermute(buf[left // 2 :], "dp", pairs(n_dp, 1))
    left //= 2
    for bit in [b for b in bits_of(n_dp) if b > 1][::-1]:
        buf = buf[: left // 2] + lax.ppermute(buf[left // 2 :], "dp", pairs(n_dp, bit))
        left //= 2
    buf = buf[0]
    for bit in bits_of(n_t):
        buf = buf + lax.ppermute(buf, "tensor", pairs(n_t, bit))
    return buf


MESH = pl.DeviceIdType.MESH


def log2(n):
    return n.bit_length() - 1


def nearest_first(n_t):
    return [sorted(range(n_t), key=lambda p: (abs(p - z), p)) for z in range(n_t)]


def pick(values, z):
    out = jnp.int32(values[0])
    for i in range(1, len(values)):
        out = jnp.where(z == i, jnp.int32(values[i]), out)
    return out


def neighbours(n_dp, n_t, me, z):
    barrier = pltpu.get_barrier_semaphore()
    masks = [1 << b for b in range(log2(n_dp))]
    for mask in masks:
        pl.semaphore_signal(barrier, 1, device_id=(me ^ mask, z), device_id_type=MESH)

    @pl.when(z > 0)
    def _():
        pl.semaphore_signal(barrier, 1, device_id=(me, z - 1), device_id_type=MESH)

    @pl.when(z < n_t - 1)
    def _():
        pl.semaphore_signal(barrier, 1, device_id=(me, z + 1), device_id_type=MESH)

    count = len(masks) + (z > 0).astype(jnp.int32) + (z < n_t - 1).astype(jnp.int32)
    pl.semaphore_wait(barrier, count)


class Gather:
    def __init__(self, n_dp, n_t, me, z, index, shard, whole, sems, lanes=None):
        self.n_dp, self.n_t, self.me, self.z = n_dp, n_t, me, z
        self.index, self.shard, self.whole, self.lanes = index, shard, whole, lanes
        self.own, self.z_send, self.z_recv, self.x_send, self.x_recv = sems
        self.bits = log2(n_dp) - 1

    def place_of(self, piece, d):
        if self.lanes is None:
            return self.whole.at[piece, d]
        return self.whole.at[piece, d, :, self.lanes]

    def local(self):
        return pltpu.make_async_copy(
            self.shard, self.place_of(self.z, self.me), self.own.at[self.index]
        )

    def hop(self, piece, direction, hops):
        source = self.place_of(piece, self.me)
        step = 1 - 2 * direction
        return pltpu.make_async_remote_copy(
            source,
            source,
            self.z_send.at[self.index, direction, hops],
            self.z_recv.at[self.index, direction, hops],
            device_id=(self.me, jnp.clip(self.z + step, 0, self.n_t - 1)),
            device_id_type=MESH,
        )

    def send_own(self):
        local = self.local()
        local.start()
        local.wait()

        @pl.when(self.z < self.n_t - 1)
        def _():
            self.hop(self.z, 0, 0).start()

        @pl.when(self.z > 0)
        def _():
            self.hop(self.z, 1, 0).start()

    def order(self, k):
        return pick([row[k] for row in nearest_first(self.n_t)], self.z)

    def arrive(self, k):
        if k == 0:
            return
        piece = self.order(k)
        direction = (piece > self.z).astype(jnp.int32)
        hops = jnp.abs(piece - self.z)
        self.hop(piece, direction, hops - 1).wait_recv()
        on = jnp.where(direction == 0, self.z < self.n_t - 1, self.z > 0)

        @pl.when(on)
        def _():
            self.hop(piece, direction, hops).start()

    def doubling(self, k, stage, i, incoming=False):
        piece = self.order(k)
        odd = (piece & 1) == 1
        bit = jnp.where(odd, 1 << (self.bits - stage), 2 << stage)
        shift = jnp.where(odd, self.bits - stage + 1, 1)
        partner = self.me ^ bit
        origin = partner if incoming else self.me
        held = self.place_of(piece, origin ^ (i << shift))
        at = (1 << stage) - 1 + i
        return pltpu.make_async_remote_copy(
            held,
            held,
            self.x_send.at[self.index, k, at],
            self.x_recv.at[self.index, k, at],
            device_id=(partner, self.z),
            device_id_type=MESH,
        )

    def core(self, k, i, incoming=False):
        piece = self.order(k)
        partner = self.me ^ 1
        origin = partner if incoming else self.me
        held = self.place_of(piece, origin ^ (i << 1))
        at = (1 << self.bits) - 1 + i
        return pltpu.make_async_remote_copy(
            held,
            held,
            self.x_send.at[self.index, k, at],
            self.x_recv.at[self.index, k, at],
            device_id=(partner, self.z),
            device_id_type=MESH,
        )

    def each(self, count, body):
        if count <= 4:
            for i in range(count):
                body(i)
        else:
            lax.fori_loop(0, count, lambda i, _: (body(i), 0)[1], 0)

    def spread(self, k, stage):
        if stage > 0:
            self.each(1 << (stage - 1), lambda i: self.doubling(k, stage - 1, i, True).wait_recv())
        if stage < self.bits:
            self.each(1 << stage, lambda i: self.doubling(k, stage, i).start())
        else:
            self.each(1 << self.bits, lambda i: self.core(k, i).start())

    def finish(self, k):
        self.each(1 << self.bits, lambda i: self.core(k, i, True).wait_recv())
        for stage in range(self.bits):
            self.each(1 << stage, lambda i: self.doubling(k, stage, i).wait_send())
        self.each(1 << self.bits, lambda i: self.core(k, i).wait_send())
        piece = self.order(k)
        hops = jnp.abs(piece - self.z)
        if k == 0:

            @pl.when(self.z < self.n_t - 1)
            def _():
                self.hop(piece, 0, 0).wait_send()

            @pl.when(self.z > 0)
            def _():
                self.hop(piece, 1, 0).wait_send()
        else:
            direction = (piece > self.z).astype(jnp.int32)
            on = jnp.where(direction == 0, self.z < self.n_t - 1, self.z > 0)

            @pl.when(on)
            def _():
                self.hop(piece, direction, hops).wait_send()


class Climb:
    def __init__(self, n_t, me, z, own, kept, sems):
        self.n_t, self.me, self.z, self.own, self.kept = n_t, me, z, own, kept
        self.send, self.recv = sems

    def hop(self, r):
        source = self.own if r == 0 else self.kept[r - 1]
        return pltpu.make_async_remote_copy(
            source,
            self.kept[r],
            self.send.at[r],
            self.recv.at[r],
            device_id=(self.me, jnp.minimum(self.z + 1, self.n_t - 1)),
            device_id_type=MESH,
        )

    def start(self, r):
        @pl.when((self.z >= r) & (self.z < self.n_t - 1))
        def _():
            self.hop(r).start()

    def arrive(self, r):
        @pl.when(self.z >= r)
        def _():
            self.hop(r - 1).wait_recv()

    def finish(self, r):
        @pl.when((self.z >= r) & (self.z < self.n_t - 1))
        def _():
            self.hop(r).wait_send()


def attend_part(r, z, length, q_ref, kv_ref, m_ref, l_ref, acc_ref):
    rows = q_ref.shape[1]
    groups = m_ref.shape[0]
    group = q_ref.shape[0] // (groups * HEAD_SIZE)
    first = z * rows

    @pl.when(z >= r)
    def _():
        def body(g, _):
            base = pl.multiple_of(g * (group * HEAD_SIZE), 32)
            at = pl.multiple_of(g * HEAD_SIZE, 32)
            q = jnp.concatenate(
                [q_ref[pl.ds(base + a * HEAD_SIZE, HEAD_SIZE), :] for a in range(group)], axis=1
            )
            if r == 0:
                m = jnp.full((1, group * rows), NEG, f32)
                total = jnp.zeros((1, group * rows), f32)
                acc = jnp.zeros((HEAD_SIZE, group * rows), f32)
            else:
                m, total, acc = m_ref[g], l_ref[g], acc_ref[g]
            for j in range(rows // KEY_TILE):
                part = slice(j * KEY_TILE, (j + 1) * KEY_TILE)
                k = kv_ref[0, pl.ds(at, HEAD_SIZE), part]
                v = kv_ref[1, pl.ds(at, HEAD_SIZE), part]
                s = dot(k, q, ((0,), (0,)))
                ok = key_mask(s, first - r * rows + j * KEY_TILE, first, length, rows, r == 0)
                s = jnp.where(ok, s, NEG)
                new = jnp.maximum(m, jnp.max(s, axis=0, keepdims=True))
                shrink = jnp.exp2((m - new) * SCALE2)
                p = jnp.exp2(s * SCALE2 - new * SCALE2)
                total = total * shrink + jnp.sum(p, axis=0, keepdims=True)
                acc = acc * shrink + dot(v, p.astype(bf16))
                m = new
            m_ref[g], l_ref[g], acc_ref[g] = m, total, acc
            return 0

        lax.fori_loop(0, groups, body, 0)


def attend_end(q_shape, m_ref, l_ref, acc_ref, att_ref):
    groups = m_ref.shape[0]
    rows = q_shape[1]
    group = q_shape[0] // (groups * HEAD_SIZE)

    def body(g, _):
        out = acc_ref[g] / l_ref[g]
        for a in range(group):
            own = pl.ds(pl.multiple_of((g * group + a) * HEAD_SIZE, 32), HEAD_SIZE)
            att_ref[own, :] = out[:, a * rows : (a + 1) * rows].astype(bf16)
        m_ref[g] = m_ref[g] * SCALE2 + jnp.log2(l_ref[g])
        return 0

    lax.fori_loop(0, groups, body, 0)


def gather_kernel(n_dp, n_t, count, merged, climbs, *refs):
    refs = list(refs)

    def take(k):
        out = refs[:k]
        del refs[:k]
        return out

    shards = take(count)
    if climbs:
        own, q_ref, length_ref = take(3)
    wholes = [(ref, None) for ref in take(count - merged)]
    if merged:
        (ref,) = take(1)
        wide = shards[-1].shape[1]
        wholes += [(ref, slice(i * wide, (i + 1) * wide)) for i in range(merged)]
    if climbs:
        kept = take(n_t - 1)
        att_ref, lse_ref = take(2)
    sems = take(5)
    me, z = lax.axis_index("dp"), lax.axis_index("tensor")
    neighbours(n_dp, n_t, me, z)
    works = [
        Gather(n_dp, n_t, me, z, c, shards[c], wholes[c][0], sems, wholes[c][1])
        for c in range(count)
    ]
    if climbs:
        climb_sems = take(2)
        l_ref, acc_ref, kv_ref, kv_sem = take(4)
        climb = Climb(n_t, me, z, own, kept, climb_sems)
        climb.start(0)
        length = length_ref[0]

    def attend_step(r):
        if r > 0:
            climb.arrive(r)
            if r < n_t - 1:
                climb.start(r)

        @pl.when(z >= r)
        def _():
            fetch = pltpu.make_async_copy(own if r == 0 else kept[r - 1], kv_ref, kv_sem)
            fetch.start()
            fetch.wait()

        attend_part(r, z, length, q_ref, kv_ref, lse_ref, l_ref, acc_ref)

    stages = log2(n_dp)
    works[0].send_own()
    total = count * n_t
    todo = list(range(n_t)) if climbs else []
    for n in range(total + 2 * (stages - 1)):
        if n < total:
            c, k = divmod(n, n_t)
            works[c].arrive(k)
            works[c].spread(k, 0)
            if k == 0 and c + 1 < count:
                works[c + 1].send_own()
        for stage in range(1, stages):
            at = n - 2 * stage
            if 0 <= at < total:
                works[at // n_t].spread(at % n_t, stage)
        if todo and (n == 2 if todo[0] == 0 else n == CLIMB_AT + CLIMB_STEP * (todo[0] - 1)):
            attend_step(todo.pop(0))
    for r in todo:
        attend_step(r)
    if climbs:
        attend_end(q_ref.shape, lse_ref, l_ref, acc_ref, att_ref)
    for c in range(count):
        for k in range(n_t):
            works[c].finish(k)
    if climbs:
        for r in range(n_t - 1):
            climb.finish(r)


def gather(shards, n_dp, n_t, collective_id, attention=None, merged=0):
    count = len(shards)
    shapes = [
        jax.ShapeDtypeStruct((n_t, n_dp) + s.shape, s.dtype) for s in shards[: count - merged]
    ]
    if merged:
        block, wide = shards[-1].shape
        shapes.append(jax.ShapeDtypeStruct((n_t, n_dp, block, merged * wide), bf16))
    args = list(shards)
    anywhere = pl.BlockSpec(memory_space=pl.ANY)
    vmem = pl.BlockSpec(memory_space=pltpu.VMEM)
    in_specs = [anywhere] * count
    out_specs = [anywhere] * len(shapes)
    scratch = [
        pltpu.SemaphoreType.DMA((count,)),
        pltpu.SemaphoreType.DMA((count, 2, n_t)),
        pltpu.SemaphoreType.DMA((count, 2, n_t)),
        pltpu.SemaphoreType.DMA((count, n_t, n_dp - 1)),
        pltpu.SemaphoreType.DMA((count, n_t, n_dp - 1)),
    ]
    if attention is not None:
        kv, q, length = attention
        rows = q.shape[1]
        groups = kv.shape[1] // HEAD_SIZE
        lanes = q.shape[0] // (groups * HEAD_SIZE) * rows
        args += [kv, q, length.reshape(1)]
        in_specs += [anywhere, vmem, pl.BlockSpec(memory_space=pltpu.SMEM)]
        shapes += [jax.ShapeDtypeStruct(kv.shape, kv.dtype)] * (n_t - 1)
        shapes += [
            jax.ShapeDtypeStruct(q.shape, bf16),
            jax.ShapeDtypeStruct((groups, 1, lanes), f32),
        ]
        out_specs += [anywhere] * (n_t - 1) + [vmem, vmem]
        scratch += [pltpu.SemaphoreType.DMA((n_t,))] * 2
        scratch += [
            pltpu.VMEM((groups, 1, lanes), f32),
            pltpu.VMEM((groups, HEAD_SIZE, lanes), f32),
            pltpu.VMEM(kv.shape, bf16),
            pltpu.SemaphoreType.DMA,
        ]
    return pl.pallas_call(
        functools.partial(gather_kernel, n_dp, n_t, count, merged, attention is not None),
        in_specs=in_specs,
        out_specs=out_specs,
        out_shape=shapes,
        scratch_shapes=scratch,
        compiler_params=pltpu.CompilerParams(
            collective_id=collective_id, has_side_effects=True, vmem_limit_bytes=VMEM_LIMIT
        ),
        name="gather_weights",
    )(*args)


def mlp_gather_kernel(
    n_dp, n_t, tile, n2_ref, g_ref, w_ref, shard_ref,
    out_ref, dn_ref, n2t_ref, gt_ref, grad_ref, whole_ref, *sems
):
    me, z = lax.axis_index("dp"), lax.axis_index("tensor")
    step = pl.program_id(0) * pl.num_programs(1) + pl.program_id(1)
    steps = w_ref.shape[0] * MERGED * n_t
    work = Gather(n_dp, n_t, me, z, 0, shard_ref, whole_ref, sems)
    stages = log2(n_dp)

    @pl.when(step == 0)
    def _():
        neighbours(n_dp, n_t, me, z)
        work.send_own()
        n2t_ref[...] = n2_ref[...].T
        gt_ref[...] = g_ref[...].T
        out_ref[...] = jnp.zeros_like(out_ref)
        dn_ref[...] = jnp.zeros_like(dn_ref)

    for n in range(n_t + 2 * (stages - 1)):

        @pl.when(step == min(n, steps - 1))
        def _():
            if n < n_t:
                work.arrive(n)
                work.spread(n, 0)
            for stage in range(1, stages):
                at = n - 2 * stage
                if 0 <= at < n_t:
                    work.spread(at, stage)

    mlp_step(
        tile, me, n2_ref, n2t_ref, g_ref, gt_ref, w_ref, out_ref, dn_ref, grad_ref.at[0]
    )

    @pl.when(step == steps - 1)
    def _():
        for k in range(n_t):
            work.finish(k)


def mlp_gather(n2, g, w, shard, tile, n_dp, n_t, collective_id):
    rows, width = n2.shape
    block = width // n_dp
    full = pl.BlockSpec((rows, width), lambda c, i: (0, 0))
    full_t = pl.BlockSpec((width, rows), lambda c, i: (0, 0))
    anywhere = pl.BlockSpec(memory_space=pl.ANY)
    cols = 3 * tile
    return pl.pallas_call(
        functools.partial(mlp_gather_kernel, n_dp, n_t, tile),
        grid=(MERGED, n_t),
        in_specs=[
            full,
            full,
            pl.BlockSpec((1, width, cols), lambda c, i: (i, 0, c)),
            anywhere,
        ],
        out_specs=[
            full,
            full,
            full_t,
            full_t,
            pl.BlockSpec(
                (1, 1, n_dp, block, cols),
                lambda c, i: (c, i ^ lax.axis_index("tensor"), 0, 0, 0),
            ),
            anywhere,
        ],
        out_shape=[
            jax.ShapeDtypeStruct((rows, width), f32),
            jax.ShapeDtypeStruct((rows, width), f32),
            jax.ShapeDtypeStruct((width, rows), bf16),
            jax.ShapeDtypeStruct((width, rows), bf16),
            jax.ShapeDtypeStruct((MERGED, n_t, n_dp, block, cols), bf16),
            jax.ShapeDtypeStruct((n_t, n_dp, block, cols), bf16),
        ],
        scratch_shapes=[
            pltpu.SemaphoreType.DMA((1,)),
            pltpu.SemaphoreType.DMA((1, 2, n_t)),
            pltpu.SemaphoreType.DMA((1, 2, n_t)),
            pltpu.SemaphoreType.DMA((1, n_t, n_dp - 1)),
            pltpu.SemaphoreType.DMA((1, n_t, n_dp - 1)),
        ],
        compiler_params=pltpu.CompilerParams(
            dimension_semantics=("arbitrary", "arbitrary"),
            collective_id=collective_id,
            has_side_effects=True,
            vmem_limit_bytes=VMEM_LIMIT,
        ),
        name="mlp_gather",
    )(n2, g, w, shard)


def greet_all(n_dp, n_t, me, z):
    barrier = pltpu.get_barrier_semaphore()
    masks = [1 << b for b in range(log2(n_dp))]
    for mask in masks:
        pl.semaphore_signal(barrier, 1, device_id=(me ^ mask, z), device_id_type=MESH)
    for other in range(1, n_t):
        pl.semaphore_signal(barrier, 1, device_id=(me, z ^ other), device_id_type=MESH)
    pl.semaphore_wait(barrier, len(masks) + n_t - 1)


def count_of(shape):
    return math.prod(shape)


def add_blocks(target, source, dtype=bf16):
    lead = target.shape[:-2]

    def body(i, _):
        at = []
        for extent in lead[::-1]:
            at.append(lax.rem(i, extent))
            i = i // extent
        at = tuple(at[::-1])
        target[at] = (target[at].astype(f32) + source[at].astype(f32)).astype(dtype)
        return 0

    lax.fori_loop(0, count_of(lead), body, 0)


class Scatter:
    def __init__(self, n_dp, n_t, me, z, index, grad, land, out, held, first, cols, tile, landings, sems):
        self.n_t, self.me, self.z, self.index = n_t, me, z, index
        ref, lead = grad
        self.keep, self.send = ref.at[lead + (slice(None), 0)], ref.at[lead + (slice(None), 1)]
        self.land, self.out, self.held = land, out, held
        self.tile, self.landings, self.sems = tile, landings, sems
        self.bits, self.t_bits = log2(n_dp) - 1, log2(n_t)
        self.stages = 2 + self.bits + self.t_bits
        self.cols, self.lanes = cols, slice(first, first + cols)
        self.lead = (n_t,) + (2,) * self.bits

    def remote(self, source, target, slot, dp, z):
        send, recv = self.sems[0], self.sems[1]
        return pltpu.make_async_remote_copy(
            source,
            target,
            send.at[self.index, slot],
            recv.at[self.index, slot],
            device_id=(dp, z),
            device_id_type=MESH,
        )

    def at(self, index=()):
        return index + (slice(None),) * (len(self.lead) - len(index) + 1) + (self.lanes,)

    def load(self):
        return pltpu.make_async_copy(
            self.keep, self.held.at[self.at()], self.sems[2].at[self.index]
        )

    def core(self):
        return self.remote(self.send, self.land, 0, self.me ^ 1, self.z)

    def part(self, half, stage, bit):
        rest = (slice(None),) * (self.bits - 1 - stage)
        done = (0,) * stage
        if half == 0:
            return self.held.at[self.at((slice(0, self.n_t // 2),) + rest + (bit,) + done)]
        return self.held.at[self.at((slice(self.n_t // 2, self.n_t),) + done + (bit,) + rest)]

    def landing(self, which):
        ref = self.landings[which]
        at = (self.index % 2,) + (slice(None),) * (len(ref.shape) - 2) + (slice(0, self.cols),)
        return ref.at[at]

    def plane(self, half, stage):
        mask = 2 << stage if half == 0 else 1 << (self.bits - stage)
        return self.remote(
            self.part(half, stage, 1),
            self.landing(2 * stage + half),
            1 + 2 * stage + half,
            self.me ^ mask,
            self.z,
        )

    def column(self, stage, first, count):
        return self.held.at[self.at((slice(first, first + count),) + (0,) * self.bits)]

    def along(self, stage):
        count = self.n_t >> (stage + 1)
        return self.remote(
            self.column(stage, count, count),
            self.landing(2 * self.bits + stage),
            1 + 2 * self.bits + stage,
            self.me,
            self.z ^ count,
        )

    def start(self, stage):
        if stage < self.bits:
            self.plane(0, stage).start()
            self.plane(1, stage).start()
        elif stage < self.bits + self.t_bits:
            self.along(stage - self.bits).start()

    def event(self, number):
        if number == 0:
            self.core().start()
            self.load().start()
        elif number == 1:
            self.load().wait()
            self.core().wait_recv()
            self.add_land()
            self.start(0)
        elif number <= 1 + self.bits:
            stage = number - 2
            for half in (0, 1):
                self.plane(half, stage).wait_recv()
                add_blocks(self.part(half, stage, 0), self.landing(2 * stage + half))
            self.start(stage + 1)
        else:
            stage = number - 2 - self.bits
            self.along(stage).wait_recv()
            count = self.n_t >> (stage + 1)
            if stage < self.t_bits - 1:
                add_blocks(
                    self.column(stage, 0, count), self.landing(2 * self.bits + stage)
                )
                self.start(number - 1)
            else:
                mine = self.held[self.at((0,) * (1 + self.bits))].astype(f32)
                got = self.landing(2 * self.bits + stage)[0].astype(f32)
                self.out[...] = mine + got

    def add_land(self):
        lead = self.lead

        def at_of(i):
            at = []
            for extent in lead[::-1]:
                at.append(lax.rem(i, extent))
                i = i // extent
            return tuple(at[::-1])

        def fetch(i):
            return pltpu.make_async_copy(
                self.land.at[at_of(i)],
                self.tile.at[lax.rem(i, 2), :, pl.ds(0, self.cols)],
                self.sems[3].at[lax.rem(i, 2)],
            )

        total = count_of(lead)
        fetch(0).start()

        def body(i, _):
            @pl.when(i + 1 < total)
            def _():
                fetch(i + 1).start()

            fetch(i).wait()
            at = self.at(at_of(i))
            got = self.tile[lax.rem(i, 2), :, pl.ds(0, self.cols)].astype(f32)
            self.held[at] = (self.held[at].astype(f32) + got).astype(bf16)
            return 0

        lax.fori_loop(0, total, body, 0)

    def finish(self):
        self.core().wait_send()
        for stage in range(self.bits):
            for half in (0, 1):
                self.plane(half, stage).wait_send()
        for stage in range(self.t_bits):
            self.along(stage).wait_send()


class Descend:
    def __init__(self, n_t, me, z, sums, landed, sems):
        self.n_t, self.me, self.z = n_t, me, z
        self.sums, self.landed, self.send, self.recv = sums, landed, sems[0], sems[1]

    def hop(self, r):
        return pltpu.make_async_remote_copy(
            self.sums[r],
            self.landed[r - 1],
            self.send.at[r],
            self.recv.at[r],
            device_id=(self.me, jnp.maximum(self.z - 1, 0)),
            device_id_type=MESH,
        )

    def start(self, r):
        @pl.when(self.z >= r)
        def _():
            self.hop(r).start()

    def finish(self, r):
        @pl.when(self.z >= r)
        def _():
            self.hop(r).wait_send()


def attention_part(r, group, n_t, z, length, q_ref, do_ref, lse_ref, delta_ref, kv_ref, dq_ref, sum_ref):
    rows = q_ref.shape[1]
    groups = lse_ref.shape[0]
    per = group * HEAD_SIZE
    first = z * rows
    active = z >= r
    fresh = r == n_t - 1

    def beside(ref, base):
        return jnp.concatenate(
            [ref[pl.ds(base + a * HEAD_SIZE, HEAD_SIZE), :] for a in range(group)], axis=1
        )

    @pl.when(active)
    def _():
        def body(g, _):
            base = pl.multiple_of(g * per, 32)
            at = pl.multiple_of(g * HEAD_SIZE, 32)
            q = beside(q_ref, base)
            do = beside(do_ref, base)
            delta, lse = delta_ref[g], lse_ref[g]
            dq = jnp.zeros(q.shape, f32)
            for j in range(rows // KEY_TILE):
                part = slice(j * KEY_TILE, (j + 1) * KEY_TILE)
                k, v = kv_ref[0, pl.ds(at, HEAD_SIZE), part], kv_ref[1, pl.ds(at, HEAD_SIZE), part]
                s = dot(k, q, ((0,), (0,)))
                ok = key_mask(s, first - r * rows + j * KEY_TILE, first, length, rows, r == 0)
                p = jnp.where(ok, jnp.exp2(s * SCALE2 - lse), 0.0)
                dp = dot(v, do, ((0,), (0,)))
                ds = (p * (dp - delta)).astype(bf16)
                dv = dot(do, p.astype(bf16), ((1,), (1,)))
                dk = dot(q, ds, ((1,), (1,))) * SCALE
                sum_ref[0, pl.ds(at, HEAD_SIZE), part] = dk.astype(bf16)
                sum_ref[1, pl.ds(at, HEAD_SIZE), part] = dv.astype(bf16)
                dq += dot(k, ds)
            for a in range(group):
                own = pl.ds(base + a * HEAD_SIZE, HEAD_SIZE)
                term = dq[:, a * rows : (a + 1) * rows] * SCALE
                if fresh:
                    dq_ref[own, :] = term
                else:
                    dq_ref[own, :] += term
            return 0

        lax.fori_loop(0, groups, body, 0)

    @pl.when(jnp.logical_not(active))
    def _():
        sum_ref[...] = jnp.zeros_like(sum_ref)
        if fresh:
            dq_ref[...] = jnp.zeros_like(dq_ref)


def back_part(
    n_dp, n_t, me, z, nq, nk, dq_ref, dkv_ref, cos_ref, sin_ref, n1t_ref, w_hbm, wq_ref, wkv_ref,
    dn_ref, gbufs, parts, sems
):
    width = n1t_ref.shape[0]
    block = width // n_dp
    bits = log2(n_dp) - 1
    step = width // 4
    cosine, sine = cos_ref[...], sin_ref[...]

    def body(i, _):
        copies = [
            pltpu.make_async_copy(w_hbm.at[i, :, 0:nq], wq_ref.at[:, 0:nq], sems.at[0]),
            pltpu.make_async_copy(w_hbm.at[i, :, nq : nq + 2 * nk], wkv_ref, sems.at[1]),
        ]
        for copy in copies:
            copy.start()
        q_rows = pl.ds(pl.multiple_of(i * nq, 32), nq)
        k_rows = pl.ds(pl.multiple_of(i * nk, 32), nk)
        dq = turn(dq_ref[q_rows, :], cosine, sine, -1.0).astype(bf16).T
        dk = turn(dkv_ref[0, k_rows, :].astype(f32), cosine, sine, -1.0).astype(bf16)
        dkv = jnp.concatenate([dk, dkv_ref[1, k_rows, :]], axis=0).T
        for copy in copies:
            copy.wait()
        for c in range(4):
            part = slice(c * step, (c + 1) * step)
            dn_ref[:, part] += dot(dq, wq_ref[part, 0:nq], ((1,), (1,))) + dot(
                dkv, wkv_ref[part, :], ((1,), (1,))
            )
            for d, gbuf in ((dq, gbufs[0]), (dkv, gbufs[1])):
                grad = dot(n1t_ref[part, :], d).astype(bf16)
                for b in range(step // block):
                    r = me ^ (c * (step // block) + b)
                    at = (r & 1,) + tuple((r >> bit) & 1 for bit in range(bits, 0, -1))
                    gbuf[at] = grad[b * block : (b + 1) * block]
        stores = [
            pltpu.make_async_copy(gbufs[k], parts[k].at[i ^ z], sems.at[2 + k]) for k in (0, 1)
        ]
        for store in stores:
            store.start()
        for store in stores:
            store.wait()
        return 0

    dn_ref[...] = jnp.zeros_like(dn_ref)
    lax.fori_loop(0, n_t, body, 0)


def scatter_kernel(n_dp, n_t, stacked, cols, nq, nk, *refs):
    refs = list(refs)

    def take(k):
        out = refs[:k]
        del refs[:k]
        return out

    grads = []
    for ref, depth in zip(take(len(stacked)), stacked):
        grads += [(ref, (c,)) for c in range(depth)] if depth else [(ref, ())]
    early = len(grads)
    count = early + 2
    sc_ref, q_hbm, do_hbm, lse_ref, delta_ref = take(5)
    kvs = take(n_t)
    cos_ref, sin_ref, n1t_hbm, w_hbm = take(4)
    lands, outs = take(count), take(count)
    dn_ref, q_part, kv_part = take(3)
    grads += [(q_part, ()), (kv_part, ())]
    helds = take(early)
    (tile,) = take(1)
    landings = take(2 * (log2(n_dp) - 1) + log2(n_t))
    sems = take(4)
    dq_ref, dkv_ref, q_ref, do_ref, kv_ref, wkv_ref, gbuf_q, gbuf_kv, own_sems = take(9)
    sums, landed = take(n_t - 1), take(n_t - 1)
    chain_sems = take(2)
    me, z = lax.axis_index("dp"), lax.axis_index("tensor")
    greet_all(n_dp, n_t, me, z)
    places = [(held, 0) for held in helds] + [(helds[0], 0), (helds[0], cols[early])]
    works = [
        Scatter(
            n_dp, n_t, me, z, c, grads[c], lands[c], outs[c], *places[c], cols[c], tile, landings, sems
        )
        for c in range(count)
    ]
    stages = works[0].stages

    shift = max(0, stages - 1 - early)
    turns = [c if c < early else c + shift for c in range(count)]

    def tick(k):
        for number in range(stages - 1, 0, -1):
            if k - (number - 1) in turns:
                works[turns.index(k - (number - 1))].event(number)
        if k + 2 < early:
            works[k + 2].event(0)

    works[0].event(0)
    works[1].event(0)
    loads = [
        pltpu.make_async_copy(q_hbm, q_ref, own_sems.at[0]),
        pltpu.make_async_copy(do_hbm, do_ref, own_sems.at[1]),
    ]
    for load in loads:
        load.start()
    for load in loads:
        load.wait()
    ticks = list(range(count + shift + stages - 2))
    length = sc_ref[1]
    descend = Descend(n_t, me, z, [dkv_ref] + sums, landed, chain_sems)
    for r in range(n_t - 1, -1, -1):
        target = dkv_ref if r == 0 else sums[r - 1]
        fetch = pltpu.make_async_copy(kvs[r], kv_ref, own_sems.at[2])
        fetch.start()
        fetch.wait()
        attention_part(
            r, nq // nk, n_t, z, length, q_ref, do_ref, lse_ref, delta_ref, kv_ref, dq_ref, target
        )
        if r < n_t - 1:
            @pl.when((z + 1 < n_t) & (z >= r))
            def _():
                descend.hop(r + 1).wait_recv()
                add_blocks(target, landed[r])

        if r > 0:
            descend.start(r)
        tick(ticks.pop(0))
    fetch = pltpu.make_async_copy(n1t_hbm, do_ref, own_sems.at[3])
    fetch.start()
    fetch.wait()
    back_part(
        n_dp, n_t, me, z, nq, nk, dq_ref, dkv_ref, cos_ref, sin_ref, do_ref, w_hbm, q_ref, wkv_ref,
        dn_ref, (gbuf_q, gbuf_kv), (q_part, kv_part), own_sems
    )
    while ticks[0] < stages - 1:
        tick(ticks.pop(0))
    works[0].finish()
    works[early].event(0)
    works[early + 1].event(0)
    for k in ticks:
        tick(k)
    for work in works[1:]:
        work.finish()
    for r in range(1, n_t):
        descend.finish(r)


def scatter(grads, n_dp, n_t, collective_id, attention, back):
    bits = log2(n_dp) - 1
    block = grads[0].shape[-2]
    widest = max(k.shape[-1] for k in grads)
    stacked = [k.shape[0] if k.ndim == 5 else 0 for k in grads]
    sc, q, do, lse, delta, kvs = attention
    cosine, sine, n1t, w, nq, nk = back
    cols = []
    for k, depth in zip(grads, stacked):
        cols += [k.shape[-1]] * max(depth, 1)
    early = len(cols)
    cols += [nq, 2 * nk]
    shapes = [(n_t,) + (2,) * bits + (block, c) for c in cols]
    args = [
        k.reshape(k.shape[: k.ndim - 3] + (2,) * (bits + 1) + k.shape[-2:]) for k in grads
    ]
    anywhere = pl.BlockSpec(memory_space=pl.ANY)
    vmem = pl.BlockSpec(memory_space=pltpu.VMEM)
    smem = pl.BlockSpec(memory_space=pltpu.SMEM)
    in_specs = [anywhere] * len(args) + [smem, anywhere, anywhere, vmem, vmem] + [anywhere] * n_t
    in_specs += [vmem, vmem, anywhere, anywhere]
    args += [sc, q, do, lse, delta] + list(kvs) + [cosine, sine, n1t, w]
    wide = [(2,) * (bits + 1) + (block, c) for c in cols[early:]]
    out_shape = [jax.ShapeDtypeStruct(s, bf16) for s in shapes] + [
        jax.ShapeDtypeStruct((block, c), f32) for c in cols
    ]
    out_shape.append(jax.ShapeDtypeStruct((n1t.shape[1], n1t.shape[0]), f32))
    out_shape += [jax.ShapeDtypeStruct((n_t,) + s, bf16) for s in wide]
    out_specs = [anywhere] * len(cols) + [vmem] * (len(cols) + 1) + [anywhere] * 2
    scratch = [pltpu.VMEM(s, bf16) for s in shapes[:early]]
    scratch.append(pltpu.VMEM((2, block, widest), bf16))
    for stage in range(bits):
        for _ in (0, 1):
            scratch.append(
                pltpu.VMEM((2, n_t // 2) + (2,) * (bits - 1 - stage) + (block, widest), bf16)
            )
    for stage in range(log2(n_t)):
        scratch.append(pltpu.VMEM((2, n_t >> (stage + 1), block, widest), bf16))
    copies = 1 + 2 * bits + log2(n_t)
    scratch += [
        pltpu.SemaphoreType.DMA((len(cols), copies)),
        pltpu.SemaphoreType.DMA((len(cols), copies)),
        pltpu.SemaphoreType.DMA((len(cols),)),
        pltpu.SemaphoreType.DMA((2,)),
        pltpu.VMEM(q.shape, f32),
        pltpu.VMEM(kvs[0].shape, bf16),
        pltpu.VMEM(q.shape, bf16),
        pltpu.VMEM(do.shape, bf16),
        pltpu.VMEM(kvs[0].shape, bf16),
        pltpu.VMEM((n1t.shape[0], 2 * nk), bf16),
        pltpu.VMEM(wide[0], bf16),
        pltpu.VMEM(wide[1], bf16),
        pltpu.SemaphoreType.DMA((4,)),
    ]
    scratch += [pltpu.VMEM(kvs[0].shape, bf16)] * (2 * (n_t - 1))
    scratch += [pltpu.SemaphoreType.DMA((n_t,))] * 2
    outs = pl.pallas_call(
        functools.partial(scatter_kernel, n_dp, n_t, stacked, cols, nq, nk),
        in_specs=in_specs,
        out_specs=out_specs,
        out_shape=out_shape,
        scratch_shapes=scratch,
        compiler_params=pltpu.CompilerParams(
            collective_id=collective_id, has_side_effects=True, vmem_limit_bytes=63 * 1024 * 1024
        ),
        name="scatter_grads",
    )(*args)
    return outs[len(cols) : 2 * len(cols) + 1]


def local(
    n_dp,
    n_t,
    tokens,
    lengths,
    cotangent,
    attn_gain,
    query_weight,
    key_matrix,
    value_matrix,
    out_weight,
    mlp_gain,
    gate_weight,
    up_weight,
    down_weight,
):
    rows, width = tokens.shape
    block = query_weight.shape[0]
    nq, nk = query_weight.shape[1], key_matrix.shape[1]
    no = out_weight.shape[0]
    units = gate_weight.shape[1]
    tile = units // CHUNKS
    me_dp = lax.axis_index("dp")
    me_t = lax.axis_index("tensor")
    length = lengths[0]
    me = jnp.stack([me_t, me_dp]).astype(jnp.int32)
    sc = jnp.stack([me_t.astype(jnp.int32), length])

    gains = jnp.stack([attn_gain, mlp_gain], axis=1)
    gains = jnp.pad(gains, ((0, 0), (0, GAIN_LANES - 2)))
    shard_qkv = jnp.concatenate([query_weight, key_matrix, value_matrix, gains], axis=1)
    down_t = down_weight.T
    shard_mlp = []
    for c in range(CHUNKS):
        cols = slice(c * tile, (c + 1) * tile)
        shard_mlp.append(
            jnp.concatenate([gate_weight[:, cols], up_weight[:, cols], down_t[:, cols]], axis=1)
        )
    (w_qkv,) = gather([shard_qkv], n_dp, n_t, 0)
    w_qkv = w_qkv.reshape(n_t, width, shard_qkv.shape[1])
    gain_cols = w_qkv[0, :, nq + 2 * nk : nq + 2 * nk + 2].astype(f32)
    gain_one, gain_two = gain_cols[:, 0], gain_cols[:, 1]

    position = (me_t * rows + jnp.arange(rows, dtype=jnp.int32)).astype(f32)
    freqs = rope_base ** (-(jnp.arange(HALF, dtype=f32) * 2.0) / HEAD_SIZE)
    angles = freqs[:, None] * position[None, :]
    cosine, sine = jnp.cos(angles), jnp.sin(angles)
    live = (me_t * rows + jnp.arange(rows, dtype=jnp.int32) < length).astype(f32)[:, None]
    x = tokens.astype(f32)
    inv_one = lax.rsqrt(jnp.mean(x * x, axis=1, keepdims=True) + eps_norm)
    g32 = cotangent.astype(f32) * live
    g = g32.astype(bf16)
    n1 = (x * inv_one * gain_one).astype(bf16)
    q, kv, n1t = qkv_project(n1, w_qkv, cosine, sine, nq, nk)
    q = q.reshape(n_t * nq, rows)

    w_out, w_mlp, *above, att, lse = gather(
        [out_weight.T] + shard_mlp[:MERGED], n_dp, n_t, 1, (kv, q, length), MERGED
    )
    w_out = w_out.reshape(n_t, width, no)
    w_mlp = w_mlp.reshape(n_t, width, 3 * tile * MERGED)
    kvs = [kv] + above
    att_z = att.reshape(n_t, no, rows)
    h_one = out_project(att_z, w_out, tokens, no, 0)

    inv_two = lax.rsqrt(jnp.mean(h_one * h_one, axis=1, keepdims=True) + eps_norm)
    n2 = (h_one * inv_two * gain_two).astype(bf16)
    out_sum, dn_sum, n2t, gt, share, w_last = mlp_gather(
        n2, g, w_mlp, shard_mlp[MERGED], tile, n_dp, n_t, 4
    )
    w_last = w_last.reshape(n_t, width, 3 * tile)
    shares = [share]
    out_sum, dn_sum, share = mlp(
        me, n2, n2t, g, gt, w_last, 0, tile, (out_sum, dn_sum), n_dp
    )
    shares.append(share)
    carry = (out_sum, dn_sum)
    mlp_out, d_n2 = carry
    block_out = (live * (h_one + mlp_out)).astype(bf16)

    scaled = d_n2 * gain_two
    inner = jnp.mean(scaled * h_one, axis=1, keepdims=True)
    gain_two_part = jnp.sum(d_n2 * h_one * inv_two, axis=0)
    d_h = g32 + inv_two * scaled - h_one * (inv_two * inv_two * inv_two * inner)
    d_h_low = d_h.astype(bf16)
    d_att, share = out_back(me, d_h_low, att_z, w_out, no, 0, n_dp)
    shares.append(share)

    d_att = d_att.reshape(n_t * no, rows)
    groups, _, lanes = lse.shape
    delta = (d_att.astype(f32) * att.astype(f32)).reshape(groups, -1, HEAD_SIZE, rows).sum(axis=2)
    delta = delta.reshape(groups, 1, lanes)
    *grads, out_share, q_share, kv_share, d_n1 = scatter(
        shares,
        n_dp,
        n_t,
        2,
        (sc, q, d_att, lse, delta, kvs),
        (cosine, sine, n1t, w_qkv, nq, nk),
    )

    scaled = d_n1 * gain_one
    inner = jnp.mean(scaled * x, axis=1, keepdims=True)
    gain_one_part = jnp.sum(d_n1 * x * inv_one, axis=0)
    d_x = inv_one * scaled - x * (inv_one * inv_one * inv_one * inner)
    tokens_grad = (d_h + d_x).astype(bf16)

    gain_parts = jnp.stack([gain_one_part.reshape(n_dp, block), gain_two_part.reshape(n_dp, block)], 1)
    gain_parts = to_relative(gain_parts, me_dp, n_dp)
    gain_share = reduce_small(gain_parts, me_dp, n_dp, n_t)

    gate_share = jnp.concatenate([s[:, :tile] for s in grads], axis=1)
    up_share = jnp.concatenate([s[:, tile : 2 * tile] for s in grads], axis=1)
    down_share = jnp.concatenate([s[:, 2 * tile :].T for s in grads], axis=0)
    return (
        block_out,
        tokens_grad,
        gain_share[0],
        q_share,
        kv_share[:, :nk],
        kv_share[:, nk:],
        out_share.T,
        gain_share[1],
        gate_share,
        up_share,
        down_share,
    )


def solution(mesh):
    in_specs = (
        P(("dp", "tensor"), None),
        P("dp"),
        P(("dp", "tensor"), None),
        P("dp"),
        P("dp", "tensor"),
        P("dp", "tensor"),
        P("dp", "tensor"),
        P("tensor", "dp"),
        P("dp"),
        P("dp", "tensor"),
        P("dp", "tensor"),
        P("tensor", "dp"),
    )
    out_specs = (
        P(("dp", "tensor"), None),
        P(("dp", "tensor"), None),
        P("dp"),
        P("dp", "tensor"),
        P("dp", "tensor"),
        P("dp", "tensor"),
        P("tensor", "dp"),
        P("dp"),
        P("dp", "tensor"),
        P("dp", "tensor"),
        P("tensor", "dp"),
    )
    fn = functools.partial(local, mesh.shape["dp"], mesh.shape["tensor"])
    return jax.shard_map(fn, mesh=mesh, in_specs=in_specs, out_specs=out_specs, check_vma=False)
```
